32 devices in a mesh: dp: 8 (over z, x), tensor: 4 (over y, core).
Axes of the slice: x: 2, y: 2, z: 4, core: 2. Of those that a mesh axis runs over, the one named last changes fastest.
Arguments:
- block_input: bfloat16 [16384, 768], P(('dp', 'tensor')), may hold values from -6 to 6
- output_grad: bfloat16 [16384, 768], P(('dp', 'tensor')), may hold values from -6 to 6
- lengths: int32 [8], P('dp'), may hold values from 1024 to 2048, as said below
- in_proj: float32 [768, 2, 1536], P('dp', None, 'tensor'), may hold values from -0.21875 to 0.21875
- step_proj: float32 [768, 24], P('dp', 'tensor'), may hold values from -0.21875 to 0.21875
- out_proj: float32 [768, 1536], P('dp', 'tensor'), may hold values from -0.15625 to 0.15625
- channel_params: float32 [6, 1536], P(None, 'tensor'), may hold values from -0.6 to 1.5
- head_params: float32 [3, 24], P(None, 'tensor'), may hold values from -6 to 2.31
- state_proj: float32 [768, 256], P(('dp', 'tensor')), may hold values from -0.21875 to 0.21875
- state_conv: float32 [256, 5], P(('dp', 'tensor')), may hold values from -0.5 to 0.5
- norm_gain: float32 [768], P(('dp', 'tensor')), may hold values from 0.5 to 1.5
- first_in_proj: float32 [768, 2, 1536], P('dp', None, 'tensor'), may hold values from -1200 to 1200
- first_step_proj: float32 [768, 24], P('dp', 'tensor'), may hold values from -1200 to 1200
- first_out_proj: float32 [768, 1536], P('dp', 'tensor'), may hold values from -1200 to 1200
- first_channel_params: float32 [6, 1536], P(None, 'tensor'), may hold values from -1200 to 1200
- first_head_params: float32 [3, 24], P(None, 'tensor'), may hold values from -1200 to 1200
- first_state_proj: float32 [768, 256], P(('dp', 'tensor')), may hold values from -1200 to 1200
- first_state_conv: float32 [256, 5], P(('dp', 'tensor')), may hold values from -1200 to 1200
- first_norm_gain: float32 [768], P(('dp', 'tensor')), may hold values from -1200 to 1200
- second_in_proj: float32 [768, 2, 1536], P('dp', None, 'tensor'), may hold values from 1000 to 100000
- second_step_proj: float32 [768, 24], P('dp', 'tensor'), may hold values from 1000 to 100000
- second_out_proj: float32 [768, 1536], P('dp', 'tensor'), may hold values from 1000 to 100000
- second_channel_params: float32 [6, 1536], P(None, 'tensor'), may hold values from 1000 to 100000
- second_head_params: float32 [3, 24], P(None, 'tensor'), may hold values from 1000 to 100000
- second_state_proj: float32 [768, 256], P(('dp', 'tensor')), may hold values from 1000 to 100000
- second_state_conv: float32 [256, 5], P(('dp', 'tensor')), may hold values from 1000 to 100000
- second_norm_gain: float32 [768], P(('dp', 'tensor')), may hold values from 1000 to 100000
Outputs:
- output: bfloat16 [16384, 768], P(('dp', 'tensor'))
- input_grad: float32 [16384, 768], P(('dp', 'tensor'))
- grad_in_proj: float32 [768, 2, 1536], P('dp', None, 'tensor')
- grad_step_proj: float32 [768, 24], P('dp', 'tensor')
- grad_out_proj: float32 [768, 1536], P('dp', 'tensor')
- grad_channel_params: float32 [6, 1536], P(None, 'tensor')
- grad_head_params: float32 [3, 24], P(None, 'tensor')
- grad_state_proj: float32 [768, 256], P(('dp', 'tensor'))
- grad_state_conv: float32 [256, 5], P(('dp', 'tensor'))
- grad_norm_gain: float32 [768], P(('dp', 'tensor'))
- new_first_in_proj: float32 [768, 2, 1536], P('dp', None, 'tensor')
- new_first_step_proj: float32 [768, 24], P('dp', 'tensor')
- new_first_out_proj: float32 [768, 1536], P('dp', 'tensor')
- new_first_channel_params: float32 [6, 1536], P(None, 'tensor')
- new_first_head_params: float32 [3, 24], P(None, 'tensor')
- new_first_state_proj: float32 [768, 256], P(('dp', 'tensor'))
- new_first_state_conv: float32 [256, 5], P(('dp', 'tensor'))
- new_first_norm_gain: float32 [768], P(('dp', 'tensor'))
- new_second_in_proj: float32 [768, 2, 1536], P('dp', None, 'tensor')
- new_second_step_proj: float32 [768, 24], P('dp', 'tensor')
- new_second_out_proj: float32 [768, 1536], P('dp', 'tensor')
- new_second_channel_params: float32 [6, 1536], P(None, 'tensor')
- new_second_head_params: float32 [3, 24], P(None, 'tensor')
- new_second_state_proj: float32 [768, 256], P(('dp', 'tensor'))
- new_second_state_conv: float32 [256, 5], P(('dp', 'tensor'))
- new_second_norm_gain: float32 [768], P(('dp', 'tensor'))
- update_in_proj: float32 [768, 2, 1536], P('dp', None, 'tensor')
- update_step_proj: float32 [768, 24], P('dp', 'tensor')
- update_out_proj: float32 [768, 1536], P('dp', 'tensor')
- update_channel_params: float32 [6, 1536], P(None, 'tensor')
- update_head_params: float32 [3, 24], P(None, 'tensor')
- update_state_proj: float32 [768, 256], P(('dp', 'tensor'))
- update_state_conv: float32 [256, 5], P(('dp', 'tensor'))
- update_norm_gain: float32 [768], P(('dp', 'tensor'))
- lamb_norms: float32 [2, 8], replicated
The draws below stay inside these ranges and needn't reach their ends.
Inputs may be any that keep to these rules, and one draw needn't show every extreme that they name: `lengths`: some sequence has exactly 2048 live positions.
All inputs are finite; a program needn't handle non-finite values.
Results may differ from the reference program's by a relative error of at most 0.012.
The reference program's roundings to bfloat16 on the way count: a program that leaves them out, or rounds other values in their place, can miss the bound.
Values may be sent and summed in bfloat16 or wider, within the bound.
No kernel may reach another device: no remote copies, remote signals or barrier semaphores. Data moves between devices by JAX's collectives and lax.ppermute only.
A program may use at most 192 MiB of HBM per device.

```python
import math
import jax
import jax.numpy as jnp
from jax import lax

D = 768
HEADS = 24
STATE = 128
CONV = 4
SPAN = 256
LMAX = 2048
LMIN = 1024
INNER = 1536
NSEQ = 8
TOKENS = 16384


def draw_lengths(key, part):
    picked = jax.random.randint(jax.random.fold_in(key, 11), (NSEQ,), LMIN, LMAX + 1)
    longest = jax.random.randint(jax.random.fold_in(key, 12), (), 0, NSEQ)
    return jnp.where(jnp.arange(NSEQ) == longest, LMAX, picked).astype(jnp.int32)


def draw_channel_params(key, part):
    kernel = jax.random.uniform(jax.random.fold_in(key, 21), (CONV, INNER), jnp.float32, -0.6, 0.6)
    offsets = jax.random.uniform(jax.random.fold_in(key, 22), (1, INNER), jnp.float32, -0.5, 0.5)
    gains = jax.random.uniform(jax.random.fold_in(key, 23), (1, INNER), jnp.float32, 0.5, 1.5)
    return jnp.concatenate([kernel, offsets, gains], axis=0)


def draw_head_params(key, part):
    rates = jax.random.uniform(jax.random.fold_in(key, 31), (1, HEADS), jnp.float32, math.log(0.01), math.log(10.0))
    biases = jax.random.uniform(jax.random.fold_in(key, 32), (1, HEADS), jnp.float32, -6.0, -2.0)
    skips = jax.random.uniform(jax.random.fold_in(key, 33), (1, HEADS), jnp.float32, 0.5, 1.5)
    return jnp.concatenate([rates, biases, skips], axis=0)


def steps_of(stream_key, extent, cuts, low, largest):
    level, own = 1.0, jax.random.fold_in(stream_key, 6)
    for dim, blocks in cuts:
        heights = jnp.exp(jax.random.uniform(jax.random.fold_in(own, dim), (blocks,), jnp.float32, low / len(cuts), largest / len(cuts)))
        level = level * jnp.repeat(heights, extent[dim] // blocks).reshape([-1 if axis == dim else 1 for axis in range(len(extent))])
    return level


def noise(key, shape, width, reach, cuts=(), held_as=jnp.bfloat16):
    drawn = jax.random.normal(key, shape, jnp.float32) * width
    if len(cuts) > 0:
        drawn = steps_of(key, shape, cuts, -0.22, 0.18) * drawn
    return jnp.clip(drawn, min=-reach, max=reach).astype(held_as)


def setup_inputs(seed: int = 0) -> dict:
    arg_keys = jax.random.split(jax.random.key(seed), 28)
    return {
        "block_input": noise(arg_keys[0], (TOKENS, D), 1.0, 6.0, ((0, 32),)),
        "output_grad": noise(arg_keys[1], (TOKENS, D), 1.0, 6.0, ((0, 32),)),
        "lengths": draw_lengths(jax.random.fold_in(arg_keys[27], 71), 0),
        "in_proj": noise(arg_keys[3], (D, 2, INNER), D ** -0.5, 0.21875, ((0, 8), (2, 4)), jnp.float32),
        "step_proj": noise(arg_keys[4], (D, HEADS), D ** -0.5, 0.21875, ((0, 8), (1, 4)), jnp.float32),
        "out_proj": noise(arg_keys[5], (D, INNER), INNER ** -0.5, 0.15625, ((0, 8), (1, 4)), jnp.float32),
        "channel_params": draw_channel_params(jax.random.fold_in(arg_keys[27], 71), 0),
        "head_params": draw_head_params(jax.random.fold_in(arg_keys[27], 71), 0),
        "state_proj": noise(arg_keys[8], (D, 2 * STATE), D ** -0.5, 0.21875, ((0, 32),), jnp.float32),
        "state_conv": jnp.clip(jax.random.uniform(arg_keys[9], (2 * STATE, CONV + 1), jnp.float32, -0.5, 0.5) * steps_of(arg_keys[9], (2 * STATE, CONV + 1), ((0, 32),), -0.4, 0.0), -0.5, 0.5),
        "norm_gain": jnp.clip(1.0 + 0.1 * jax.random.normal(arg_keys[10], (D,), jnp.float32), 0.5, 1.5),
        "first_in_proj": noise(arg_keys[11], (D, 2, INNER), 200.0, 1200.0, ((0, 8), (2, 4)), jnp.float32),
        "first_step_proj": noise(arg_keys[12], (D, HEADS), 200.0, 1200.0, ((0, 8), (1, 4)), jnp.float32),
        "first_out_proj": noise(arg_keys[13], (D, INNER), 200.0, 1200.0, ((0, 8), (1, 4)), jnp.float32),
        "first_channel_params": noise(arg_keys[14], (CONV + 2, INNER), 200.0, 1200.0, ((1, 4),), jnp.float32),
        "first_head_params": noise(arg_keys[15], (3, HEADS), 200.0, 1200.0, ((1, 4),), jnp.float32),
        "first_state_proj": noise(arg_keys[16], (D, 2 * STATE), 200.0, 1200.0, ((0, 32),), jnp.float32),
        "first_state_conv": noise(arg_keys[17], (2 * STATE, CONV + 1), 200.0, 1200.0, ((0, 32),), jnp.float32),
        "first_norm_gain": noise(arg_keys[18], (D,), 200.0, 1200.0, ((0, 32),), jnp.float32),
        "second_in_proj": jnp.clip(jnp.exp(math.log(100000.0) - 4.6051702 * jax.random.uniform(arg_keys[19], (D, 2, INNER), jnp.float32) ** steps_of(arg_keys[19], (D, 2, INNER), ((0, 8), (2, 4)), -0.2, 0.2)), 1000.0, 100000.0),
        "second_step_proj": jnp.clip(jnp.exp(math.log(100000.0) - 4.6051702 * jax.random.uniform(arg_keys[20], (D, HEADS), jnp.float32) ** steps_of(arg_keys[20], (D, HEADS), ((0, 8), (1, 4)), -0.2, 0.2)), 1000.0, 100000.0),
        "second_out_proj": jnp.clip(jnp.exp(math.log(100000.0) - 4.6051702 * jax.random.uniform(arg_keys[21], (D, INNER), jnp.float32) ** steps_of(arg_keys[21], (D, INNER), ((0, 8), (1, 4)), -0.2, 0.2)), 1000.0, 100000.0),
        "second_channel_params": jnp.clip(jnp.exp(math.log(100000.0) - 4.6051702 * jax.random.uniform(arg_keys[22], (CONV + 2, INNER), jnp.float32) ** steps_of(arg_keys[22], (CONV + 2, INNER), ((1, 4),), -0.2, 0.2)), 1000.0, 100000.0),
        "second_head_params": jnp.clip(jnp.exp(math.log(100000.0) - 4.6051702 * jax.random.uniform(arg_keys[23], (3, HEADS), jnp.float32) ** steps_of(arg_keys[23], (3, HEADS), ((1, 4),), -0.2, 0.2)), 1000.0, 100000.0),
        "second_state_proj": jnp.clip(jnp.exp(math.log(100000.0) - 4.6051702 * jax.random.uniform(arg_keys[24], (D, 2 * STATE), jnp.float32) ** steps_of(arg_keys[24], (D, 2 * STATE), ((0, 32),), -0.2, 0.2)), 1000.0, 100000.0),
        "second_state_conv": jnp.clip(jnp.exp(math.log(100000.0) - 4.6051702 * jax.random.uniform(arg_keys[25], (2 * STATE, CONV + 1), jnp.float32) ** steps_of(arg_keys[25], (2 * STATE, CONV + 1), ((0, 32),), -0.2, 0.2)), 1000.0, 100000.0),
        "second_norm_gain": jnp.clip(jnp.exp(math.log(100000.0) - 4.6051702 * jax.random.uniform(arg_keys[26], (D,), jnp.float32) ** steps_of(arg_keys[26], (D,), ((0, 32),), -0.2, 0.2)), 1000.0, 100000.0),
    }


EPSILON = 1e-05
ADAM_EPSILON = 1e-06
DECAY = 0.5
BIAS_FIRST = 0.875
BIAS_SECOND = 0.875
RATE = 0.3
WEIGHT_DECAY = 0.01
HIGHEST = lax.Precision.HIGHEST

@jax.custom_vjp
def low(v):
    return lax.optimization_barrier(v.astype(jnp.bfloat16)).astype(jnp.float32)

@jax.custom_vjp
def low_back(v):
    return v

def low_keep(v):
    return (low(v), None)

def low_pass(kept, grad):
    return (grad,)

def back_keep(v):
    return (v, None)

def back_low(kept, grad):
    return (low(grad),)
low.defvjp(low_keep, low_pass)
low_back.defvjp(back_keep, back_low)

def matmul(left, right):
    return jnp.dot(left, right, precision=HIGHEST, preferred_element_type=jnp.float32)

def causal_conv(values, kernel, offsets):
    padded = jnp.pad(values, ((kernel.shape[0] - 1, 0), (0, 0)))
    summed = offsets[None, :] + jnp.zeros_like(values)
    for offset in range(kernel.shape[0]):
        summed = summed + kernel[offset][None, :] * padded[offset:offset + values.shape[0]]
    return jax.nn.silu(summed)

def ssd_scan(signal, b_rows, c_rows, step_size, log_rate):
    length, head_count, head_width = signal.shape
    blocks = length // SPAN
    decay_log = -jnp.exp(log_rate)[None, :] * step_size
    x_blocks = signal.reshape(blocks, SPAN, head_count, head_width)
    dt_blocks = step_size.reshape(blocks, SPAN, head_count)
    b_blocks = b_rows.reshape(blocks, SPAN, -1)
    c_blocks = c_rows.reshape(blocks, SPAN, -1)
    cumulative = jnp.cumsum(decay_log.reshape(blocks, SPAN, head_count), axis=1)
    intersection = jnp.einsum('cqn,ckn->cqk', c_blocks, b_blocks, precision=HIGHEST)
    causal = jnp.arange(SPAN)[:, None] >= jnp.arange(SPAN)[None, :]
    spread = cumulative[:, :, None, :] - cumulative[:, None, :, :]
    damping = jnp.exp(jnp.where(causal[None, :, :, None], spread, -jnp.inf))
    mixing = intersection[:, :, :, None] * damping * dt_blocks[:, None, :, :]
    within = jnp.einsum('cqkh,ckhp->cqhp', mixing, x_blocks, precision=HIGHEST)
    closing = cumulative[:, -1, :]
    weights_end = jnp.exp(closing[:, None, :] - cumulative) * dt_blocks
    states = jnp.einsum('ckh,ckhp,ckn->chpn', weights_end, x_blocks, b_blocks, precision=HIGHEST)

    def carry_step(carried, element):
        state_new, closing_new = element
        return (jnp.exp(closing_new)[:, None, None] * carried + state_new, carried)
    initial = jnp.zeros(states.shape[1:], jnp.float32)
    unused, entering = lax.scan(carry_step, initial, (states, closing))
    across = jnp.einsum('cqn,chpn->cqhp', c_blocks, entering, precision=HIGHEST) * jnp.exp(cumulative)[..., None]
    return (within + across).reshape(length, head_count, head_width)

def gate_mix(signal, b_rows, c_rows, step_raw, gate_raw, head_local):
    length = signal.shape[0]
    head_count = head_local.shape[1]
    step_size = jax.nn.softplus(step_raw + head_local[1][None, :])
    shaped = signal.reshape(length, head_count, -1)
    mixed = ssd_scan(shaped, b_rows, c_rows, step_size, head_local[0]) + head_local[2][None, :, None] * shaped
    return mixed.reshape(length, -1) * jax.nn.silu(gate_raw)

def lamb_parts(weight, gradient, first_old, second_old):
    first_new = DECAY * first_old + (1.0 - DECAY) * gradient
    second_new = DECAY * second_old + (1.0 - DECAY) * gradient * gradient
    direction = first_new / BIAS_FIRST / (jnp.sqrt(second_new / BIAS_SECOND) + ADAM_EPSILON) + WEIGHT_DECAY * weight
    return (first_new, second_new, direction)

def sequence_block(inputs, live_row, in_low, step_low, out_low, channel_params, head_params, state_low, state_conv, norm_gain):
    scale = lax.rsqrt(lax.optimization_barrier(jnp.mean(inputs * inputs, axis=-1, keepdims=True)) + EPSILON)
    normed = low(inputs * scale * norm_gain[None, :])
    gate_raw = low_back(matmul(normed, in_low[:, 0, :]))
    signal_raw = low_back(matmul(normed, in_low[:, 1, :]))
    state_raw = low_back(matmul(normed, state_low))
    step_raw = low_back(matmul(normed, step_low))
    signal = low(causal_conv(signal_raw, channel_params[:CONV], channel_params[CONV]))
    maps = causal_conv(state_raw, state_conv[:, :CONV].T, state_conv[:, CONV])
    b_rows = low(maps[:, :STATE])
    c_rows = low(maps[:, STATE:])
    gated = gate_mix(signal, b_rows, c_rows, step_raw, gate_raw, head_params)
    gate_scale = lax.rsqrt(lax.optimization_barrier(jnp.mean(gated * gated, axis=-1, keepdims=True)) + EPSILON)
    merged = low(gated * gate_scale * channel_params[CONV + 1][None, :])
    branch = low_back(matmul(merged, out_low.T)) * live_row[:, None]
    return inputs + branch

def reference(block_input, output_grad, lengths, in_proj, step_proj, out_proj, channel_params, head_params, state_proj, state_conv, norm_gain, first_in_proj, first_step_proj, first_out_proj, first_channel_params, first_head_params, first_state_proj, first_state_conv, first_norm_gain, second_in_proj, second_step_proj, second_out_proj, second_channel_params, second_head_params, second_state_proj, second_state_conv, second_norm_gain):
    inputs = block_input.astype(jnp.float32).reshape(NSEQ, LMAX, D)
    upstream = output_grad.astype(jnp.float32).reshape(NSEQ, LMAX, D)
    live = (jnp.arange(LMAX, dtype=jnp.int32)[None, :] < lengths[:, None]).astype(jnp.float32)
    masters = (in_proj, step_proj, out_proj, channel_params, head_params, state_proj, state_conv, norm_gain)
    firsts = (first_in_proj, first_step_proj, first_out_proj, first_channel_params, first_head_params, first_state_proj, first_state_conv, first_norm_gain)
    seconds = (second_in_proj, second_step_proj, second_out_proj, second_channel_params, second_head_params, second_state_proj, second_state_conv, second_norm_gain)

    def whole(values, w_in, w_step, w_out, channels, heads_local, w_state, conv_state, gain):
        in_low = low(w_in)
        step_low = low(w_step)
        out_low = low(w_out)
        state_low = low(w_state)
        checked = jax.checkpoint(sequence_block)

        def one_sequence(element):
            return checked(element[0], element[1], in_low, step_low, out_low, channels, heads_local, state_low, conv_state, gain)
        return lax.map(one_sequence, (values, live))
    summed, backward = jax.vjp(whole, inputs, *masters)
    grads = backward(upstream)
    output = summed.reshape(TOKENS, D).astype(jnp.bfloat16)
    input_grad = grads[0].reshape(TOKENS, D)
    first_list = []
    second_list = []
    update_list = []
    weight_norms = []
    direction_norms = []
    for weight, gradient, first_old, second_old in zip(masters, grads[1:], firsts, seconds):
        first_new, second_new, direction = lamb_parts(weight, gradient, first_old, second_old)
        weight_norm = jnp.sqrt(jnp.sum(weight * weight))
        direction_norm = jnp.sqrt(jnp.sum(direction * direction))
        first_list.append(first_new)
        second_list.append(second_new)
        update_list.append(-RATE * weight_norm / direction_norm * direction)
        weight_norms.append(weight_norm)
        direction_norms.append(direction_norm)
    lamb_norms = jnp.stack([jnp.stack(weight_norms), jnp.stack(direction_norms)])
    return (output, input_grad, grads[1], grads[2], grads[3], grads[4], grads[5], grads[6], grads[7], grads[8], first_list[0], first_list[1], first_list[2], first_list[3], first_list[4], first_list[5], first_list[6], first_list[7], second_list[0], second_list[1], second_list[2], second_list[3], second_list[4], second_list[5], second_list[6], second_list[7], update_list[0], update_list[1], update_list[2], update_list[3], update_list[4], update_list[5], update_list[6], update_list[7], lamb_norms)
```

```python
import functools

import jax
import jax.numpy as jnp
from jax import lax
from jax.experimental import pallas as pl
from jax.experimental.pallas import tpu as pltpu
from jax.sharding import PartitionSpec as P

STATE = 128
CONV = 4
SPAN = 256
LMAX = 2048
INNER = 1536
HEAD = 64
MAPS = 2 * STATE
LANES = 128
SMALL = 16

EPSILON = 1e-05
ADAM_EPSILON = 1e-06
DECAY = 0.5
BIAS_FIRST = 0.875
BIAS_SECOND = 0.875
RATE = 0.3
WEIGHT_DECAY = 0.01
HIGHEST = lax.Precision.HIGHEST
BF = jnp.bfloat16
F32 = jnp.float32


def dot(left, right, left_dim=1, right_dim=0, precision=None):
    return lax.dot_general(
        left,
        right,
        (((left_dim,), (right_dim,)), ((), ())),
        precision=precision,
        preferred_element_type=F32,
    )


def exchange(values, axis, mask):
    count = lax.axis_size(axis)
    return lax.ppermute(values, axis, [(at, at ^ mask) for at in range(count)])


def low_count(count):
    low = 1
    while low * low * 4 <= count:
        low *= 2
    return low


def gather_pieces(own, axis, low):
    count = lax.axis_size(axis)
    pieces = {0: own}
    for high in range(low, count, low):
        pieces[high] = exchange(own, axis, high)
    for high in range(0, count, low):
        for near in range(1, low):
            pieces[high + near] = exchange(pieces[high], axis, near)
    return [pieces[mask] for mask in range(count)]


def slot_masks(count, low):
    return [high + near for near in range(low) for high in range(0, count, low)]


def scatter_parts(slots, axis, low, small=0):
    count = lax.axis_size(axis)
    highs = count // low
    total = slots[:highs].astype(F32)
    for near in range(1, low):
        sent = slots[near * highs : (near + 1) * highs]
        total = total + exchange(sent, axis, near).astype(F32)
    if small > 0:
        joined = total[:, :small] + total[:, small : 2 * small]
        high = lax.reduce_precision(joined, 8, 7)
        total = jnp.concatenate([high, joined - high, total[:, 2 * small :]], axis=1)
    received = [
        exchange(total[position].astype(slots.dtype), axis, position * low)
        for position in range(1, highs)
    ]
    return total[0], received


def scatter_sum(slots, axis, low):
    kept, received = scatter_parts(slots, axis, low)
    for values in received:
        kept = kept + values.astype(F32)
    return kept


def lane_ids(shape):
    return lax.broadcasted_iota(jnp.int32, shape, len(shape) - 1)


def spread_heads(columns, heads):
    rows = columns.shape[0]
    left = lane_ids((rows, LANES)) < HEAD
    return jnp.concatenate(
        [
            jnp.where(left, columns[:, head : head + 1], columns[:, head + 1 : head + 2])
            for head in range(0, heads, 2)
        ],
        axis=1,
    )


def causal_mask():
    rows = lax.broadcasted_iota(jnp.int32, (SPAN, SPAN), 0)
    columns = lax.broadcasted_iota(jnp.int32, (SPAN, SPAN), 1)
    return rows >= columns


def step_terms(step_in, heads_ref):
    step = jnp.maximum(step_in, 0.0) + jnp.log1p(jnp.exp(-jnp.abs(step_in)))
    rate = jnp.exp(heads_ref[0:1, :])
    decay = -rate * step
    lower = causal_mask().astype(F32).astype(BF)
    cumulative = sum(dot(lower, part) for part in thirds(decay))
    return step, rate, decay, cumulative


def halves(values):
    high = values.astype(BF)
    return high, (values - high.astype(F32)).astype(BF)


def thirds(values):
    high = values.astype(BF)
    rest = values - high.astype(F32)
    middle = rest.astype(BF)
    return high, middle, (rest - middle.astype(F32)).astype(BF)


def sigmoid(values):
    return 1.0 / (1.0 + jnp.exp(-values))


def forward_kernel(
    channels, pieces, blocks_per, ids, u_ref, *refs
):
    width = channels
    heads = width // HEAD
    mixed_width = width + MAPS
    piece_refs = refs[:pieces]
    (
        state_w_ref,
        gain_ref,
        taps_ref,
        heads_ref,
        skip_ref,
        normed_ref,
        gate_ref,
        raw_ref,
        pre_ref,
        act_ref,
        step_ref,
        state_ref,
        mixed_ref,
        weight_ref,
        tail,
        carried,
    ) = refs[pieces:]
    at = pl.program_id(0)

    @pl.when(at == 0)
    def _():
        rows = weight_ref.shape[0] // pieces
        for mask in range(pieces):
            block = ids[0] ^ mask if pieces > 1 else 0
            where_ = pl.ds(pl.multiple_of(block * rows, 8), rows) if pieces > 1 else slice(None)
            weight_ref[where_, : 2 * width] = piece_refs[mask][:, : 2 * width]
            weight_ref[where_, 2 * width + MAPS :] = piece_refs[mask][:, 2 * width :]
        weight_ref[:, 2 * width : 2 * width + MAPS] = state_w_ref[...]

    @pl.when(at % (LMAX // SPAN) == 0)
    def _():
        tail[0:8, :] = jnp.zeros((8, mixed_width), F32)
        carried[...] = jnp.zeros_like(carried)

    inputs = u_ref[0].astype(F32)
    scale = lax.rsqrt(jnp.mean(inputs * inputs, axis=-1, keepdims=True) + EPSILON)
    normed = (inputs * scale * gain_ref[0:1, :]).astype(BF)
    normed_ref[...] = normed
    gate_ref[...] = dot(normed, weight_ref[:, :width])
    raw = dot(normed, weight_ref[:, width : 2 * width + MAPS])
    raw_ref[...] = raw
    tail[8:, :] = raw
    step_in = dot(normed, weight_ref[:, 2 * width + MAPS :]) + heads_ref[1:2, :]
    step_ref[...] = step_in
    pre = taps_ref[CONV : CONV + 1, :] + taps_ref[0:1, :] * tail[5 : 5 + SPAN, :]
    for tap in range(1, CONV):
        pre = pre + taps_ref[tap : tap + 1, :] * tail[5 + tap : 5 + tap + SPAN, :]
    tail[0:8, :] = tail[SPAN : SPAN + 8, :]
    pre_ref[...] = pre
    act = (pre * sigmoid(pre)).astype(BF)
    act_ref[...] = act
    signal = act[:, :width].astype(F32)
    b_rows = act[:, width : width + STATE]
    c_rows = act[:, width + STATE :]
    step, rate, decay, cumulative = step_terms(step_in, heads_ref)
    across_rows = jnp.transpose(cumulative)
    closing = cumulative[SPAN - 1 : SPAN, :]
    held = jnp.where(causal_mask(), dot(c_rows, b_rows, 1, 1), 0.0)
    weighted = (spread_heads(step, heads) * signal).astype(BF)
    left = lane_ids((SPAN, LANES)) < HEAD
    state = carried[...]
    state_ref[0] = state
    across = dot(
        jnp.concatenate([c_rows, c_rows], axis=1),
        jnp.concatenate(halves(state), axis=1),
        1,
        1,
    ) * spread_heads(jnp.exp(cumulative), heads)
    within = []
    for head in range(0, heads, 2):
        lanes = slice(head * HEAD, head * HEAD + LANES)
        pair = weighted[:, lanes]
        total = None
        for side in range(2):
            spread = (
                cumulative[:, head + side : head + side + 1]
                - across_rows[head + side : head + side + 1, :]
            )
            mixing = (held * jnp.exp(jnp.minimum(spread, 0.0))).astype(BF)
            kept = jnp.where(left if side == 0 else ~left, pair, jnp.zeros_like(pair))
            part = dot(mixing, kept)
            total = part if total is None else total + part
        within.append(total)
    mixed_ref[...] = jnp.concatenate(within, axis=1) + across + skip_ref[0:1, :] * signal
    ended = weighted.astype(F32) * spread_heads(jnp.exp(closing - cumulative), heads)
    fresh = sum(dot(part, b_rows, 0, 0) for part in halves(ended))
    kept_rate = jnp.exp(closing)
    for head in range(heads):
        rows = slice(head * HEAD, (head + 1) * HEAD)
        carried[rows, :] = kept_rate[:, head : head + 1] * state[rows, :] + fresh[rows, :]


def rows_live(ids, at, lengths):
    sequence = at // (LMAX // SPAN)
    position = (at % (LMAX // SPAN)) * SPAN + lax.broadcasted_iota(jnp.int32, (SPAN, 1), 0)
    return position < lengths[sequence]


def middle_kernel(ids, lengths, grad_ref, gate_ref, mixed_ref, *refs):
    weight, gain_ref, merged_grad_ref, branch_ref, sums_ref = refs
    at = pl.program_id(0)

    upstream = grad_ref[0]
    upstream = jnp.where(rows_live(ids, at, lengths), upstream, jnp.zeros_like(upstream))
    merged_grad = dot(upstream, weight[...])
    merged_grad_ref[...] = merged_grad
    gate = gate_ref[...]
    gated = mixed_ref[...] * (gate * sigmoid(gate))
    gained = gated * gain_ref[0:1, :]
    squares = jnp.sum(gated * gated, axis=1, keepdims=True)
    products = jnp.sum(merged_grad * gained, axis=1, keepdims=True)
    branch_ref[0] = dot(gained.astype(BF), weight[...], 1, 1).astype(BF)
    lanes = lane_ids((SPAN, LANES))
    both = jnp.where(lanes == 0, squares, jnp.where(lanes == 1, products, 0.0))
    sums_ref[...] = jnp.transpose(both)[0:2, :]


def backward_kernel(
    channels,
    masks,
    ids,
    lengths,
    sums_ref,
    u_ref,
    grad_ref,
    normed_ref,
    gate_ref,
    mixed_ref,
    merged_grad_ref,
    raw_ref,
    pre_ref,
    act_ref,
    step_ref,
    state_ref,
    state_next_ref,
    weight_ref,
    taps_ref,
    heads_ref,
    skip_ref,
    gain_ref,
    part_ref,
    slots_ref,
    carried,
    ahead,
    weight_sum,
    out_sum,
    tap_sum,
    head_sum,
    gain_sum,
):
    width = channels
    heads = width // HEAD
    mixed_width = width + MAPS
    step_at = pl.program_id(0)
    at = pl.num_programs(0) - 1 - step_at

    @pl.when(step_at == 0)
    def _():
        weight_sum[...] = jnp.zeros_like(weight_sum)
        out_sum[...] = jnp.zeros_like(out_sum)
        tap_sum[...] = jnp.zeros_like(tap_sum)
        head_sum[...] = jnp.zeros_like(head_sum)
        gain_sum[...] = jnp.zeros_like(gain_sum)

    @pl.when(step_at % (LMAX // SPAN) == 0)
    def _():
        carried[...] = jnp.zeros_like(carried)
        ahead[SPAN:, :] = jnp.zeros((8, mixed_width), F32)

    sums = sums_ref[...]
    scale_row = lax.rsqrt(sums[0:1, :] / INNER + EPSILON)
    cross_row = scale_row * scale_row * scale_row * (sums[1:2, :] / INNER)
    row_ids = lax.broadcasted_iota(jnp.int32, (LANES, SPAN), 0)
    columns = jnp.transpose(jnp.where(row_ids == 0, scale_row, cross_row))
    gate_scale = columns[:, 0:1]
    cross = columns[:, 1:2]

    gate = gate_ref[...]
    gate_s = sigmoid(gate)
    gate_act = gate * gate_s
    mixed = mixed_ref[...]
    gated = mixed * gate_act
    merged_grad = merged_grad_ref[...]
    gain = skip_ref[1:2, :]
    scaled = gated * gate_scale
    tap_sum[5:6, :width] += jnp.sum(merged_grad * scaled, axis=0, keepdims=True)
    merged = (scaled * gain).astype(BF)
    upstream = grad_ref[0]
    upstream = jnp.where(rows_live(ids, at, lengths), upstream, jnp.zeros_like(upstream))
    out_sum[...] += dot(upstream, merged, 0, 0)
    gated_grad = gate_scale * (merged_grad * gain) - gated * cross
    mixed_grad = gated_grad * gate_act
    gate_grad = gated_grad * mixed * (gate_s * (1.0 + gate * (1.0 - gate_s)))

    act = act_ref[...]
    signal = act[:, :width].astype(F32)
    b_rows = act[:, width : width + STATE]
    c_rows = act[:, width + STATE :]
    skip = skip_ref[0:1, :]
    tap_sum[6:7, :width] += jnp.sum(mixed_grad * signal, axis=0, keepdims=True)
    grad_high, grad_rest = halves(mixed_grad)
    grad_rows = grad_high.astype(F32) + grad_rest.astype(F32)

    step_in = step_ref[...]
    step, rate, decay, cumulative = step_terms(step_in, heads_ref)
    across_rows = jnp.transpose(cumulative)
    closing = cumulative[SPAN - 1 : SPAN, :]
    causal = causal_mask()
    held = jnp.where(causal, dot(c_rows, b_rows, 1, 1), 0.0)
    step_wide = spread_heads(step, heads)
    weighted = (step_wide * signal).astype(BF)
    weighted_rows = weighted.astype(F32)
    end_wide = spread_heads(jnp.exp(closing - cumulative), heads)
    state_grad = carried[...]
    state_parts = halves(state_grad)
    grown = halves(grad_rows * spread_heads(jnp.exp(cumulative), heads))
    before = halves(state_ref[0])
    c_grad = dot(grown[0], before[0]) + dot(grown[0], before[1]) + dot(grown[1], before[0])
    ended = halves(weighted_rows * end_wide)
    b_grad = (
        dot(ended[0], state_parts[0])
        + dot(ended[0], state_parts[1])
        + dot(ended[1], state_parts[0])
    )
    from_state = end_wide * dot(
        jnp.concatenate([b_rows, b_rows], axis=1), jnp.concatenate(state_parts, axis=1), 1, 1
    )
    left = lane_ids((SPAN, LANES)) < HEAD
    held_grad = None
    within = []
    for head in range(0, heads, 2):
        lanes = slice(head * HEAD, head * HEAD + LANES)
        pair = weighted[:, lanes]
        pair_twice = jnp.concatenate([pair, pair], axis=1)
        total = None
        for side in range(2):
            spread = (
                cumulative[:, head + side : head + side + 1]
                - across_rows[head + side : head + side + 1, :]
            )
            damping = jnp.exp(jnp.minimum(spread, 0.0))
            mixing = (held * damping).astype(BF)
            side_lanes = left if side == 0 else ~left
            kept = jnp.concatenate(
                [
                    jnp.where(side_lanes, part[:, lanes], jnp.zeros_like(pair))
                    for part in (grad_high, grad_rest)
                ],
                axis=1,
            )
            term = dot(kept, pair_twice, 1, 1) * damping
            held_grad = term if held_grad is None else held_grad + term
            part = dot(mixing, kept, 0, 0)
            total = part if total is None else total + part
        within.append(total[:, :LANES] + total[:, LANES:])
    held_low = jnp.where(causal, held_grad, 0.0).astype(BF)
    c_grad = c_grad + dot(held_low, b_rows)
    b_grad = b_grad + dot(held_low, c_rows, 0, 0)
    weighted_grad = jnp.concatenate(within, axis=1) + from_state
    fresh = sum(dot(part, c_rows, 0, 0) for part in grown)
    kept_rate = jnp.exp(closing)
    overlap = jnp.sum(state_grad * state_next_ref[0], axis=1, keepdims=True)
    lane_row = lane_ids((1, LANES))
    closing_grad = jnp.zeros((1, LANES), F32)
    for head in range(heads):
        rows = slice(head * HEAD, (head + 1) * HEAD)
        carried[rows, :] = kept_rate[:, head : head + 1] * state_grad[rows, :] + fresh[rows, :]
        closing_grad = closing_grad + jnp.where(
            lane_row == head, jnp.sum(overlap[rows, :], axis=0, keepdims=True), 0.0
        )
    picker = (
        lax.broadcasted_iota(jnp.int32, (width, LANES), 0) // HEAD
        == lax.broadcasted_iota(jnp.int32, (width, LANES), 1)
    ).astype(F32).astype(BF)
    shaped = mixed - skip * signal
    cumulative_grad = sum(
        dot(part, picker)
        for part in halves(grad_rows * shaped - weighted_rows * weighted_grad)
    )
    lower = causal.astype(F32).astype(BF)
    decay_grad = sum(dot(lower, part, 0, 0) for part in halves(cumulative_grad)) + closing_grad
    step_grad = (
        sum(dot(part, picker) for part in halves(signal * weighted_grad)) - rate * decay_grad
    )
    step_in_grad = step_grad * sigmoid(step_in)
    head_sum[0:1, :] += jnp.sum(decay * decay_grad, axis=0, keepdims=True)
    head_sum[1:2, :] += jnp.sum(step_in_grad, axis=0, keepdims=True)
    signal_grad = step_wide * weighted_grad + skip * mixed_grad

    pre = pre_ref[...]
    pre_s = sigmoid(pre)
    slope = pre_s * (1.0 + pre * (1.0 - pre_s))
    ahead[:SPAN, :] = jnp.concatenate([signal_grad, b_grad, c_grad], axis=1) * slope
    raw = raw_ref[...]
    raw_grad = None
    for shift in range(CONV):
        moved = ahead[shift : shift + SPAN, :]
        tap = CONV - 1 - shift
        term = taps_ref[tap : tap + 1, :] * moved
        raw_grad = term if raw_grad is None else raw_grad + term
        tap_sum[tap : tap + 1, :] += jnp.sum(raw * moved, axis=0, keepdims=True)
        if shift == 0:
            tap_sum[CONV : CONV + 1, :] += jnp.sum(moved, axis=0, keepdims=True)
    ahead[SPAN:, :] = ahead[0:8, :]

    low = jnp.concatenate(
        [gate_grad.astype(BF), raw_grad.astype(BF), step_in_grad.astype(BF)], axis=1
    )
    normed = normed_ref[...]
    weight_sum[...] += dot(normed, low, 0, 0)
    part = dot(low, weight_ref[...], 1, 1)
    part_ref[0] = part.astype(BF)
    inputs = u_ref[0].astype(F32)
    scale = lax.rsqrt(jnp.mean(inputs * inputs, axis=-1, keepdims=True) + EPSILON)
    gain_sum[0:1, :] += jnp.sum(part * (inputs * scale), axis=0, keepdims=True)

    @pl.when(step_at == pl.num_programs(0) - 1)
    def _():
        columns_in = weight_sum.shape[1]
        rows = weight_sum.shape[0] // len(masks)
        channel_count = rows * len(masks)
        for position, mask in enumerate(masks):
            block = ids[0] ^ mask
            small = jnp.concatenate(
                [
                    tap_sum[:, :width],
                    head_sum[...],
                    pltpu.roll(
                        tap_sum[:, width:], (MAPS - block * (MAPS // len(masks))) % MAPS, 1
                    )[:, :LANES],
                    pltpu.roll(gain_sum[...], (channel_count - block * rows) % channel_count, 1)[
                        :, :LANES
                    ],
                ],
                axis=1,
            )
            both = jnp.concatenate(halves(small), axis=0)
            picked = pl.ds(pl.multiple_of(block * rows, 8), rows)
            slots_ref[position, 0:SMALL, : both.shape[1]] = both
            slots_ref[position, 0:SMALL, both.shape[1] :] = jnp.zeros(
                (SMALL, slots_ref.shape[2] - both.shape[1]), BF
            )
            slots_ref[position, SMALL:, :columns_in] = weight_sum[picked, :].astype(BF)
            slots_ref[position, SMALL:, columns_in:] = out_sum[picked, :].astype(BF)


def pad_to(values, axis, size):
    if values.shape[axis] == size:
        return values
    pads = [(0, 0)] * values.ndim
    pads[axis] = (0, size - values.shape[axis])
    return jnp.pad(values, pads)


def whole_spec(shape):
    return pl.BlockSpec(shape, lambda *_: (0,) * len(shape))


def lamb_parts(weight, gradient, first_old, second_old):
    first_new = DECAY * first_old + (1.0 - DECAY) * gradient
    second_new = DECAY * second_old + (1.0 - DECAY) * gradient * gradient
    direction = (
        first_new / BIAS_FIRST / (jnp.sqrt(second_new / BIAS_SECOND) + ADAM_EPSILON)
        + WEIGHT_DECAY * weight
    )
    return (first_new, second_new, direction)


def total_of(values):
    while len(values.shape) > 2:
        values = jnp.sum(values, axis=0)
    return jnp.sum(jnp.sum(values, axis=1, keepdims=True), axis=0, keepdims=True)


def lamb_one(position, copies, gradient, olds, outs, norms):
    weight = olds[0][...]
    first_new, second_new, direction = lamb_parts(weight, gradient, olds[1][...], olds[2][...])
    outs[0][...] = gradient
    outs[1][...] = first_new
    outs[2][...] = second_new
    outs[3][...] = direction
    lanes = lane_ids((1, LANES))
    share = 1.0 / copies
    return (
        norms
        + jnp.where(lanes == position, total_of(weight * weight) * share, 0.0)
        + jnp.where(lanes == 8 + position, total_of(direction * direction) * share, 0.0)
    )


def pack_kernel(width, tensor_count, kept_ref, *refs):
    received = refs[:-1]
    packed_ref = refs[-1]
    maps_rows = packed_ref.shape[1] - 8
    lanes = slice(2 * width, 2 * width + MAPS)
    state = kept_ref[SMALL:, lanes]
    small = kept_ref[0:SMALL, width + LANES : width + LANES + MAPS]
    for ref in received:
        state = state + ref[SMALL:, lanes].astype(F32)
        small = small + ref[0:SMALL, width + LANES : width + LANES + MAPS].astype(F32)
    small = small[:8] + small[8:]
    for at in range(tensor_count):
        packed_ref[at, 0:8, :] = small
        packed_ref[at, 8:, :] = state[at * maps_rows : (at + 1) * maps_rows, :]


def lamb_wide_kernel(width, channels, heads, copies, count, kept_ref, *refs):
    received = refs[:count]
    olds = refs[count : count + 15]
    outs = refs[count + 15 : count + 35]
    norms_ref = refs[count + 35]
    whole = kept_ref[...]
    for ref in received:
        whole = whole + ref[...].astype(F32)
    columns = 2 * width + MAPS + LANES
    block = whole[SMALL:]
    small = whole[:8] + whole[8:SMALL]
    norms = jnp.zeros((1, LANES), F32)
    in_grad = jnp.stack([block[:, :channels], block[:, width : width + channels]], axis=1)
    step_grad = block[:, 2 * width + MAPS : 2 * width + MAPS + heads]
    out_grad = block[:, columns : columns + channels]
    channel_grad = small[: CONV + 2, :channels]
    picker = (
        lax.broadcasted_iota(jnp.int32, (width, LANES), 0) // HEAD
        == lax.broadcasted_iota(jnp.int32, (width, LANES), 1)
    ).astype(F32)
    skips = dot(small[:, :width], picker, precision=HIGHEST)
    head_grad = jnp.concatenate(
        [small[0:2, width : width + LANES], skips[6:7, :]], axis=0
    )[:, :heads]
    gradients = (in_grad, step_grad, out_grad, channel_grad, head_grad)
    for position, gradient in enumerate(gradients):
        norms = lamb_one(
            position,
            copies if position > 2 else 1.0,
            gradient,
            olds[position::5],
            outs[position::5],
            norms,
        )
    norms_ref[...] = norms


def lamb_maps_kernel(ids, packed_ref, *refs):
    olds = refs[:9]
    norms_in_ref = refs[9]
    outs = refs[10:22]
    norms_ref = refs[22]
    whole = jnp.sum(packed_ref[...], axis=0)
    small = whole[:8]
    conv_rows = olds[1].shape[0]
    gain_size = olds[2].shape[1]
    picker = (
        lax.broadcasted_iota(jnp.int32, (conv_rows, LANES), 0) + ids[1] * conv_rows
        == lax.broadcasted_iota(jnp.int32, (conv_rows, LANES), 1)
    ).astype(F32)
    conv_grad = dot(picker, small[:, :LANES], 1, 1, precision=HIGHEST)[:, : CONV + 1]
    gain_grad = pltpu.roll(small[:, LANES:], (LANES - ids[1] * gain_size) % LANES, 1)[
        0:1, :gain_size
    ]
    norms = norms_in_ref[...]
    for position, gradient in enumerate((whole[8:], conv_grad, gain_grad)):
        norms = lamb_one(
            5 + position, 1.0, gradient, olds[position::3], outs[position::3], norms
        )
    norms_ref[...] = jnp.broadcast_to(norms[None], norms_ref.shape)


def update_kernel(norms_ref, *refs):
    norms = jnp.sqrt(jnp.sum(norms_ref[...], axis=0))
    refs[-1][...] = jnp.concatenate([norms[:, :8], norms[:, 8:16]], axis=0)
    for position in range(8):
        ratio = -RATE * norms[:, position : position + 1] / norms[:, 8 + position : 9 + position]
        direction = refs[position][...]
        if direction.ndim == 3:
            ratio = ratio[None]
        refs[8 + position][...] = ratio * direction


def split_three(values):
    high = lax.reduce_precision(values, 8, 7)
    rest = values - high
    middle = lax.reduce_precision(rest, 8, 7)
    return [high.astype(BF), middle.astype(BF), (rest - middle).astype(BF)]


def local(*arguments):
    block_input, output_grad, lengths = arguments[:3]
    masters = arguments[3:11]
    firsts = arguments[11:19]
    seconds = arguments[19:27]
    (
        in_proj,
        step_proj,
        out_proj,
        channel_params,
        head_params,
        state_proj,
        state_conv,
        norm_gain,
    ) = masters
    dp_count = lax.axis_size("dp")
    tensor_count = lax.axis_size("tensor")
    dp_at = lax.axis_index("dp")
    tensor_at = lax.axis_index("tensor")
    everywhere = dp_count * tensor_count
    own_count, model = block_input.shape
    tokens = own_count * tensor_count
    chunks = tokens // SPAN
    own_chunks = own_count // SPAN
    rows = in_proj.shape[0]
    channels = in_proj.shape[2]
    heads = head_params.shape[1]
    width = -(-channels // LANES) * LANES
    mixed_width = width + MAPS
    columns = 2 * width + MAPS + LANES
    dp_low = low_count(dp_count)
    ids = jnp.stack([dp_at, tensor_at]).astype(jnp.int32)

    in_low = jnp.concatenate(
        [
            pad_to(in_proj[:, 0, :].astype(BF), 1, width),
            pad_to(in_proj[:, 1, :].astype(BF), 1, width),
            pad_to(step_proj.astype(BF), 1, LANES),
        ],
        axis=1,
    )
    out_low = pad_to(out_proj.astype(BF), 1, width)
    u_pieces = jnp.stack(gather_pieces(block_input, "tensor", 2))
    in_pieces = gather_pieces(in_low, "dp", dp_low)
    maps_rows = state_proj.shape[0]
    conv_rows = state_conv.shape[0]
    small_own = jnp.concatenate(
        split_three(state_conv.reshape(-1)) + split_three(norm_gain), axis=0
    )
    shared_own = jnp.concatenate(
        [state_proj.astype(BF), pad_to(small_own, 0, MAPS)[None, :]], axis=0
    )
    shared = lax.all_to_all(
        jnp.broadcast_to(shared_own[None], (everywhere,) + shared_own.shape),
        ("dp", "tensor"),
        0,
        0,
    )
    state_weight = shared[:, :maps_rows].reshape(-1, MAPS)
    small_all = shared[:, maps_rows].astype(F32)
    conv_size = conv_rows * (CONV + 1)
    conv_whole = sum(
        small_all[:, part * conv_size : (part + 1) * conv_size] for part in range(3)
    ).reshape(-1, CONV + 1)
    gain_base = 3 * conv_size
    gain_size = norm_gain.shape[0]
    gain_whole = sum(
        small_all[:, gain_base + part * gain_size : gain_base + (part + 1) * gain_size]
        for part in range(3)
    ).reshape(-1)
    grad_far = {
        high: exchange(output_grad, "tensor", high) for high in range(2, tensor_count, 2)
    }
    out_spread = lax.all_to_all(
        jnp.broadcast_to(out_low[None], (dp_count,) + out_low.shape), "dp", 0, 0
    ).reshape(model, width)
    if rows % 16 != 0:
        order = dp_at ^ jnp.arange(dp_count)
        in_pieces = [jnp.stack(in_pieces)[order].reshape(model, -1)]
    pieces = len(in_pieces)

    channel_wide = pad_to(channel_params, 1, width)
    taps = pad_to(
        jnp.concatenate([channel_wide[: CONV + 1], conv_whole.T], axis=1), 0, 8
    )
    heads_wide = pad_to(pad_to(head_params, 1, LANES), 0, 8)
    skip_wide = jnp.repeat(pad_to(head_params[2], 0, width // HEAD), HEAD)
    skip_gain = pad_to(jnp.stack([skip_wide, channel_wide[CONV + 1]]), 0, 8)
    gain_rows = pad_to(gain_whole[None, :], 0, 8)

    def token_spec(size, reverse=False):
        if reverse:
            return pl.BlockSpec((SPAN, size), lambda at, *_: (chunks - 1 - at, 0))
        return pl.BlockSpec((SPAN, size), lambda at, *_: (at, 0))

    def piece_spec(reverse=False):
        def index(at, ids_ref, *_):
            block = chunks - 1 - at if reverse else at
            return ((block // own_chunks) ^ ids_ref[1], block % own_chunks, 0)

        return pl.BlockSpec((1, SPAN, model), index)

    def struct(shape, dtype=F32):
        return jax.ShapeDtypeStruct(shape, dtype)

    arbitrary = pltpu.CompilerParams(
        dimension_semantics=("arbitrary",), vmem_limit_bytes=56 * 1024 * 1024
    )
    normed, gate_raw, raw, pre, act, step_in, states, mixed, weight = pl.pallas_call(
        functools.partial(forward_kernel, width, pieces, own_chunks),
        grid_spec=pltpu.PrefetchScalarGridSpec(
            num_scalar_prefetch=1,
            grid=(chunks,),
            in_specs=[piece_spec()]
            + [whole_spec(piece.shape) for piece in in_pieces]
            + [
                whole_spec(state_weight.shape),
                whole_spec(gain_rows.shape),
                whole_spec(taps.shape),
                whole_spec(heads_wide.shape),
                whole_spec(skip_gain.shape),
            ],
            out_specs=[
                token_spec(model),
                token_spec(width),
                token_spec(mixed_width),
                token_spec(mixed_width),
                token_spec(mixed_width),
                token_spec(LANES),
                pl.BlockSpec((1, width, STATE), lambda at, *_: (at, 0, 0)),
                token_spec(width),
                whole_spec((model, columns)),
            ],
            scratch_shapes=[
                pltpu.VMEM((SPAN + 8, mixed_width), F32),
                pltpu.VMEM((width, STATE), F32),
            ],
        ),
        out_shape=[
            struct((tokens, model), BF),
            struct((tokens, width)),
            struct((tokens, mixed_width)),
            struct((tokens, mixed_width)),
            struct((tokens, mixed_width), BF),
            struct((tokens, LANES)),
            struct((chunks, width, STATE)),
            struct((tokens, width)),
            struct((model, columns), BF),
        ],
        compiler_params=arbitrary,
        name="ssd_forward",
    )(ids, u_pieces, *in_pieces, state_weight, gain_rows, taps, heads_wide, skip_gain)

    masks_far = list(grad_far)
    *far, gate_raw = lax.optimization_barrier([grad_far[mask] for mask in masks_far] + [gate_raw])
    grad_far = dict(zip(masks_far, far))
    grad_far[0] = output_grad
    grad_pieces = jnp.stack(
        [
            exchange(grad_far[mask & ~1], "tensor", 1) if mask & 1 else grad_far[mask]
            for mask in range(tensor_count)
        ]
    )
    gate_gain_rows = pad_to(channel_wide[CONV + 1][None, :], 0, 8)
    merged_grad, branch_part, sums_part = pl.pallas_call(
        middle_kernel,
        grid_spec=pltpu.PrefetchScalarGridSpec(
            num_scalar_prefetch=2,
            grid=(chunks,),
            in_specs=[
                piece_spec(),
                token_spec(width),
                token_spec(width),
                whole_spec(out_spread.shape),
                whole_spec(gate_gain_rows.shape),
            ],
            out_specs=[
                token_spec(width),
                piece_spec(),
                pl.BlockSpec((2, SPAN), lambda at, *_: (0, at)),
            ],
        ),
        out_shape=[
            struct((tokens, width)),
            struct((tensor_count, own_count, model), BF),
            struct((2, tokens)),
        ],
        compiler_params=arbitrary,
        name="gate_middle",
    )(ids, lengths, grad_pieces, gate_raw, mixed, out_spread, gate_gain_rows)

    sums = sums_part
    bit = 1
    while bit < tensor_count:
        sums = sums + exchange(sums, "tensor", bit)
        bit *= 2

    masks = slot_masks(dp_count, dp_low)
    slot_columns = columns + width
    token_back = functools.partial(token_spec, reverse=True)
    normed_part, slots = pl.pallas_call(
        functools.partial(backward_kernel, width, masks),
        grid_spec=pltpu.PrefetchScalarGridSpec(
            num_scalar_prefetch=2,
            grid=(chunks,),
            in_specs=[
                pl.BlockSpec((2, SPAN), lambda at, *_: (0, chunks - 1 - at)),
                piece_spec(True),
                piece_spec(True),
                token_back(model),
                token_back(width),
                token_back(width),
                token_back(width),
                token_back(mixed_width),
                token_back(mixed_width),
                token_back(mixed_width),
                token_back(LANES),
                pl.BlockSpec((1, width, STATE), lambda at, *_: (chunks - 1 - at, 0, 0)),
                pl.BlockSpec(
                    (1, width, STATE), lambda at, *_: (jnp.minimum(chunks - at, chunks - 1), 0, 0)
                ),
                whole_spec((model, columns)),
                whole_spec(taps.shape),
                whole_spec(heads_wide.shape),
                whole_spec(skip_gain.shape),
                whole_spec(gain_rows.shape),
            ],
            out_specs=[
                piece_spec(True),
                whole_spec((dp_count, SMALL + rows, slot_columns)),
            ],
            scratch_shapes=[
                pltpu.VMEM((width, STATE), F32),
                pltpu.VMEM((SPAN + 8, mixed_width), F32),
                pltpu.VMEM((model, columns), F32),
                pltpu.VMEM((model, width), F32),
                pltpu.VMEM((8, mixed_width), F32),
                pltpu.VMEM((8, LANES), F32),
                pltpu.VMEM((8, model), F32),
            ],
        ),
        out_shape=[
            struct((tensor_count, own_count, model), BF),
            struct((dp_count, SMALL + rows, slot_columns), BF),
        ],
        compiler_params=arbitrary,
        name="ssd_backward",
    )(
        ids,
        lengths,
        sums,
        u_pieces,
        grad_pieces,
        normed,
        gate_raw,
        mixed,
        merged_grad,
        raw,
        pre,
        act,
        step_in,
        states,
        states,
        weight,
        taps,
        heads_wide,
        skip_gain,
        gain_rows,
    )

    def owner_sum(parts):
        ordered = jnp.stack([parts[mask] for mask in slot_masks(tensor_count, 2)])
        return scatter_sum(ordered, "tensor", 2)

    inputs = block_input.astype(F32)
    branch = owner_sum(branch_part)
    position_all = tensor_at * own_count + jnp.arange(own_count, dtype=jnp.int32)
    length_of = jnp.sum(
        jnp.where(
            (position_all // LMAX)[:, None]
            == jnp.arange(lengths.shape[0], dtype=jnp.int32)[None, :],
            lengths[None, :],
            0,
        ),
        axis=1,
    )
    live_own = (position_all % LMAX < length_of)[:, None]
    own_squares = lax.dynamic_slice(sums[0], (tensor_at * own_count,), (own_count,))
    own_scale = lax.rsqrt(own_squares / INNER + EPSILON)[:, None]
    output = (inputs + jnp.where(live_own, branch * own_scale, 0.0)).astype(BF)

    normed_grad = owner_sum(normed_part)
    scale = lax.rsqrt(jnp.mean(inputs * inputs, axis=-1, keepdims=True) + EPSILON)
    scaled_grad = normed_grad * gain_whole[None, :]
    input_grad = (
        output_grad.astype(F32)
        + scale * scaled_grad
        - inputs * scale**3 * jnp.mean(scaled_grad * inputs, axis=-1, keepdims=True)
    )

    kept, received = scatter_parts(slots, "dp", dp_low, SMALL // 2)
    whole_vmem = pl.BlockSpec(memory_space=pltpu.VMEM)
    plain = pltpu.CompilerParams(vmem_limit_bytes=48 * 1024 * 1024)
    packed = pl.pallas_call(
        functools.partial(pack_kernel, width, tensor_count),
        in_specs=[whole_vmem] * (1 + len(received)),
        out_specs=whole_vmem,
        out_shape=struct((tensor_count, maps_rows + 8, MAPS)),
        compiler_params=plain,
        name="pack_maps",
    )(kept, *received)
    maps_parts = lax.all_to_all(packed, "tensor", 0, 0)
    wide_shapes = [struct(weight_.shape) for weight_ in masters[:5]]
    wide = pl.pallas_call(
        functools.partial(
            lamb_wide_kernel, width, channels, heads, float(dp_count), len(received)
        ),
        in_specs=[whole_vmem] * (1 + len(received) + 15),
        out_specs=[whole_vmem] * 21,
        out_shape=wide_shapes * 4 + [struct((1, LANES))],
        compiler_params=plain,
        name="lamb_wide",
    )(kept, *received, *masters[:5], *firsts[:5], *seconds[:5])

    def flat(values):
        return [values[5], values[6], values[7][None, :]]

    maps_shapes = [struct(values.shape) for values in flat(masters)]
    maps = pl.pallas_call(
        lamb_maps_kernel,
        in_specs=[pl.BlockSpec(memory_space=pltpu.SMEM)] + [whole_vmem] * 11,
        out_specs=[whole_vmem] * 13,
        out_shape=maps_shapes * 4 + [struct((everywhere, 1, LANES))],
        compiler_params=plain,
        name="lamb_maps",
    )(ids, maps_parts, *flat(masters), *flat(firsts), *flat(seconds), wide[20])
    spread = lax.all_to_all(maps[12], ("dp", "tensor"), 0, 0)
    updates = pl.pallas_call(
        update_kernel,
        in_specs=[whole_vmem] * 9,
        out_specs=[whole_vmem] * 9,
        out_shape=wide_shapes + maps_shapes + [struct((2, 8))],
        compiler_params=plain,
        name="lamb_update",
    )(spread, *wide[15:20], *maps[9:12])

    def joined(kind):
        values = list(wide[5 * kind : 5 * kind + 5]) + list(maps[3 * kind : 3 * kind + 3])
        return tuple(values[:7]) + (values[7][0],)

    return (
        (output, input_grad)
        + joined(0)
        + joined(1)
        + joined(2)
        + tuple(updates[:7])
        + (updates[7][0], updates[8])
    )


WEIGHT_SPECS = (
    P("dp", None, "tensor"),
    P("dp", "tensor"),
    P("dp", "tensor"),
    P(None, "tensor"),
    P(None, "tensor"),
    P(("dp", "tensor"), None),
    P(("dp", "tensor"), None),
    P(("dp", "tensor")),
)


def solution(mesh):
    tokens = P(("dp", "tensor"), None)
    return jax.shard_map(
        local,
        mesh=mesh,
        in_specs=(tokens, tokens, P("dp")) + WEIGHT_SPECS * 3,
        out_specs=(tokens, tokens) + WEIGHT_SPECS * 4 + (P(),),
        check_vma=False,
    )
```

```python
import functools

import jax
import jax.numpy as jnp
from jax import lax
from jax.experimental import pallas as pl
from jax.experimental.pallas import tpu as pltpu
from jax.sharding import PartitionSpec as P

STATE = 128
CONV = 4
SPAN = 256
LMAX = 2048
INNER = 1536
HEAD = 64
MAPS = 2 * STATE
LANES = 128
SMALL = 16
VMEM = 60 * 1024 * 1024

EPSILON = 1e-05
ADAM_EPSILON = 1e-06
DECAY = 0.5
BIAS_FIRST = 0.875
BIAS_SECOND = 0.875
RATE = 0.3
WEIGHT_DECAY = 0.01
HIGHEST = lax.Precision.HIGHEST
BF = jnp.bfloat16
F32 = jnp.float32


def dot(left, right, left_dim=1, right_dim=0, precision=None):
    return lax.dot_general(
        left,
        right,
        (((left_dim,), (right_dim,)), ((), ())),
        precision=precision,
        preferred_element_type=F32,
    )


def exchange(values, axis, mask):
    count = lax.axis_size(axis)
    return lax.ppermute(values, axis, [(at, at ^ mask) for at in range(count)])


def low_count(count):
    low = 1
    while low * low * 4 <= count:
        low *= 2
    return low


def together(*values):
    return lax.optimization_barrier(values)


def gather_far(own, axis, low):
    return {high: exchange(own, axis, high) for high in range(low, lax.axis_size(axis), low)}


def gather_near(own, far, axis, low):
    count = lax.axis_size(axis)
    pieces = dict(far)
    pieces[0] = own
    for high in range(0, count, low):
        for near in range(1, low):
            pieces[high + near] = exchange(pieces[high], axis, near)
    return [pieces[mask] for mask in range(count)]


def slot_masks(count, low):
    return [high + near for near in range(low) for high in range(0, count, low)]


def near_sum(kept, sent, axis, low):
    highs = kept.shape[0]
    total = kept.astype(F32)
    for near in range(1, low):
        part = sent if low == 2 else sent[(near - 1) * highs : near * highs]
        total = total + exchange(part, axis, near).astype(F32)
    return total


def far_parts(total, axis, low):
    return [
        exchange(total[position].astype(BF), axis, position * low)
        for position in range(1, total.shape[0])
    ]


def lane_ids(shape):
    return lax.broadcasted_iota(jnp.int32, shape, len(shape) - 1)


def spread_heads(columns, heads):
    rows = columns.shape[0]
    left = lane_ids((rows, LANES)) < HEAD
    return jnp.concatenate(
        [
            jnp.where(left, columns[:, head : head + 1], columns[:, head + 1 : head + 2])
            for head in range(0, heads, 2)
        ],
        axis=1,
    )


def causal_mask():
    rows = lax.broadcasted_iota(jnp.int32, (SPAN, SPAN), 0)
    columns = lax.broadcasted_iota(jnp.int32, (SPAN, SPAN), 1)
    return rows >= columns


def step_terms(step_in, heads_ref):
    step = jnp.maximum(step_in, 0.0) + jnp.log1p(jnp.exp(-jnp.abs(step_in)))
    rate = jnp.exp(heads_ref[0:1, :])
    decay = -rate * step
    lower = causal_mask().astype(F32).astype(BF)
    cumulative = sum(dot(lower, part) for part in thirds(decay))
    return step, rate, decay, cumulative


def halves(values):
    high = values.astype(BF)
    return high, (values - high.astype(F32)).astype(BF)


def thirds(values):
    high = values.astype(BF)
    rest = values - high.astype(F32)
    middle = rest.astype(BF)
    return high, middle, (rest - middle.astype(F32)).astype(BF)


def sigmoid(values):
    return 1.0 / (1.0 + jnp.exp(-values))


def forward_kernel(channels, pieces, masks, owners, own_chunks, ids, *refs):
    width = channels
    heads = width // HEAD
    mixed_width = width + MAPS
    u_refs = refs[:owners]
    refs = refs[owners:]
    piece_refs = refs[:pieces]
    (
        state_w_ref,
        gain_ref,
        taps_ref,
        heads_ref,
        skip_ref,
        normed_ref,
        gate_ref,
        raw_ref,
        pre_ref,
        act_ref,
        step_ref,
        state_ref,
        mixed_ref,
        weight_ref,
        tail,
        carried,
        u_own,
    ) = refs[pieces:]
    at = pl.program_id(0)

    @pl.when(at == 0)
    def _():
        place_rows(
            ids,
            masks,
            piece_refs,
            (
                (slice(0, 2 * width), weight_ref, slice(0, 2 * width)),
                (
                    slice(2 * width, 2 * width + LANES),
                    weight_ref,
                    slice(2 * width + MAPS, 2 * width + MAPS + LANES),
                ),
            ),
        )
        weight_ref[:, 2 * width : 2 * width + MAPS] = state_w_ref[...]

    @pl.when(at % (LMAX // SPAN) == 0)
    def _():
        tail[0:8, :] = jnp.zeros((8, mixed_width), F32)
        carried[...] = jnp.zeros_like(carried)

    pick_piece(ids, at, own_chunks, u_refs, u_own)
    inputs = u_own[...].astype(F32)
    scale = lax.rsqrt(jnp.mean(inputs * inputs, axis=-1, keepdims=True) + EPSILON)
    normed = (inputs * scale * gain_ref[0:1, :]).astype(BF)
    normed_ref[...] = normed
    gate_ref[...] = dot(normed, weight_ref[:, :width])
    raw = dot(normed, weight_ref[:, width : 2 * width + MAPS])
    raw_ref[...] = raw
    tail[8:, :] = raw
    step_in = dot(normed, weight_ref[:, 2 * width + MAPS :]) + heads_ref[1:2, :]
    step_ref[...] = step_in
    pre = taps_ref[CONV : CONV + 1, :] + taps_ref[0:1, :] * tail[5 : 5 + SPAN, :]
    for tap in range(1, CONV):
        pre = pre + taps_ref[tap : tap + 1, :] * tail[5 + tap : 5 + tap + SPAN, :]
    tail[0:8, :] = tail[SPAN : SPAN + 8, :]
    pre_ref[...] = pre
    act = (pre * sigmoid(pre)).astype(BF)
    act_ref[...] = act
    signal = act[:, :width].astype(F32)
    b_rows = act[:, width : width + STATE]
    c_rows = act[:, width + STATE :]
    step, rate, decay, cumulative = step_terms(step_in, heads_ref)
    across_rows = jnp.transpose(cumulative)
    closing = cumulative[SPAN - 1 : SPAN, :]
    held = jnp.where(causal_mask(), dot(c_rows, b_rows, 1, 1), 0.0)
    weighted = (spread_heads(step, heads) * signal).astype(BF)
    left = lane_ids((SPAN, LANES)) < HEAD
    state = carried[...]
    state_ref[0] = state
    across = dot(
        jnp.concatenate([c_rows, c_rows], axis=1),
        jnp.concatenate(halves(state), axis=1),
        1,
        1,
    ) * spread_heads(jnp.exp(cumulative), heads)
    within = []
    for head in range(0, heads, 2):
        lanes = slice(head * HEAD, head * HEAD + LANES)
        pair = weighted[:, lanes]
        total = None
        for side in range(2):
            spread = (
                cumulative[:, head + side : head + side + 1]
                - across_rows[head + side : head + side + 1, :]
            )
            mixing = (held * jnp.exp(jnp.minimum(spread, 0.0))).astype(BF)
            kept = jnp.where(left if side == 0 else ~left, pair, jnp.zeros_like(pair))
            part = dot(mixing, kept)
            total = part if total is None else total + part
        within.append(total)
    mixed_ref[...] = jnp.concatenate(within, axis=1) + across + skip_ref[0:1, :] * signal
    ended = weighted.astype(F32) * spread_heads(jnp.exp(closing - cumulative), heads)
    fresh = sum(dot(part, b_rows, 0, 0) for part in halves(ended))
    kept_rate = jnp.exp(closing)
    for head in range(heads):
        rows = slice(head * HEAD, (head + 1) * HEAD)
        carried[rows, :] = kept_rate[:, head : head + 1] * state[rows, :] + fresh[rows, :]


def place_rows(ids, masks, refs, stores):
    at = 0
    for ref in refs:
        stacked = len(ref.shape) == 3
        for inner in range(ref.shape[0] if stacked else 1):
            rows = ref.shape[-2]
            if masks[at] is None:
                target = slice(None)
            else:
                target = pl.ds(pl.multiple_of((ids[0] ^ masks[at]) * rows, 8), rows)
            for columns, into, lanes in stores:
                into[target, lanes] = ref[inner, :, columns] if stacked else ref[:, columns]
            at += 1


def pick_piece(ids, block, own_chunks, refs, scratch):
    mask = (block // own_chunks) ^ ids[1]
    for at, ref in enumerate(refs):

        @pl.when(mask == at)
        def _():
            scratch[...] = ref[...]


def store_part(ids, block, own_chunks, refs, value):
    odd = ((block // own_chunks) ^ ids[1]) & 1
    for at, ref in enumerate(refs):

        @pl.when(odd == at)
        def _():
            ref[0] = value


def rows_live(ids, at, lengths):
    sequence = at // (LMAX // SPAN)
    position = (at % (LMAX // SPAN)) * SPAN + lax.broadcasted_iota(jnp.int32, (SPAN, 1), 0)
    return position < lengths[sequence]


def middle_kernel(owners, pieces, masks, own_chunks, ids, lengths, *refs):
    grad_refs = refs[:owners]
    piece_refs = refs[owners : owners + pieces]
    (
        gate_ref,
        mixed_ref,
        gain_ref,
        merged_grad_ref,
        kept_ref,
        sent_ref,
        sums_ref,
        grad_own,
        weight,
    ) = refs[owners + pieces :]
    at = pl.program_id(0)

    @pl.when(at == 0)
    def _():
        at_mask = 0
        for ref in piece_refs:
            count = ref.shape[0] if len(ref.shape) == 3 else 1
            place_rows(
                ids,
                masks[at_mask : at_mask + count],
                [ref],
                ((slice(ref.shape[-1] - weight.shape[1], ref.shape[-1]), weight, slice(None)),),
            )
            at_mask += count

    pick_piece(ids, at, own_chunks, grad_refs, grad_own)
    upstream = grad_own[...]
    upstream = jnp.where(rows_live(ids, at, lengths), upstream, jnp.zeros_like(upstream))
    merged_grad = dot(upstream, weight[...])
    merged_grad_ref[...] = merged_grad
    gate = gate_ref[...]
    gated = mixed_ref[...] * (gate * sigmoid(gate))
    gained = gated * gain_ref[0:1, :]
    squares = jnp.sum(gated * gated, axis=1, keepdims=True)
    products = jnp.sum(merged_grad * gained, axis=1, keepdims=True)
    branch = dot(gained.astype(BF), weight[...], 1, 1).astype(BF)
    store_part(ids, at, own_chunks, (kept_ref, sent_ref), branch)
    lanes = lane_ids((SPAN, LANES))
    both = jnp.where(lanes == 0, squares, jnp.where(lanes == 1, products, 0.0))
    sums_ref[...] = jnp.transpose(both)[0:2, :]


def backward_kernel(channels, masks, owners, own_chunks, ids, lengths, *refs):
    u_refs = refs[:owners]
    grad_refs = refs[owners : 2 * owners]
    sums_refs = refs[2 * owners : 3 * owners]
    backward_step(
        channels, masks, own_chunks, ids, lengths, u_refs, grad_refs, sums_refs, *refs[3 * owners :]
    )


def backward_step(
    channels,
    masks,
    own_chunks,
    ids,
    lengths,
    u_refs,
    grad_refs,
    sums_ref,
    normed_ref,
    gate_ref,
    mixed_ref,
    merged_grad_ref,
    raw_ref,
    pre_ref,
    act_ref,
    step_ref,
    state_ref,
    state_next_ref,
    weight_ref,
    taps_ref,
    heads_ref,
    skip_ref,
    gain_ref,
    part_kept_ref,
    part_sent_ref,
    first_kept_ref,
    first_sent_ref,
    *refs,
):
    low = low_count(len(masks))
    second_refs = refs[: len(masks) // low]
    backward_body(
        channels,
        masks,
        own_chunks,
        ids,
        lengths,
        u_refs,
        grad_refs,
        (sums_ref, normed_ref, gate_ref, mixed_ref, merged_grad_ref, raw_ref, pre_ref, act_ref),
        (step_ref, state_ref, state_next_ref, weight_ref, taps_ref, heads_ref, skip_ref, gain_ref),
        (part_kept_ref, part_sent_ref),
        (first_kept_ref, first_sent_ref, second_refs),
        *refs[len(masks) // low :],
    )


def backward_body(
    channels,
    masks,
    own_chunks,
    ids,
    lengths,
    u_refs,
    grad_refs,
    token_refs,
    other_refs,
    part_refs,
    slot_refs,
    carried,
    ahead,
    weight_sum,
    out_sum,
    tap_sum,
    head_sum,
    gain_sum,
    u_own,
    grad_own,
):
    sums_ref, normed_ref, gate_ref, mixed_ref, merged_grad_ref, raw_ref, pre_ref, act_ref = token_refs
    step_ref, state_ref, state_next_ref, weight_ref, taps_ref, heads_ref, skip_ref, gain_ref = other_refs
    first_kept_ref, first_sent_ref, second_refs = slot_refs
    width = channels
    heads = width // HEAD
    mixed_width = width + MAPS
    step_at = pl.program_id(0)
    at = pl.num_programs(0) - 1 - step_at

    @pl.when(step_at == 0)
    def _():
        weight_sum[...] = jnp.zeros_like(weight_sum)
        out_sum[...] = jnp.zeros_like(out_sum)
        tap_sum[...] = jnp.zeros_like(tap_sum)
        head_sum[...] = jnp.zeros_like(head_sum)
        gain_sum[...] = jnp.zeros_like(gain_sum)

    @pl.when(step_at % (LMAX // SPAN) == 0)
    def _():
        carried[...] = jnp.zeros_like(carried)
        ahead[SPAN:, :] = jnp.zeros((8, mixed_width), F32)

    pick_piece(ids, at, own_chunks, u_refs, u_own)
    pick_piece(ids, at, own_chunks, grad_refs, grad_own)
    sums = sum(ref[...] for ref in sums_ref)
    scale_row = lax.rsqrt(sums[0:1, :] / INNER + EPSILON)
    cross_row = scale_row * scale_row * scale_row * (sums[1:2, :] / INNER)
    row_ids = lax.broadcasted_iota(jnp.int32, (LANES, SPAN), 0)
    columns = jnp.transpose(jnp.where(row_ids == 0, scale_row, cross_row))
    gate_scale = columns[:, 0:1]
    cross = columns[:, 1:2]

    gate = gate_ref[...]
    gate_s = sigmoid(gate)
    gate_act = gate * gate_s
    mixed = mixed_ref[...]
    gated = mixed * gate_act
    merged_grad = merged_grad_ref[...]
    gain = skip_ref[1:2, :]
    scaled = gated * gate_scale
    tap_sum[5:6, :width] += jnp.sum(merged_grad * scaled, axis=0, keepdims=True)
    merged = (scaled * gain).astype(BF)
    upstream = grad_own[...]
    upstream = jnp.where(rows_live(ids, at, lengths), upstream, jnp.zeros_like(upstream))
    out_sum[...] += dot(upstream, merged, 0, 0)
    gated_grad = gate_scale * (merged_grad * gain) - gated * cross
    mixed_grad = gated_grad * gate_act
    gate_grad = gated_grad * mixed * (gate_s * (1.0 + gate * (1.0 - gate_s)))

    act = act_ref[...]
    signal = act[:, :width].astype(F32)
    b_rows = act[:, width : width + STATE]
    c_rows = act[:, width + STATE :]
    skip = skip_ref[0:1, :]
    tap_sum[6:7, :width] += jnp.sum(mixed_grad * signal, axis=0, keepdims=True)
    grad_high, grad_rest = halves(mixed_grad)
    grad_rows = grad_high.astype(F32) + grad_rest.astype(F32)

    step_in = step_ref[...]
    step, rate, decay, cumulative = step_terms(step_in, heads_ref)
    across_rows = jnp.transpose(cumulative)
    closing = cumulative[SPAN - 1 : SPAN, :]
    causal = causal_mask()
    held = jnp.where(causal, dot(c_rows, b_rows, 1, 1), 0.0)
    step_wide = spread_heads(step, heads)
    weighted = (step_wide * signal).astype(BF)
    weighted_rows = weighted.astype(F32)
    end_wide = spread_heads(jnp.exp(closing - cumulative), heads)
    state_grad = carried[...]
    state_parts = halves(state_grad)
    grown = halves(grad_rows * spread_heads(jnp.exp(cumulative), heads))
    before = halves(state_ref[0])
    c_grad = dot(grown[0], before[0]) + dot(grown[0], before[1]) + dot(grown[1], before[0])
    ended = halves(weighted_rows * end_wide)
    b_grad = (
        dot(ended[0], state_parts[0])
        + dot(ended[0], state_parts[1])
        + dot(ended[1], state_parts[0])
    )
    from_state = end_wide * dot(
        jnp.concatenate([b_rows, b_rows], axis=1), jnp.concatenate(state_parts, axis=1), 1, 1
    )
    left = lane_ids((SPAN, LANES)) < HEAD
    held_grad = None
    within = []
    for head in range(0, heads, 2):
        lanes = slice(head * HEAD, head * HEAD + LANES)
        pair = weighted[:, lanes]
        pair_twice = jnp.concatenate([pair, pair], axis=1)
        total = None
        for side in range(2):
            spread = (
                cumulative[:, head + side : head + side + 1]
                - across_rows[head + side : head + side + 1, :]
            )
            damping = jnp.exp(jnp.minimum(spread, 0.0))
            mixing = (held * damping).astype(BF)
            side_lanes = left if side == 0 else ~left
            kept = jnp.concatenate(
                [
                    jnp.where(side_lanes, part[:, lanes], jnp.zeros_like(pair))
                    for part in (grad_high, grad_rest)
                ],
                axis=1,
            )
            term = dot(kept, pair_twice, 1, 1) * damping
            held_grad = term if held_grad is None else held_grad + term
            part = dot(mixing, kept, 0, 0)
            total = part if total is None else total + part
        within.append(total[:, :LANES] + total[:, LANES:])
    held_low = jnp.where(causal, held_grad, 0.0).astype(BF)
    c_grad = c_grad + dot(held_low, b_rows)
    b_grad = b_grad + dot(held_low, c_rows, 0, 0)
    weighted_grad = jnp.concatenate(within, axis=1) + from_state
    fresh = sum(dot(part, c_rows, 0, 0) for part in grown)
    kept_rate = jnp.exp(closing)
    overlap = jnp.sum(state_grad * state_next_ref[0], axis=1, keepdims=True)
    lane_row = lane_ids((1, LANES))
    closing_grad = jnp.zeros((1, LANES), F32)
    for head in range(heads):
        rows = slice(head * HEAD, (head + 1) * HEAD)
        carried[rows, :] = kept_rate[:, head : head + 1] * state_grad[rows, :] + fresh[rows, :]
        closing_grad = closing_grad + jnp.where(
            lane_row == head, jnp.sum(overlap[rows, :], axis=0, keepdims=True), 0.0
        )
    picker = (
        lax.broadcasted_iota(jnp.int32, (width, LANES), 0) // HEAD
        == lax.broadcasted_iota(jnp.int32, (width, LANES), 1)
    ).astype(F32).astype(BF)
    shaped = mixed - skip * signal
    cumulative_grad = sum(
        dot(part, picker)
        for part in halves(grad_rows * shaped - weighted_rows * weighted_grad)
    )
    lower = causal.astype(F32).astype(BF)
    decay_grad = sum(dot(lower, part, 0, 0) for part in halves(cumulative_grad)) + closing_grad
    step_grad = (
        sum(dot(part, picker) for part in halves(signal * weighted_grad)) - rate * decay_grad
    )
    step_in_grad = step_grad * sigmoid(step_in)
    head_sum[0:1, :] += jnp.sum(decay * decay_grad, axis=0, keepdims=True)
    head_sum[1:2, :] += jnp.sum(step_in_grad, axis=0, keepdims=True)
    signal_grad = step_wide * weighted_grad + skip * mixed_grad

    pre = pre_ref[...]
    pre_s = sigmoid(pre)
    slope = pre_s * (1.0 + pre * (1.0 - pre_s))
    ahead[:SPAN, :] = jnp.concatenate([signal_grad, b_grad, c_grad], axis=1) * slope
    raw = raw_ref[...]
    raw_grad = None
    for shift in range(CONV):
        moved = ahead[shift : shift + SPAN, :]
        tap = CONV - 1 - shift
        term = taps_ref[tap : tap + 1, :] * moved
        raw_grad = term if raw_grad is None else raw_grad + term
        tap_sum[tap : tap + 1, :] += jnp.sum(raw * moved, axis=0, keepdims=True)
        if shift == 0:
            tap_sum[CONV : CONV + 1, :] += jnp.sum(moved, axis=0, keepdims=True)
    ahead[SPAN:, :] = ahead[0:8, :]

    low = jnp.concatenate(
        [gate_grad.astype(BF), raw_grad.astype(BF), step_in_grad.astype(BF)], axis=1
    )
    normed = normed_ref[...]
    weight_sum[...] += dot(normed, low, 0, 0)
    part = dot(low, weight_ref[...], 1, 1)
    store_part(ids, at, own_chunks, part_refs, part.astype(BF))
    inputs = u_own[...].astype(F32)
    scale = lax.rsqrt(jnp.mean(inputs * inputs, axis=-1, keepdims=True) + EPSILON)
    gain_sum[0:1, :] += jnp.sum(part * (inputs * scale), axis=0, keepdims=True)

    @pl.when(step_at == pl.num_programs(0) - 1)
    def _():
        rows = weight_sum.shape[0] // len(masks)
        model = weight_sum.shape[0]
        first = first_kept_ref.shape[2]
        kept_count = first_kept_ref.shape[0]
        step_lanes = weight_sum.shape[1] - first
        for place, mask in enumerate(masks):
            first_ref = first_kept_ref if place < kept_count else first_sent_ref
            position = place if place < kept_count else place - kept_count
            block = ids[0] ^ mask
            small = jnp.concatenate(
                [
                    tap_sum[:, :width],
                    head_sum[...],
                    pltpu.roll(
                        tap_sum[:, width:], (MAPS - block * (MAPS // len(masks))) % MAPS, 1
                    )[:, :LANES],
                    pltpu.roll(gain_sum[...], (model - block * rows) % model, 1)[:, :LANES],
                ],
                axis=1,
            )
            both = jnp.concatenate(halves(small), axis=0)
            picked = pl.ds(pl.multiple_of(block * rows, 8), rows)
            first_ref[position, 0:SMALL, : both.shape[1]] = both
            first_ref[position, 0:SMALL, both.shape[1] :] = jnp.zeros(
                (SMALL, first - both.shape[1]), BF
            )
            first_ref[position, SMALL:, :] = weight_sum[picked, :first].astype(BF)
            second_ref = second_refs[place % kept_count]
            near = place // kept_count
            second_ref[near, :, :step_lanes] = weight_sum[picked, first:].astype(BF)
            second_ref[near, :, step_lanes:] = out_sum[picked, :].astype(BF)


def pad_to(values, axis, size):
    if values.shape[axis] == size:
        return values
    pads = [(0, 0)] * values.ndim
    pads[axis] = (0, size - values.shape[axis])
    return jnp.pad(values, pads)


def whole_spec(shape):
    return pl.BlockSpec(shape, lambda *_: (0,) * len(shape))


def lamb_parts(weight, gradient, first_old, second_old):
    first_new = DECAY * first_old + (1.0 - DECAY) * gradient
    second_new = DECAY * second_old + (1.0 - DECAY) * gradient * gradient
    direction = (
        first_new / BIAS_FIRST / (jnp.sqrt(second_new / BIAS_SECOND) + ADAM_EPSILON)
        + WEIGHT_DECAY * weight
    )
    return (first_new, second_new, direction)


def total_of(values):
    while len(values.shape) > 2:
        values = jnp.sum(values, axis=0)
    return jnp.sum(jnp.sum(values, axis=1, keepdims=True), axis=0, keepdims=True)


def lamb_one(position, copies, gradient, olds, outs, norms):
    weight = olds[0][...]
    first_new, second_new, direction = lamb_parts(weight, gradient, olds[1][...], olds[2][...])
    outs[0][...] = gradient
    outs[1][...] = first_new
    outs[2][...] = second_new
    outs[3][...] = direction
    lanes = lane_ids((1, LANES))
    share = 1.0 / copies
    return (
        norms
        + jnp.where(lanes == position, total_of(weight * weight) * share, 0.0)
        + jnp.where(lanes == 8 + position, total_of(direction * direction) * share, 0.0)
    )


def pack_kernel(width, tensor_count, ids, kept_ref, *refs):
    received = refs[:-1]
    packed_ref = refs[-1]
    maps_rows = packed_ref.shape[1] - 8
    lanes = slice(2 * width, 2 * width + MAPS)
    state = kept_ref[SMALL:, lanes]
    small = kept_ref[0:SMALL, width + LANES : width + LANES + MAPS]
    for ref in received:
        state = state + ref[SMALL:, lanes].astype(F32)
        small = small + ref[0:SMALL, width + LANES : width + LANES + MAPS].astype(F32)
    small = small[:8] + small[8:]
    for at in range(tensor_count):
        packed_ref[at, 0:8, :] = small
        packed_ref[at, 8:, :] = state[at * maps_rows : (at + 1) * maps_rows, :]


def lamb_wide_kernel(width, channels, heads, copies, firsts, seconds, ids, *refs):
    whole = sum(ref[...].astype(F32) for ref in refs[:firsts])
    rest = sum(ref[...].astype(F32) for ref in refs[firsts : firsts + seconds])
    count = firsts + seconds
    olds = refs[count : count + 15]
    outs = refs[count + 15 : count + 35]
    norms_ref = refs[count + 35]
    block = whole[SMALL:]
    small = whole[:8] + whole[8:SMALL]
    norms = jnp.zeros((1, LANES), F32)
    in_grad = jnp.stack([block[:, :channels], block[:, width : width + channels]], axis=1)
    step_grad = jnp.transpose(rest[:, :LANES])[:heads]
    out_grad = rest[:, LANES : LANES + channels]
    channel_grad = small[: CONV + 2, :channels]
    picker = (
        lax.broadcasted_iota(jnp.int32, (width, LANES), 0) // HEAD
        == lax.broadcasted_iota(jnp.int32, (width, LANES), 1)
    ).astype(F32)
    skips = dot(small[:, :width], picker, precision=HIGHEST)
    head_grad = jnp.concatenate(
        [small[0:2, width : width + LANES], skips[6:7, :]], axis=0
    )[:, :heads]
    gradients = (in_grad, step_grad, out_grad, channel_grad, head_grad)
    for position, gradient in enumerate(gradients):
        norms = lamb_one(
            position,
            copies if position > 2 else 1.0,
            gradient,
            olds[position::5],
            outs[position::5],
            norms,
        )
    norms_ref[...] = norms


def lamb_maps_kernel(ids, packed_ref, *refs):
    olds = refs[:9]
    norms_in_ref = refs[9]
    outs = refs[10:22]
    norms_ref = refs[22]
    whole = jnp.sum(packed_ref[...], axis=0)
    small = whole[:8]
    conv_rows = olds[1].shape[0]
    gain_size = olds[2].shape[1]
    picker = (
        lax.broadcasted_iota(jnp.int32, (conv_rows, LANES), 0) + ids[1] * conv_rows
        == lax.broadcasted_iota(jnp.int32, (conv_rows, LANES), 1)
    ).astype(F32)
    conv_grad = dot(picker, small[:, :LANES], 1, 1, precision=HIGHEST)[:, : CONV + 1]
    gain_grad = pltpu.roll(small[:, LANES:], (LANES - ids[1] * gain_size) % LANES, 1)[
        0:1, :gain_size
    ]
    norms = norms_in_ref[...]
    for position, gradient in enumerate((whole[8:], conv_grad, gain_grad)):
        norms = lamb_one(
            5 + position, 1.0, gradient, olds[position::3], outs[position::3], norms
        )
    norms_ref[...] = jnp.broadcast_to(norms[None], norms_ref.shape)


def update_kernel(ids, norms_ref, *refs):
    norms = jnp.sqrt(jnp.sum(norms_ref[...], axis=0))
    refs[-1][...] = jnp.concatenate([norms[:, :8], norms[:, 8:16]], axis=0)
    for position in range(8):
        ratio = -RATE * norms[:, position : position + 1] / norms[:, 8 + position : 9 + position]
        direction = refs[position][...]
        if direction.ndim == 3:
            ratio = ratio[None]
        refs[8 + position][...] = ratio * direction


def split_three(values):
    high = lax.reduce_precision(values, 8, 7)
    rest = values - high
    middle = lax.reduce_precision(rest, 8, 7)
    return [high.astype(BF), middle.astype(BF), (rest - middle).astype(BF)]


def local(*arguments):
    block_input, output_grad, lengths = arguments[:3]
    masters = arguments[3:11]
    firsts = arguments[11:19]
    seconds = arguments[19:27]
    (
        in_proj,
        step_proj,
        out_proj,
        channel_params,
        head_params,
        state_proj,
        state_conv,
        norm_gain,
    ) = masters
    dp_count = lax.axis_size("dp")
    tensor_count = lax.axis_size("tensor")
    dp_at = lax.axis_index("dp")
    tensor_at = lax.axis_index("tensor")
    everywhere = dp_count * tensor_count
    own_count, model = block_input.shape
    tokens = own_count * tensor_count
    chunks = tokens // SPAN
    own_chunks = own_count // SPAN
    rows = in_proj.shape[0]
    channels = in_proj.shape[2]
    heads = head_params.shape[1]
    width = -(-channels // LANES) * LANES
    mixed_width = width + MAPS
    columns = 2 * width + MAPS + LANES
    dp_low = low_count(dp_count)
    ids = jnp.stack([dp_at, tensor_at]).astype(jnp.int32)

    in_low = jnp.concatenate(
        [
            pad_to(in_proj[:, 0, :].astype(BF), 1, width),
            pad_to(in_proj[:, 1, :].astype(BF), 1, width),
            pad_to(step_proj.astype(BF), 1, LANES),
        ],
        axis=1,
    )
    out_low = pad_to(out_proj.astype(BF), 1, width)
    both_low = jnp.concatenate([in_low, out_low], axis=1)
    split = in_low.shape[1]
    highs = list(range(dp_low, dp_count, dp_low))
    nears = list(range(1, dp_low))
    tensor_highs = list(range(2, tensor_count, 2))
    landed = together(
        *[exchange(block_input, "tensor", mask) for mask in tensor_highs],
        *[exchange(both_low, "dp", mask) for mask in highs],
        *[exchange(both_low, "dp", mask) for mask in nears],
    )
    u_far = dict(zip(tensor_highs, landed))
    both_far = list(landed[len(tensor_highs) : len(tensor_highs) + len(highs)])
    both_near = list(landed[len(tensor_highs) + len(highs) :])
    maps_rows = state_proj.shape[0]
    conv_rows = state_conv.shape[0]
    small_own = jnp.concatenate(
        split_three(state_conv.reshape(-1)) + split_three(norm_gain), axis=0
    )
    shared_own = jnp.concatenate(
        [state_proj.astype(BF), pad_to(small_own, 0, MAPS)[None, :]], axis=0
    )
    shared_own, *both_far = together(shared_own, *both_far)
    in_stack = jnp.stack([piece[:, :split] for piece in both_far])
    out_stack = jnp.stack([piece[:, split:] for piece in both_far])
    shared = lax.all_to_all(
        jnp.broadcast_to(shared_own[None], (everywhere,) + shared_own.shape),
        ("dp", "tensor"),
        0,
        0,
    )
    u_pieces = gather_near(block_input, u_far, "tensor", 2)
    shared, *landed = together(
        shared, *u_pieces[1:], *[exchange(in_stack, "dp", near) for near in nears]
    )
    u_pieces = [block_input] + landed[: tensor_count - 1]
    in_near = landed[tensor_count - 1 :]
    grad_own, out_stack, *_ = together(output_grad, out_stack, u_far[2])
    grad_far = gather_far(grad_own, "tensor", 2)
    out_near = [exchange(out_stack, "dp", near) for near in nears]
    in_pieces = [both_low] + both_near + both_far + in_near
    piece_masks = [0] + nears + highs + [high + near for near in nears for high in highs]
    direct = rows % 16 == 0
    if not direct:
        order = dp_at ^ jnp.arange(dp_count)
        order = jnp.array([piece_masks.index(mask) for mask in range(dp_count)])[order]

        def ordered(pieces):
            parts = [piece if piece.ndim == 3 else piece[None] for piece in pieces]
            return jnp.concatenate(parts, axis=0)[order].reshape(model, -1)

        in_pieces = [
            ordered([piece[:, :split] for piece in [both_low] + both_near + both_far] + in_near)
        ]
    state_weight = shared[:, :maps_rows].reshape(-1, MAPS)
    small_all = shared[:, maps_rows].astype(F32)
    conv_size = conv_rows * (CONV + 1)
    conv_whole = sum(
        small_all[:, part * conv_size : (part + 1) * conv_size] for part in range(3)
    ).reshape(-1, CONV + 1)
    gain_base = 3 * conv_size
    gain_size = norm_gain.shape[0]
    gain_whole = sum(
        small_all[:, gain_base + part * gain_size : gain_base + (part + 1) * gain_size]
        for part in range(3)
    ).reshape(-1)
    channel_wide = pad_to(channel_params, 1, width)
    taps = pad_to(
        jnp.concatenate([channel_wide[: CONV + 1], conv_whole.T], axis=1), 0, 8
    )
    heads_wide = pad_to(pad_to(head_params, 1, LANES), 0, 8)
    skip_wide = jnp.repeat(pad_to(head_params[2], 0, width // HEAD), HEAD)
    skip_gain = pad_to(jnp.stack([skip_wide, channel_wide[CONV + 1]]), 0, 8)
    gain_rows = pad_to(gain_whole[None, :], 0, 8)

    def token_spec(size, reverse=False):
        if reverse:
            return pl.BlockSpec((SPAN, size), lambda at, *_: (chunks - 1 - at, 0))
        return pl.BlockSpec((SPAN, size), lambda at, *_: (at, 0))

    def piece_specs(reverse=False):
        def spec(mask):
            def index(at, ids_ref, *_):
                block = chunks - 1 - at if reverse else at
                mine = (block // own_chunks) ^ ids_ref[1] == mask
                return (jnp.where(mine, block % own_chunks, 0), 0)

            return pl.BlockSpec((SPAN, model), index)

        return [spec(mask) for mask in range(tensor_count)]

    def part_specs(reverse=False):
        def spec(odd):
            def index(at, ids_ref, *_):
                block = chunks - 1 - at if reverse else at
                owner = block // own_chunks
                inner = block % own_chunks
                mine = ((owner ^ ids_ref[1]) & 1) == odd
                if reverse:
                    other = jnp.where(owner > 0, owner - 1, 1)
                    other_inner = jnp.where(owner > 0, own_chunks - 1, 0)
                else:
                    last = tensor_count - 1
                    other = jnp.where(owner < last, owner + 1, last - 1)
                    other_inner = jnp.where(owner < last, 0, own_chunks - 1)
                owner = jnp.where(mine, owner, other)
                return ((owner ^ ids_ref[1]) >> 1, jnp.where(mine, inner, other_inner), 0)

            return pl.BlockSpec((1, SPAN, model), index)

        return [spec(0), spec(1)]

    def struct(shape, dtype=F32):
        return jax.ShapeDtypeStruct(shape, dtype)

    arbitrary = pltpu.CompilerParams(
        dimension_semantics=("arbitrary",), vmem_limit_bytes=VMEM
    )
    if not direct:
        piece_masks = [None]
    normed, gate_raw, raw, pre, act, step_in, states, mixed, weight = pl.pallas_call(
        functools.partial(forward_kernel, width, len(in_pieces), piece_masks, tensor_count, own_chunks),
        grid_spec=pltpu.PrefetchScalarGridSpec(
            num_scalar_prefetch=1,
            grid=(chunks,),
            in_specs=piece_specs()
            + [whole_spec(piece.shape) for piece in in_pieces]
            + [
                whole_spec(state_weight.shape),
                whole_spec(gain_rows.shape),
                whole_spec(taps.shape),
                whole_spec(heads_wide.shape),
                whole_spec(skip_gain.shape),
            ],
            out_specs=[
                token_spec(model),
                token_spec(width),
                token_spec(mixed_width),
                token_spec(mixed_width),
                token_spec(mixed_width),
                token_spec(LANES),
                pl.BlockSpec((1, width, STATE), lambda at, *_: (at, 0, 0)),
                token_spec(width),
                whole_spec((model, columns)),
            ],
            scratch_shapes=[
                pltpu.VMEM((SPAN + 8, mixed_width), F32),
                pltpu.VMEM((width, STATE), F32),
                pltpu.VMEM((SPAN, model), BF),
            ],
        ),
        out_shape=[
            struct((tokens, model), BF),
            struct((tokens, width)),
            struct((tokens, mixed_width)),
            struct((tokens, mixed_width)),
            struct((tokens, mixed_width), BF),
            struct((tokens, LANES)),
            struct((chunks, width, STATE)),
            struct((tokens, width)),
            struct((model, columns), BF),
        ],
        compiler_params=arbitrary,
        name="ssd_forward",
    )(ids, *u_pieces, *in_pieces, state_weight, gain_rows, taps, heads_wide, skip_gain)

    gate_raw, *landed = together(gate_raw, *grad_far.values(), *out_near)
    grad_far = dict(zip(grad_far, landed))
    out_near = landed[len(grad_far) :]
    grad_pieces = gather_near(grad_own, grad_far, "tensor", 2)
    out_pieces = [both_low] + both_near + both_far + out_near
    if not direct:
        out_pieces = [
            ordered([piece[:, split:] for piece in [both_low] + both_near + both_far] + out_near)
        ]
    gate_gain_rows = pad_to(channel_wide[CONV + 1][None, :], 0, 8)
    merged_grad, *branch_parts, sums_part = pl.pallas_call(
        functools.partial(middle_kernel, tensor_count, len(out_pieces), piece_masks, own_chunks),
        grid_spec=pltpu.PrefetchScalarGridSpec(
            num_scalar_prefetch=2,
            grid=(chunks,),
            in_specs=[
                *piece_specs(),
                *[whole_spec(piece.shape) for piece in out_pieces],
                token_spec(width),
                token_spec(width),
                whole_spec(gate_gain_rows.shape),
            ],
            out_specs=[
                token_spec(width),
                *part_specs(),
                pl.BlockSpec((2, SPAN), lambda at, *_: (0, at)),
            ],
            scratch_shapes=[pltpu.VMEM((SPAN, model), BF), pltpu.VMEM((model, width), BF)],
        ),
        out_shape=[
            struct((tokens, width)),
            *[struct((tensor_count // 2, own_count, model), BF)] * 2,
            struct((2, tokens)),
        ],
        compiler_params=arbitrary,
        name="gate_middle",
    )(ids, lengths, *grad_pieces, *out_pieces, gate_raw, mixed, gate_gain_rows)

    branch_total = near_sum(*branch_parts, "tensor", 2)
    branch_total, *sums = together(
        branch_total, *[exchange(sums_part, "tensor", mask) for mask in range(1, tensor_count)]
    )
    sums = [sums_part] + sums
    branch_far = far_parts(branch_total, "tensor", 2)
    masks = slot_masks(dp_count, dp_low)
    first_columns = 2 * width + MAPS
    second_columns = LANES + width
    kept_slots = dp_count // dp_low
    token_back = functools.partial(token_spec, reverse=True)
    normed_kept, normed_sent, first_kept, first_sent, *seconds_out = pl.pallas_call(
        functools.partial(backward_kernel, width, masks, tensor_count, own_chunks),
        grid_spec=pltpu.PrefetchScalarGridSpec(
            num_scalar_prefetch=2,
            grid=(chunks,),
            in_specs=[
                *piece_specs(True),
                *piece_specs(True),
                *[pl.BlockSpec((2, SPAN), lambda at, *_: (0, chunks - 1 - at))] * tensor_count,
                token_back(model),
                token_back(width),
                token_back(width),
                token_back(width),
                token_back(mixed_width),
                token_back(mixed_width),
                token_back(mixed_width),
                token_back(LANES),
                pl.BlockSpec((1, width, STATE), lambda at, *_: (chunks - 1 - at, 0, 0)),
                pl.BlockSpec(
                    (1, width, STATE), lambda at, *_: (jnp.minimum(chunks - at, chunks - 1), 0, 0)
                ),
                whole_spec((model, columns)),
                whole_spec(taps.shape),
                whole_spec(heads_wide.shape),
                whole_spec(skip_gain.shape),
                whole_spec(gain_rows.shape),
            ],
            out_specs=[
                *part_specs(True),
                whole_spec((kept_slots, SMALL + rows, first_columns)),
                whole_spec((dp_count - kept_slots, SMALL + rows, first_columns)),
                *[whole_spec((dp_low, rows, second_columns))] * kept_slots,
            ],
            scratch_shapes=[
                pltpu.VMEM((width, STATE), F32),
                pltpu.VMEM((SPAN + 8, mixed_width), F32),
                pltpu.VMEM((model, columns), F32),
                pltpu.VMEM((model, width), F32),
                pltpu.VMEM((8, mixed_width), F32),
                pltpu.VMEM((8, LANES), F32),
                pltpu.VMEM((8, model), F32),
                pltpu.VMEM((SPAN, model), BF),
                pltpu.VMEM((SPAN, model), BF),
            ],
        ),
        out_shape=[
            *[struct((tensor_count // 2, own_count, model), BF)] * 2,
            struct((kept_slots, SMALL + rows, first_columns), BF),
            struct((dp_count - kept_slots, SMALL + rows, first_columns), BF),
            *[struct((dp_low, rows, second_columns), BF)] * kept_slots,
        ],
        compiler_params=arbitrary,
        name="ssd_backward",
    )(
        ids,
        lengths,
        *u_pieces,
        *grad_pieces,
        *sums,
        normed,
        gate_raw,
        mixed,
        merged_grad,
        raw,
        pre,
        act,
        step_in,
        states,
        states,
        weight,
        taps,
        heads_wide,
        skip_gain,
        gain_rows,
    )

    first_kept, first_sent, *branch_far = together(first_kept, first_sent, *branch_far)
    highs_count = first_kept.shape[0]
    first_near = [
        exchange(
            first_sent
            if dp_low == 2
            else first_sent[(near - 1) * highs_count : near * highs_count],
            "dp",
            near,
        )
        for near in nears
    ]
    second_far = [
        exchange(seconds_out[position], "dp", position * dp_low)
        for position in range(1, kept_slots)
    ]
    normed_near = exchange(normed_sent, "tensor", 1)
    landed = together(normed_near, *first_near, *second_far)
    normed_total = normed_kept.astype(F32) + landed[0].astype(F32)
    first_total = first_kept.astype(F32)
    for values in landed[1 : 1 + len(first_near)]:
        first_total = first_total + values.astype(F32)
    second_far = landed[1 + len(first_near) :]
    joined = first_total[:, : SMALL // 2] + first_total[:, SMALL // 2 : SMALL]
    high = lax.reduce_precision(joined, 8, 7)
    first_total = jnp.concatenate([high, joined - high, first_total[:, SMALL:]], axis=1)
    first_parts = [first_total[0]] + far_parts(first_total, "dp", dp_low)
    second_total = seconds_out[0].astype(F32)
    for values in second_far:
        second_total = second_total + values.astype(F32)
    second_parts = [second_total[0]] + [
        exchange(second_total[near].astype(BF), "dp", near) for near in range(1, dp_low)
    ]
    landed = together(*first_parts, *second_parts)
    first_parts = landed[: len(first_parts)]
    second_parts = landed[len(first_parts) :]

    inputs = block_input.astype(F32)
    position_all = tensor_at * own_count + jnp.arange(own_count, dtype=jnp.int32)
    length_of = jnp.sum(
        jnp.where(
            (position_all // LMAX)[:, None]
            == jnp.arange(lengths.shape[0], dtype=jnp.int32)[None, :],
            lengths[None, :],
            0,
        ),
        axis=1,
    )
    live_own = (position_all % LMAX < length_of)[:, None]
    own_squares = lax.dynamic_slice(sum(part[0] for part in sums), (tensor_at * own_count,), (own_count,))
    own_scale = lax.rsqrt(own_squares / INNER + EPSILON)[:, None]
    branch = branch_total[0]
    for values in branch_far:
        branch = branch + values.astype(F32)
    output = (inputs + jnp.where(live_own, branch * own_scale, 0.0)).astype(BF)
    normed_grad = normed_total[0]
    for values in far_parts(normed_total, "tensor", 2):
        normed_grad = normed_grad + values.astype(F32)
    scale = lax.rsqrt(jnp.mean(inputs * inputs, axis=-1, keepdims=True) + EPSILON)
    scaled_grad = normed_grad * gain_whole[None, :]
    input_grad = (
        output_grad.astype(F32)
        + scale * scaled_grad
        - inputs * scale**3 * jnp.mean(scaled_grad * inputs, axis=-1, keepdims=True)
    )

    plain = pltpu.CompilerParams(
        dimension_semantics=("arbitrary",), vmem_limit_bytes=VMEM
    )

    def whole_call(kernel, operands, shapes, name):
        return pl.pallas_call(
            kernel,
            grid_spec=pltpu.PrefetchScalarGridSpec(
                num_scalar_prefetch=1,
                grid=(1,),
                in_specs=[whole_spec(value.shape) for value in operands],
                out_specs=[whole_spec(shape.shape) for shape in shapes],
            ),
            out_shape=shapes,
            compiler_params=plain,
            name=name,
        )(ids, *operands)

    (packed,) = whole_call(
        functools.partial(pack_kernel, width, tensor_count),
        first_parts,
        [struct((tensor_count, maps_rows + 8, MAPS))],
        "pack_maps",
    )
    maps_parts = lax.all_to_all(packed, "tensor", 0, 0)
    def wide_of(values):
        return [values[0], values[1].T] + list(values[2:5])

    wide_shapes = [struct(values.shape) for values in wide_of(masters)]
    wide = whole_call(
        functools.partial(
            lamb_wide_kernel,
            width,
            channels,
            heads,
            float(dp_count),
            len(first_parts),
            len(second_parts),
        ),
        [*first_parts, *second_parts, *wide_of(masters), *wide_of(firsts), *wide_of(seconds)],
        wide_shapes * 4 + [struct((1, LANES))],
        "lamb_wide",
    )

    def flat(values):
        return [values[5], values[6], values[7][None, :]]

    maps_shapes = [struct(values.shape) for values in flat(masters)]
    maps = whole_call(
        lamb_maps_kernel,
        [maps_parts, *flat(masters), *flat(firsts), *flat(seconds), wide[20]],
        maps_shapes * 4 + [struct((everywhere, 1, LANES))],
        "lamb_maps",
    )
    spread = lax.all_to_all(maps[12], ("dp", "tensor"), 0, 0)
    spread, input_grad, output = together(spread, input_grad, output)
    updates = whole_call(
        update_kernel,
        [spread, *wide[15:20], *maps[9:12]],
        wide_shapes + maps_shapes + [struct((2, 8))],
        "lamb_update",
    )

    def joined(kind):
        values = list(wide[5 * kind : 5 * kind + 5]) + list(maps[3 * kind : 3 * kind + 3])
        return (values[0], values[1].T) + tuple(values[2:7]) + (values[7][0],)

    return (
        (output, input_grad)
        + joined(0)
        + joined(1)
        + joined(2)
        + (updates[0], updates[1].T)
        + tuple(updates[2:7])
        + (updates[7][0], updates[8])
    )


WEIGHT_SPECS = (
    P("dp", None, "tensor"),
    P("dp", "tensor"),
    P("dp", "tensor"),
    P(None, "tensor"),
    P(None, "tensor"),
    P(("dp", "tensor"), None),
    P(("dp", "tensor"), None),
    P(("dp", "tensor")),
)


def solution(mesh):
    tokens = P(("dp", "tensor"), None)
    return jax.shard_map(
        local,
        mesh=mesh,
        in_specs=(tokens, tokens, P("dp")) + WEIGHT_SPECS * 3,
        out_specs=(tokens, tokens) + WEIGHT_SPECS * 4 + (P(),),
        check_vma=False,
    )
```

```python
import functools

import jax
import jax.numpy as jnp
from jax import lax
from jax.experimental import pallas as pl
from jax.experimental.pallas import tpu as pltpu
from jax.sharding import PartitionSpec as P

STATE = 128
CONV = 4
SPAN = 256
LMAX = 2048
INNER = 1536
HEAD = 64
MAPS = 2 * STATE
LANES = 128
SMALL = 16
VMEM = 60 * 1024 * 1024

EPSILON = 1e-05
ADAM_EPSILON = 1e-06
DECAY = 0.5
BIAS_FIRST = 0.875
BIAS_SECOND = 0.875
RATE = 0.3
WEIGHT_DECAY = 0.01
HIGHEST = lax.Precision.HIGHEST
BF = jnp.bfloat16
F32 = jnp.float32


def dot(left, right, left_dim=1, right_dim=0, precision=None):
    return lax.dot_general(
        left,
        right,
        (((left_dim,), (right_dim,)), ((), ())),
        precision=precision,
        preferred_element_type=F32,
    )


def exchange(values, axis, mask):
    count = lax.axis_size(axis)
    return lax.ppermute(values, axis, [(at, at ^ mask) for at in range(count)])


def low_count(count):
    low = 1
    while low * low * 4 <= count:
        low *= 2
    return low


def together(*values):
    return lax.optimization_barrier(values)


def gather_far(own, axis, low):
    return {high: exchange(own, axis, high) for high in range(low, lax.axis_size(axis), low)}


def gather_near(own, far, axis, low):
    count = lax.axis_size(axis)
    pieces = dict(far)
    pieces[0] = own
    for high in range(0, count, low):
        for near in range(1, low):
            pieces[high + near] = exchange(pieces[high], axis, near)
    return [pieces[mask] for mask in range(count)]


def slot_masks(count, low):
    return [high + near for near in range(low) for high in range(0, count, low)]


def near_sum(kept, sent, axis, low):
    highs = kept.shape[0]
    total = kept.astype(F32)
    for near in range(1, low):
        part = sent if low == 2 else sent[(near - 1) * highs : near * highs]
        total = total + exchange(part, axis, near).astype(F32)
    return total


def far_parts(total, axis, low):
    return [
        exchange(total[position].astype(BF), axis, position * low)
        for position in range(1, total.shape[0])
    ]


def lane_ids(shape):
    return lax.broadcasted_iota(jnp.int32, shape, len(shape) - 1)


def lower_mask(size):
    rows = lax.broadcasted_iota(jnp.int32, (size, size), 0)
    columns = lax.broadcasted_iota(jnp.int32, (size, size), 1)
    return rows >= columns


def paired(left, values, head):
    return jnp.where(left, values[:, head : head + 1], values[:, head + 1 : head + 2])


HALF = SPAN // 2
UP = slice(0, HALF)
DOWN = slice(HALF, SPAN)


def halves(values):
    high = values.astype(BF)
    return high, (values - high.astype(F32)).astype(BF)


def thirds(values):
    high = values.astype(BF)
    rest = values - high.astype(F32)
    middle = rest.astype(BF)
    return high, middle, (rest - middle.astype(F32)).astype(BF)


def sigmoid(values):
    return 0.5 * jnp.tanh(0.5 * values) + 0.5


def forward_kernel(channels, pieces, masks, owners, own_chunks, ids, *refs):
    width = channels
    heads = width // HEAD
    mixed_width = width + MAPS
    u_refs = refs[:owners]
    refs = refs[owners:]
    piece_refs = refs[:pieces]
    (
        state_w_ref,
        gain_ref,
        taps_ref,
        heads_ref,
        skip_ref,
        normed_ref,
        gate_ref,
        raw_ref,
        pre_ref,
        act_ref,
        step_ref,
        state_ref,
        mixed_ref,
        weight_ref,
        tail,
        carried,
        u_own,
    ) = refs[pieces:]
    at = pl.program_id(0)

    @pl.when(at == 0)
    def _():
        place_rows(
            ids,
            masks,
            piece_refs,
            (
                (slice(0, 2 * width), weight_ref, slice(0, 2 * width)),
                (
                    slice(2 * width, 2 * width + LANES),
                    weight_ref,
                    slice(2 * width + MAPS, 2 * width + MAPS + LANES),
                ),
            ),
        )
        weight_ref[:, 2 * width : 2 * width + MAPS] = state_w_ref[...]

    @pl.when(at % (LMAX // SPAN) == 0)
    def _():
        tail[0:8, :] = jnp.zeros((8, mixed_width), F32)
        carried[...] = jnp.zeros_like(carried)

    pick_piece(ids, at, own_chunks, u_refs, u_own)
    inputs = u_own[...].astype(F32)
    scale = lax.rsqrt(jnp.mean(inputs * inputs, axis=-1, keepdims=True) + EPSILON)
    normed = (inputs * scale * gain_ref[0:1, :]).astype(BF)
    normed_ref[...] = normed
    gate_ref[...] = dot(normed, weight_ref[:, :width])
    raw = dot(normed, weight_ref[:, width : 2 * width + MAPS])
    raw_ref[...] = raw
    tail[8:, :] = raw
    step_in = dot(normed, weight_ref[:, 2 * width + MAPS :]) + heads_ref[1:2, :]
    step_ref[:, :LANES] = step_in
    pre = taps_ref[CONV : CONV + 1, :] + taps_ref[0:1, :] * tail[5 : 5 + SPAN, :]
    for tap in range(1, CONV):
        pre = pre + taps_ref[tap : tap + 1, :] * tail[5 + tap : 5 + tap + SPAN, :]
    tail[0:8, :] = tail[SPAN : SPAN + 8, :]
    pre_ref[...] = pre
    act = (pre * sigmoid(pre)).astype(BF)
    act_ref[...] = act
    signal = act[:, :width].astype(F32)
    b_rows = act[:, width : width + STATE]
    c_rows = act[:, width + STATE :]
    step = jnp.maximum(step_in, 0.0) + jnp.log1p(jnp.exp(-jnp.abs(step_in)))
    decay = -jnp.exp(heads_ref[0:1, :]) * step
    lower = lower_mask(SPAN).astype(F32).astype(BF)
    cumulative = sum(dot(lower, part) for part in thirds(decay))
    step_ref[:, LANES : 2 * LANES] = step
    step_ref[:, 2 * LANES :] = cumulative
    across_rows = jnp.transpose(cumulative)
    closing = cumulative[SPAN - 1 : SPAN, :]
    mask = lower_mask(HALF)
    held_first = jnp.where(mask, dot(c_rows[UP], b_rows[UP], 1, 1), 0.0)
    held_cross = dot(c_rows[DOWN], b_rows[UP], 1, 1)
    held_last = jnp.where(mask, dot(c_rows[DOWN], b_rows[DOWN], 1, 1), 0.0)
    left = lane_ids((SPAN, LANES)) < HEAD
    left_row = left[0:1]
    state = carried[...]
    state_ref[0] = state
    across = dot(
        jnp.concatenate([c_rows, c_rows], axis=1), jnp.concatenate(halves(state), axis=0)
    )
    ended = []
    ends = []
    for head in range(0, heads, 2):
        lanes = slice(head * HEAD, head * HEAD + LANES)
        wide = [
            jnp.broadcast_to(cumulative[:, head + side : head + side + 1], (SPAN, LANES))
            for side in range(2)
        ]
        own = jnp.where(left, wide[0], wide[1])
        end = paired(left_row, closing, head)
        pair = (paired(left, step, head) * signal[:, lanes]).astype(BF)
        first = None
        for side in range(2):
            column = wide[side]
            row = across_rows[head + side : head + side + 1, :]
            top = (held_first * jnp.exp(jnp.minimum(column[UP] - row[:, UP], 0.0))).astype(BF)
            cross = (held_cross * jnp.exp(column[DOWN] - row[:, UP])).astype(BF)
            last = (
                held_last * jnp.exp(jnp.minimum(column[DOWN] - row[:, DOWN], 0.0))
            ).astype(BF)
            kept = jnp.where(left if side == 0 else ~left, pair, jnp.zeros_like(pair))
            up = dot(top, kept[UP])
            down = dot(jnp.concatenate([cross, last], axis=1), kept)
            first, second = (up, down) if first is None else (first + up, second + down)
        mixed_ref[:, lanes] = (
            jnp.concatenate([first, second], axis=0)
            + across[:, lanes] * jnp.exp(own)
            + skip_ref[0:1, lanes] * signal[:, lanes]
        )
        ended.append(pair.astype(F32) * jnp.exp(end - own))
        ends.append(jnp.exp(end))
    fresh = sum(
        dot(b_rows, part, 0, 0) for part in halves(jnp.concatenate(ended, axis=1))
    )
    carried[...] = jnp.concatenate(ends, axis=1) * state + fresh


def place_rows(ids, masks, refs, stores):
    at = 0
    for ref in refs:
        stacked = len(ref.shape) == 3
        for inner in range(ref.shape[0] if stacked else 1):
            rows = ref.shape[-2]
            if masks[at] is None:
                target = slice(None)
            else:
                target = pl.ds(pl.multiple_of((ids[0] ^ masks[at]) * rows, 8), rows)
            for columns, into, lanes in stores:
                into[target, lanes] = ref[inner, :, columns] if stacked else ref[:, columns]
            at += 1


def pick_piece(ids, block, own_chunks, refs, scratch):
    mask = (block // own_chunks) ^ ids[1]
    for at, ref in enumerate(refs):

        @pl.when(mask == at)
        def _():
            scratch[...] = ref[...]


def store_part(ids, block, own_chunks, refs, value):
    odd = ((block // own_chunks) ^ ids[1]) & 1
    for at, ref in enumerate(refs):

        @pl.when(odd == at)
        def _():
            ref[0] = value


def rows_live(ids, at, lengths):
    sequence = at // (LMAX // SPAN)
    position = (at % (LMAX // SPAN)) * SPAN + lax.broadcasted_iota(jnp.int32, (SPAN, 1), 0)
    return position < lengths[sequence]


def middle_kernel(owners, pieces, masks, own_chunks, ids, lengths, *refs):
    grad_refs = refs[:owners]
    piece_refs = refs[owners : owners + pieces]
    (
        gate_ref,
        mixed_ref,
        gain_ref,
        merged_grad_ref,
        kept_ref,
        sent_ref,
        sums_ref,
        grad_own,
        weight,
    ) = refs[owners + pieces :]
    at = pl.program_id(0)

    @pl.when(at == 0)
    def _():
        at_mask = 0
        for ref in piece_refs:
            count = ref.shape[0] if len(ref.shape) == 3 else 1
            place_rows(
                ids,
                masks[at_mask : at_mask + count],
                [ref],
                ((slice(ref.shape[-1] - weight.shape[1], ref.shape[-1]), weight, slice(None)),),
            )
            at_mask += count

    pick_piece(ids, at, own_chunks, grad_refs, grad_own)
    upstream = grad_own[...]
    upstream = jnp.where(rows_live(ids, at, lengths), upstream, jnp.zeros_like(upstream))
    merged_grad = dot(upstream, weight[...])
    merged_grad_ref[...] = merged_grad
    gate = gate_ref[...]
    gated = mixed_ref[...] * (gate * sigmoid(gate))
    gained = gated * gain_ref[0:1, :]
    squares = jnp.sum(gated * gated, axis=1, keepdims=True)
    products = jnp.sum(merged_grad * gained, axis=1, keepdims=True)
    branch = dot(gained.astype(BF), weight[...], 1, 1).astype(BF)
    store_part(ids, at, own_chunks, (kept_ref, sent_ref), branch)
    lanes = lane_ids((SPAN, LANES))
    both = jnp.where(lanes == 0, squares, jnp.where(lanes == 1, products, 0.0))
    sums_ref[...] = jnp.transpose(both)[0:2, :]


def backward_kernel(channels, masks, owners, own_chunks, ids, lengths, *refs):
    u_refs = refs[:owners]
    grad_refs = refs[owners : 2 * owners]
    sums_refs = refs[2 * owners : 3 * owners]
    backward_step(
        channels, masks, own_chunks, ids, lengths, u_refs, grad_refs, sums_refs, *refs[3 * owners :]
    )


def backward_step(
    channels,
    masks,
    own_chunks,
    ids,
    lengths,
    u_refs,
    grad_refs,
    sums_ref,
    normed_ref,
    gate_ref,
    mixed_ref,
    merged_grad_ref,
    raw_ref,
    pre_ref,
    act_ref,
    step_ref,
    state_ref,
    state_next_ref,
    weight_ref,
    taps_ref,
    heads_ref,
    skip_ref,
    gain_ref,
    part_kept_ref,
    part_sent_ref,
    first_kept_ref,
    first_sent_ref,
    *refs,
):
    low = low_count(len(masks))
    second_refs = refs[: len(masks) // low]
    backward_body(
        channels,
        masks,
        own_chunks,
        ids,
        lengths,
        u_refs,
        grad_refs,
        (sums_ref, normed_ref, gate_ref, mixed_ref, merged_grad_ref, raw_ref, pre_ref, act_ref),
        (step_ref, state_ref, state_next_ref, weight_ref, taps_ref, heads_ref, skip_ref, gain_ref),
        (part_kept_ref, part_sent_ref),
        (first_kept_ref, first_sent_ref, second_refs),
        *refs[len(masks) // low :],
    )


def backward_body(
    channels,
    masks,
    own_chunks,
    ids,
    lengths,
    u_refs,
    grad_refs,
    token_refs,
    other_refs,
    part_refs,
    slot_refs,
    carried,
    ahead,
    weight_sum,
    out_sum,
    tap_sum,
    head_sum,
    gain_sum,
    u_own,
    grad_own,
    out_rows,
):
    sums_ref, normed_ref, gate_ref, mixed_ref, merged_grad_ref, raw_ref, pre_ref, act_ref = token_refs
    step_ref, state_ref, state_next_ref, weight_ref, taps_ref, heads_ref, skip_ref, gain_ref = other_refs
    first_kept_ref, first_sent_ref, second_refs = slot_refs
    width = channels
    heads = width // HEAD
    mixed_width = width + MAPS
    step_at = pl.program_id(0)
    at = pl.num_programs(0) - 1 - step_at

    @pl.when(step_at == 0)
    def _():
        weight_sum[...] = jnp.zeros_like(weight_sum)
        out_sum[...] = jnp.zeros_like(out_sum)
        tap_sum[...] = jnp.zeros_like(tap_sum)
        head_sum[...] = jnp.zeros_like(head_sum)
        gain_sum[...] = jnp.zeros_like(gain_sum)

    @pl.when(step_at % (LMAX // SPAN) == 0)
    def _():
        carried[...] = jnp.zeros_like(carried)
        ahead[SPAN:, :] = jnp.zeros((8, mixed_width), F32)

    pick_piece(ids, at, own_chunks, u_refs, u_own)
    pick_piece(ids, at, own_chunks, grad_refs, grad_own)
    sums = sum(ref[...] for ref in sums_ref)
    scale_row = lax.rsqrt(sums[0:1, :] / INNER + EPSILON)
    cross_row = scale_row * scale_row * scale_row * (sums[1:2, :] / INNER)
    row_ids = lax.broadcasted_iota(jnp.int32, (LANES, SPAN), 0)
    columns = jnp.transpose(jnp.where(row_ids == 0, scale_row, cross_row))
    gate_scale = columns[:, 0:1]
    cross = columns[:, 1:2]

    gate = gate_ref[...]
    gate_s = sigmoid(gate)
    gate_act = gate * gate_s
    mixed = mixed_ref[...]
    gated = mixed * gate_act
    merged_grad = merged_grad_ref[...]
    gain = skip_ref[1:2, :]
    scaled = gated * gate_scale
    tap_sum[5:6, :width] += jnp.sum(merged_grad * scaled, axis=0, keepdims=True)
    merged = (scaled * gain).astype(BF)
    upstream = grad_own[...]
    upstream = jnp.where(rows_live(ids, at, lengths), upstream, jnp.zeros_like(upstream))
    out_sum[...] += dot(merged, upstream, 0, 0)
    gated_grad = gate_scale * (merged_grad * gain) - gated * cross
    mixed_grad = gated_grad * gate_act
    gate_grad = gated_grad * mixed * (gate_s * (1.0 + gate * (1.0 - gate_s)))

    act = act_ref[...]
    signal = act[:, :width].astype(F32)
    b_rows = act[:, width : width + STATE]
    c_rows = act[:, width + STATE :]
    skip = skip_ref[0:1, :]
    tap_sum[6:7, :width] += jnp.sum(mixed_grad * signal, axis=0, keepdims=True)
    grad_high, grad_rest = halves(mixed_grad)
    grad_rows = grad_high.astype(F32) + grad_rest.astype(F32)

    step_in = step_ref[:, :LANES]
    step = step_ref[:, LANES : 2 * LANES]
    cumulative = step_ref[:, 2 * LANES :]
    rate = jnp.exp(heads_ref[0:1, :])
    decay = -rate * step
    across_rows = jnp.transpose(cumulative)
    closing = cumulative[SPAN - 1 : SPAN, :]
    mask = lower_mask(HALF)
    upper = lax.broadcasted_iota(jnp.int32, (HALF, HALF), 0) <= lax.broadcasted_iota(
        jnp.int32, (HALF, HALF), 1
    )
    held_first = jnp.where(upper, dot(b_rows[UP], c_rows[UP], 1, 1), 0.0)
    held_cross = dot(b_rows[UP], c_rows[DOWN], 1, 1)
    held_last = jnp.where(upper, dot(b_rows[DOWN], c_rows[DOWN], 1, 1), 0.0)
    left = lane_ids((SPAN, LANES)) < HEAD
    left_row = left[0:1]
    state_grad = carried[...]
    state_parts = halves(state_grad)
    state_before = halves(state_ref[0])
    from_state = dot(
        jnp.concatenate([b_rows, b_rows], axis=1), jnp.concatenate(state_parts, axis=0)
    )
    grads_first = grads_last = grads_cross = None
    grown, ended, ends, weighted_grads, shaped_grads, signal_grads = [], [], [], [], [], []
    for head in range(0, heads, 2):
        lanes = slice(head * HEAD, head * HEAD + LANES)
        wide = [
            jnp.broadcast_to(cumulative[:, head + side : head + side + 1], (SPAN, LANES))
            for side in range(2)
        ]
        own = jnp.where(left, wide[0], wide[1])
        end = paired(left_row, closing, head)
        end_wide = jnp.exp(end - own)
        ends.append(jnp.exp(end))
        step_wide = paired(left, step, head)
        signal_own = signal[:, lanes]
        pair = (step_wide * signal_own).astype(BF)
        pair_rows = pair.astype(F32)
        pair_twice = jnp.concatenate([pair, pair], axis=1)
        grad_own_rows = grad_rows[:, lanes]
        grown.append(grad_own_rows * jnp.exp(own))
        ended.append(pair_rows * end_wide)
        total_up = None
        for side in range(2):
            column = wide[side]
            row = across_rows[head + side : head + side + 1, :]
            damp_first = jnp.exp(jnp.minimum(row[:, UP] - column[UP], 0.0))
            damp_cross = jnp.exp(row[:, DOWN] - column[UP])
            damp_last = jnp.exp(jnp.minimum(row[:, DOWN] - column[DOWN], 0.0))
            side_lanes = left if side == 0 else ~left
            kept = jnp.concatenate(
                [
                    jnp.where(side_lanes, part[:, lanes], jnp.zeros_like(pair))
                    for part in (grad_high, grad_rest)
                ],
                axis=1,
            )
            terms_up = dot(pair_twice[UP], kept, 1, 1)
            terms_first = terms_up[:, UP] * damp_first
            terms_cross = terms_up[:, DOWN] * damp_cross
            terms_last = dot(pair_twice[DOWN], kept[DOWN], 1, 1) * damp_last
            if grads_first is None:
                grads_first, grads_cross, grads_last = terms_first, terms_cross, terms_last
            else:
                grads_first = grads_first + terms_first
                grads_cross = grads_cross + terms_cross
                grads_last = grads_last + terms_last
            mixing_up = jnp.concatenate(
                [(held_first * damp_first).astype(BF), (held_cross * damp_cross).astype(BF)],
                axis=1,
            )
            up = dot(mixing_up, kept)
            down = dot((held_last * damp_last).astype(BF), kept[DOWN])
            total_up, total_down = (
                (up, down) if total_up is None else (total_up + up, total_down + down)
            )
        total = jnp.concatenate([total_up, total_down], axis=0)
        own_grad = total[:, :LANES] + total[:, LANES:] + end_wide * from_state[:, lanes]
        shaped = mixed[:, lanes] - skip[:, lanes] * signal_own
        weighted_grads.append(signal_own * own_grad)
        shaped_grads.append(grad_own_rows * shaped - pair_rows * own_grad)
        signal_grads.append(step_wide * own_grad + skip[:, lanes] * mixed_grad[:, lanes])
    held_low = jnp.concatenate(
        [
            jnp.concatenate(
                [jnp.where(upper, grads_first, 0.0).astype(BF), grads_cross.astype(BF)], axis=1
            ),
            jnp.concatenate(
                [jnp.zeros((HALF, HALF), BF), jnp.where(upper, grads_last, 0.0).astype(BF)], axis=1
            ),
        ],
        axis=0,
    )
    grown = halves(jnp.concatenate(grown, axis=1))
    ended = halves(jnp.concatenate(ended, axis=1))
    c_grad = (
        dot(held_low, b_rows, 0, 0)
        + dot(grown[0], state_before[0], 1, 1)
        + dot(grown[0], state_before[1], 1, 1)
        + dot(grown[1], state_before[0], 1, 1)
    )
    b_grad = (
        dot(held_low, c_rows)
        + dot(ended[0], state_parts[0], 1, 1)
        + dot(ended[0], state_parts[1], 1, 1)
        + dot(ended[1], state_parts[0], 1, 1)
    )
    fresh = sum(dot(c_rows, part, 0, 0) for part in grown)
    carried[...] = jnp.concatenate(ends, axis=1) * state_grad + fresh
    picker = (
        lax.broadcasted_iota(jnp.int32, (width, LANES), 0) // HEAD
        == lax.broadcasted_iota(jnp.int32, (width, LANES), 1)
    ).astype(F32).astype(BF)
    overlap = jnp.sum(state_grad * state_next_ref[0], axis=0, keepdims=True)
    closing_grad = sum(
        dot(part, picker) for part in thirds(jnp.broadcast_to(overlap, (8, width)))
    )[0:1]
    cumulative_grad = sum(
        dot(part, picker) for part in halves(jnp.concatenate(shaped_grads, axis=1))
    )
    lower = lower_mask(SPAN).astype(F32).astype(BF)
    decay_grad = sum(dot(lower, part, 0, 0) for part in halves(cumulative_grad)) + closing_grad
    step_grad = (
        sum(dot(part, picker) for part in halves(jnp.concatenate(weighted_grads, axis=1)))
        - rate * decay_grad
    )
    step_in_grad = step_grad * sigmoid(step_in)
    head_sum[0:1, :] += jnp.sum(decay * decay_grad, axis=0, keepdims=True)
    head_sum[1:2, :] += jnp.sum(step_in_grad, axis=0, keepdims=True)
    pre = pre_ref[...]
    pre_s = sigmoid(pre)
    slope = pre_s * (1.0 + pre * (1.0 - pre_s))
    ahead[:SPAN, :] = jnp.concatenate(signal_grads + [b_grad, c_grad], axis=1) * slope
    raw = raw_ref[...]
    raw_grad = None
    for shift in range(CONV):
        moved = ahead[shift : shift + SPAN, :]
        tap = CONV - 1 - shift
        term = taps_ref[tap : tap + 1, :] * moved
        raw_grad = term if raw_grad is None else raw_grad + term
        tap_sum[tap : tap + 1, :] += jnp.sum(raw * moved, axis=0, keepdims=True)
        if shift == 0:
            tap_sum[CONV : CONV + 1, :] += jnp.sum(moved, axis=0, keepdims=True)
    ahead[SPAN:, :] = ahead[0:8, :]

    low = jnp.concatenate(
        [gate_grad.astype(BF), raw_grad.astype(BF), step_in_grad.astype(BF)], axis=1
    )
    normed = normed_ref[...]
    weight_sum[...] += dot(normed, low, 0, 0)
    part = dot(low, weight_ref[...], 1, 1)
    store_part(ids, at, own_chunks, part_refs, part.astype(BF))
    inputs = u_own[...].astype(F32)
    scale = lax.rsqrt(jnp.mean(inputs * inputs, axis=-1, keepdims=True) + EPSILON)
    gain_sum[0:1, :] += jnp.sum(part * (inputs * scale), axis=0, keepdims=True)

    @pl.when(step_at == pl.num_programs(0) - 1)
    def _():
        rows = weight_sum.shape[0] // len(masks)
        model = weight_sum.shape[0]
        first = first_kept_ref.shape[2]
        kept_count = first_kept_ref.shape[0]
        out_rows[...] = jnp.transpose(out_sum[...])
        step_lanes = weight_sum.shape[1] - first
        for place, mask in enumerate(masks):
            first_ref = first_kept_ref if place < kept_count else first_sent_ref
            position = place if place < kept_count else place - kept_count
            block = ids[0] ^ mask
            small = jnp.concatenate(
                [
                    tap_sum[:, :width],
                    head_sum[...],
                    pltpu.roll(
                        tap_sum[:, width:], (MAPS - block * (MAPS // len(masks))) % MAPS, 1
                    )[:, :LANES],
                    pltpu.roll(gain_sum[...], (model - block * rows) % model, 1)[:, :LANES],
                ],
                axis=1,
            )
            both = jnp.concatenate(halves(small), axis=0)
            picked = pl.ds(pl.multiple_of(block * rows, 8), rows)
            first_ref[position, 0:SMALL, : both.shape[1]] = both
            first_ref[position, 0:SMALL, both.shape[1] :] = jnp.zeros(
                (SMALL, first - both.shape[1]), BF
            )
            first_ref[position, SMALL:, :] = weight_sum[picked, :first].astype(BF)
            second_ref = second_refs[place % kept_count]
            near = place // kept_count
            second_ref[near, :, :step_lanes] = weight_sum[picked, first:].astype(BF)
            second_ref[near, :, step_lanes:] = out_rows[picked, :].astype(BF)


def pad_to(values, axis, size):
    if values.shape[axis] == size:
        return values
    pads = [(0, 0)] * values.ndim
    pads[axis] = (0, size - values.shape[axis])
    return jnp.pad(values, pads)


def whole_spec(shape):
    return pl.BlockSpec(shape, lambda *_: (0,) * len(shape))


def lamb_parts(weight, gradient, first_old, second_old):
    first_new = DECAY * first_old + (1.0 - DECAY) * gradient
    second_new = DECAY * second_old + (1.0 - DECAY) * gradient * gradient
    direction = (
        first_new / BIAS_FIRST / (jnp.sqrt(second_new / BIAS_SECOND) + ADAM_EPSILON)
        + WEIGHT_DECAY * weight
    )
    return (first_new, second_new, direction)


def total_of(values):
    while len(values.shape) > 2:
        values = jnp.sum(values, axis=0)
    return jnp.sum(jnp.sum(values, axis=1, keepdims=True), axis=0, keepdims=True)


def lamb_one(position, copies, gradient, olds, outs, norms):
    weight = olds[0][...]
    first_new, second_new, direction = lamb_parts(weight, gradient, olds[1][...], olds[2][...])
    outs[0][...] = gradient
    outs[1][...] = first_new
    outs[2][...] = second_new
    outs[3][...] = direction
    lanes = lane_ids((1, LANES))
    share = 1.0 / copies
    return (
        norms
        + jnp.where(lanes == position, total_of(weight * weight) * share, 0.0)
        + jnp.where(lanes == 8 + position, total_of(direction * direction) * share, 0.0)
    )


def pack_kernel(width, tensor_count, ids, kept_ref, *refs):
    received = refs[:-1]
    packed_ref = refs[-1]
    maps_rows = packed_ref.shape[1] - 8
    lanes = slice(2 * width, 2 * width + MAPS)
    state = kept_ref[SMALL:, lanes]
    small = kept_ref[0:SMALL, width + LANES : width + LANES + MAPS]
    for ref in received:
        state = state + ref[SMALL:, lanes].astype(F32)
        small = small + ref[0:SMALL, width + LANES : width + LANES + MAPS].astype(F32)
    small = small[:8] + small[8:]
    for at in range(tensor_count):
        packed_ref[at, 0:8, :] = small
        packed_ref[at, 8:, :] = state[at * maps_rows : (at + 1) * maps_rows, :]


def lamb_wide_kernel(width, channels, heads, copies, firsts, seconds, ids, *refs):
    whole = sum(ref[...].astype(F32) for ref in refs[:firsts])
    rest = sum(ref[...].astype(F32) for ref in refs[firsts : firsts + seconds])
    count = firsts + seconds
    olds = refs[count : count + 15]
    outs = refs[count + 15 : count + 35]
    norms_ref = refs[count + 35]
    block = whole[SMALL:]
    small = whole[:8] + whole[8:SMALL]
    norms = jnp.zeros((1, LANES), F32)
    in_grad = jnp.stack([block[:, :channels], block[:, width : width + channels]], axis=1)
    step_grad = jnp.transpose(rest[:, :LANES])[:heads]
    out_grad = rest[:, LANES : LANES + channels]
    channel_grad = small[: CONV + 2, :channels]
    picker = (
        lax.broadcasted_iota(jnp.int32, (width, LANES), 0) // HEAD
        == lax.broadcasted_iota(jnp.int32, (width, LANES), 1)
    ).astype(F32)
    skips = dot(small[:, :width], picker, precision=HIGHEST)
    head_grad = jnp.concatenate(
        [small[0:2, width : width + LANES], skips[6:7, :]], axis=0
    )[:, :heads]
    gradients = (in_grad, step_grad, out_grad, channel_grad, head_grad)
    for position, gradient in enumerate(gradients):
        norms = lamb_one(
            position,
            copies if position > 2 else 1.0,
            gradient,
            olds[position::5],
            outs[position::5],
            norms,
        )
    norms_ref[...] = norms


def lamb_maps_kernel(ids, packed_ref, *refs):
    olds = refs[:9]
    norms_in_ref = refs[9]
    outs = refs[10:22]
    norms_ref = refs[22]
    whole = jnp.sum(packed_ref[...], axis=0)
    small = whole[:8]
    conv_rows = olds[1].shape[0]
    gain_size = olds[2].shape[1]
    picker = (
        lax.broadcasted_iota(jnp.int32, (conv_rows, LANES), 0) + ids[1] * conv_rows
        == lax.broadcasted_iota(jnp.int32, (conv_rows, LANES), 1)
    ).astype(F32)
    conv_grad = dot(picker, small[:, :LANES], 1, 1, precision=HIGHEST)[:, : CONV + 1]
    gain_grad = pltpu.roll(small[:, LANES:], (LANES - ids[1] * gain_size) % LANES, 1)[
        0:1, :gain_size
    ]
    norms = norms_in_ref[...]
    for position, gradient in enumerate((whole[8:], conv_grad, gain_grad)):
        norms = lamb_one(
            5 + position, 1.0, gradient, olds[position::3], outs[position::3], norms
        )
    norms_ref[...] = jnp.broadcast_to(norms[None], norms_ref.shape)


def update_kernel(ids, norms_ref, *refs):
    norms = jnp.sqrt(jnp.sum(norms_ref[...], axis=0))
    refs[-1][...] = jnp.concatenate([norms[:, :8], norms[:, 8:16]], axis=0)
    for position in range(8):
        ratio = -RATE * norms[:, position : position + 1] / norms[:, 8 + position : 9 + position]
        direction = refs[position][...]
        if direction.ndim == 3:
            ratio = ratio[None]
        refs[8 + position][...] = ratio * direction


def split_three(values):
    high = lax.reduce_precision(values, 8, 7)
    rest = values - high
    middle = lax.reduce_precision(rest, 8, 7)
    return [high.astype(BF), middle.astype(BF), (rest - middle).astype(BF)]


def local(*arguments):
    block_input, output_grad, lengths = arguments[:3]
    masters = arguments[3:11]
    firsts = arguments[11:19]
    seconds = arguments[19:27]
    (
        in_proj,
        step_proj,
        out_proj,
        channel_params,
        head_params,
        state_proj,
        state_conv,
        norm_gain,
    ) = masters
    dp_count = lax.axis_size("dp")
    tensor_count = lax.axis_size("tensor")
    dp_at = lax.axis_index("dp")
    tensor_at = lax.axis_index("tensor")
    everywhere = dp_count * tensor_count
    own_count, model = block_input.shape
    tokens = own_count * tensor_count
    chunks = tokens // SPAN
    own_chunks = own_count // SPAN
    rows = in_proj.shape[0]
    channels = in_proj.shape[2]
    heads = head_params.shape[1]
    width = -(-channels // LANES) * LANES
    mixed_width = width + MAPS
    columns = 2 * width + MAPS + LANES
    dp_low = low_count(dp_count)
    ids = jnp.stack([dp_at, tensor_at]).astype(jnp.int32)

    in_low = jnp.concatenate(
        [
            pad_to(in_proj[:, 0, :].astype(BF), 1, width),
            pad_to(in_proj[:, 1, :].astype(BF), 1, width),
            pad_to(step_proj.astype(BF), 1, LANES),
        ],
        axis=1,
    )
    out_low = pad_to(out_proj.astype(BF), 1, width)
    both_low = jnp.concatenate([in_low, out_low], axis=1)
    split = in_low.shape[1]
    highs = list(range(dp_low, dp_count, dp_low))
    nears = list(range(1, dp_low))
    tensor_highs = list(range(2, tensor_count, 2))
    landed = together(
        *[exchange(block_input, "tensor", mask) for mask in tensor_highs],
        *[exchange(both_low, "dp", mask) for mask in highs],
        *[exchange(both_low, "dp", mask) for mask in nears],
    )
    u_far = dict(zip(tensor_highs, landed))
    both_far = list(landed[len(tensor_highs) : len(tensor_highs) + len(highs)])
    both_near = list(landed[len(tensor_highs) + len(highs) :])
    maps_rows = state_proj.shape[0]
    conv_rows = state_conv.shape[0]
    small_own = jnp.concatenate(
        split_three(state_conv.reshape(-1)) + split_three(norm_gain), axis=0
    )
    shared_own = jnp.concatenate(
        [state_proj.astype(BF), pad_to(small_own, 0, MAPS)[None, :]], axis=0
    )
    shared_own, *both_far = together(shared_own, *both_far)
    in_stack = jnp.stack([piece[:, :split] for piece in both_far])
    out_stack = jnp.stack([piece[:, split:] for piece in both_far])
    shared = lax.all_to_all(
        jnp.broadcast_to(shared_own[None], (everywhere,) + shared_own.shape),
        ("dp", "tensor"),
        0,
        0,
    )
    u_pieces = gather_near(block_input, u_far, "tensor", 2)
    shared, *landed = together(
        shared, *u_pieces[1:], *[exchange(in_stack, "dp", near) for near in nears]
    )
    u_pieces = [block_input] + landed[: tensor_count - 1]
    in_near = landed[tensor_count - 1 :]
    grad_own, out_stack, *_ = together(output_grad, out_stack, u_far[2])
    grad_far = gather_far(grad_own, "tensor", 2)
    out_near = [exchange(out_stack, "dp", near) for near in nears]
    in_pieces = [both_low] + both_near + both_far + in_near
    piece_masks = [0] + nears + highs + [high + near for near in nears for high in highs]
    direct = rows % 16 == 0
    if not direct:
        order = dp_at ^ jnp.arange(dp_count)
        order = jnp.array([piece_masks.index(mask) for mask in range(dp_count)])[order]

        def ordered(pieces):
            parts = [piece if piece.ndim == 3 else piece[None] for piece in pieces]
            return jnp.concatenate(parts, axis=0)[order].reshape(model, -1)

        in_pieces = [
            ordered([piece[:, :split] for piece in [both_low] + both_near + both_far] + in_near)
        ]
    state_weight = shared[:, :maps_rows].reshape(-1, MAPS)
    small_all = shared[:, maps_rows].astype(F32)
    conv_size = conv_rows * (CONV + 1)
    conv_whole = sum(
        small_all[:, part * conv_size : (part + 1) * conv_size] for part in range(3)
    ).reshape(-1, CONV + 1)
    gain_base = 3 * conv_size
    gain_size = norm_gain.shape[0]
    gain_whole = sum(
        small_all[:, gain_base + part * gain_size : gain_base + (part + 1) * gain_size]
        for part in range(3)
    ).reshape(-1)
    channel_wide = pad_to(channel_params, 1, width)
    taps = pad_to(
        jnp.concatenate([channel_wide[: CONV + 1], conv_whole.T], axis=1), 0, 8
    )
    heads_wide = pad_to(pad_to(head_params, 1, LANES), 0, 8)
    skip_wide = jnp.repeat(pad_to(head_params[2], 0, width // HEAD), HEAD)
    skip_gain = pad_to(jnp.stack([skip_wide, channel_wide[CONV + 1]]), 0, 8)
    gain_rows = pad_to(gain_whole[None, :], 0, 8)

    def token_spec(size, reverse=False):
        if reverse:
            return pl.BlockSpec((SPAN, size), lambda at, *_: (chunks - 1 - at, 0))
        return pl.BlockSpec((SPAN, size), lambda at, *_: (at, 0))

    def piece_specs(reverse=False):
        def spec(mask):
            def index(at, ids_ref, *_):
                block = chunks - 1 - at if reverse else at
                mine = (block // own_chunks) ^ ids_ref[1] == mask
                return (jnp.where(mine, block % own_chunks, 0), 0)

            return pl.BlockSpec((SPAN, model), index)

        return [spec(mask) for mask in range(tensor_count)]

    def part_specs(reverse=False):
        def spec(odd):
            def index(at, ids_ref, *_):
                block = chunks - 1 - at if reverse else at
                owner = block // own_chunks
                inner = block % own_chunks
                mine = ((owner ^ ids_ref[1]) & 1) == odd
                if reverse:
                    other = jnp.where(owner > 0, owner - 1, 1)
                    other_inner = jnp.where(owner > 0, own_chunks - 1, 0)
                else:
                    last = tensor_count - 1
                    other = jnp.where(owner < last, owner + 1, last - 1)
                    other_inner = jnp.where(owner < last, 0, own_chunks - 1)
                owner = jnp.where(mine, owner, other)
                return ((owner ^ ids_ref[1]) >> 1, jnp.where(mine, inner, other_inner), 0)

            return pl.BlockSpec((1, SPAN, model), index)

        return [spec(0), spec(1)]

    def struct(shape, dtype=F32):
        return jax.ShapeDtypeStruct(shape, dtype)

    arbitrary = pltpu.CompilerParams(
        dimension_semantics=("arbitrary",), vmem_limit_bytes=VMEM
    )
    if not direct:
        piece_masks = [None]
    normed, gate_raw, raw, pre, act, step_in, states, mixed, weight = pl.pallas_call(
        functools.partial(forward_kernel, width, len(in_pieces), piece_masks, tensor_count, own_chunks),
        grid_spec=pltpu.PrefetchScalarGridSpec(
            num_scalar_prefetch=1,
            grid=(chunks,),
            in_specs=piece_specs()
            + [whole_spec(piece.shape) for piece in in_pieces]
            + [
                whole_spec(state_weight.shape),
                whole_spec(gain_rows.shape),
                whole_spec(taps.shape),
                whole_spec(heads_wide.shape),
                whole_spec(skip_gain.shape),
            ],
            out_specs=[
                token_spec(model),
                token_spec(width),
                token_spec(mixed_width),
                token_spec(mixed_width),
                token_spec(mixed_width),
                token_spec(3 * LANES),
                pl.BlockSpec((1, STATE, width), lambda at, *_: (at, 0, 0)),
                token_spec(width),
                whole_spec((model, columns)),
            ],
            scratch_shapes=[
                pltpu.VMEM((SPAN + 8, mixed_width), F32),
                pltpu.VMEM((STATE, width), F32),
                pltpu.VMEM((SPAN, model), BF),
            ],
        ),
        out_shape=[
            struct((tokens, model), BF),
            struct((tokens, width)),
            struct((tokens, mixed_width)),
            struct((tokens, mixed_width)),
            struct((tokens, mixed_width), BF),
            struct((tokens, 3 * LANES)),
            struct((chunks, STATE, width)),
            struct((tokens, width)),
            struct((model, columns), BF),
        ],
        compiler_params=arbitrary,
        name="ssd_forward",
    )(ids, *u_pieces, *in_pieces, state_weight, gain_rows, taps, heads_wide, skip_gain)

    gate_raw, *landed = together(gate_raw, *grad_far.values(), *out_near)
    grad_far = dict(zip(grad_far, landed))
    out_near = landed[len(grad_far) :]
    grad_pieces = gather_near(grad_own, grad_far, "tensor", 2)
    out_pieces = [both_low] + both_near + both_far + out_near
    if not direct:
        out_pieces = [
            ordered([piece[:, split:] for piece in [both_low] + both_near + both_far] + out_near)
        ]
    gate_gain_rows = pad_to(channel_wide[CONV + 1][None, :], 0, 8)
    merged_grad, *branch_parts, sums_part = pl.pallas_call(
        functools.partial(middle_kernel, tensor_count, len(out_pieces), piece_masks, own_chunks),
        grid_spec=pltpu.PrefetchScalarGridSpec(
            num_scalar_prefetch=2,
            grid=(chunks,),
            in_specs=[
                *piece_specs(),
                *[whole_spec(piece.shape) for piece in out_pieces],
                token_spec(width),
                token_spec(width),
                whole_spec(gate_gain_rows.shape),
            ],
            out_specs=[
                token_spec(width),
                *part_specs(),
                pl.BlockSpec((2, SPAN), lambda at, *_: (0, at)),
            ],
            scratch_shapes=[pltpu.VMEM((SPAN, model), BF), pltpu.VMEM((model, width), BF)],
        ),
        out_shape=[
            struct((tokens, width)),
            *[struct((tensor_count // 2, own_count, model), BF)] * 2,
            struct((2, tokens)),
        ],
        compiler_params=arbitrary,
        name="gate_middle",
    )(ids, lengths, *grad_pieces, *out_pieces, gate_raw, mixed, gate_gain_rows)

    branch_total = near_sum(*branch_parts, "tensor", 2)
    branch_total, *sums = together(
        branch_total, *[exchange(sums_part, "tensor", mask) for mask in range(1, tensor_count)]
    )
    sums = [sums_part] + sums
    branch_far = far_parts(branch_total, "tensor", 2)
    masks = slot_masks(dp_count, dp_low)
    first_columns = 2 * width + MAPS
    second_columns = LANES + width
    kept_slots = dp_count // dp_low
    token_back = functools.partial(token_spec, reverse=True)
    normed_kept, normed_sent, first_kept, first_sent, *seconds_out = pl.pallas_call(
        functools.partial(backward_kernel, width, masks, tensor_count, own_chunks),
        grid_spec=pltpu.PrefetchScalarGridSpec(
            num_scalar_prefetch=2,
            grid=(chunks,),
            in_specs=[
                *piece_specs(True),
                *piece_specs(True),
                *[pl.BlockSpec((2, SPAN), lambda at, *_: (0, chunks - 1 - at))] * tensor_count,
                token_back(model),
                token_back(width),
                token_back(width),
                token_back(width),
                token_back(mixed_width),
                token_back(mixed_width),
                token_back(mixed_width),
                token_back(3 * LANES),
                pl.BlockSpec((1, STATE, width), lambda at, *_: (chunks - 1 - at, 0, 0)),
                pl.BlockSpec(
                    (1, STATE, width), lambda at, *_: (jnp.minimum(chunks - at, chunks - 1), 0, 0)
                ),
                whole_spec((model, columns)),
                whole_spec(taps.shape),
                whole_spec(heads_wide.shape),
                whole_spec(skip_gain.shape),
                whole_spec(gain_rows.shape),
            ],
            out_specs=[
                *part_specs(True),
                whole_spec((kept_slots, SMALL + rows, first_columns)),
                whole_spec((dp_count - kept_slots, SMALL + rows, first_columns)),
                *[whole_spec((dp_low, rows, second_columns))] * kept_slots,
            ],
            scratch_shapes=[
                pltpu.VMEM((STATE, width), F32),
                pltpu.VMEM((SPAN + 8, mixed_width), F32),
                pltpu.VMEM((model, columns), F32),
                pltpu.VMEM((width, model), F32),
                pltpu.VMEM((8, mixed_width), F32),
                pltpu.VMEM((8, LANES), F32),
                pltpu.VMEM((8, model), F32),
                pltpu.VMEM((SPAN, model), BF),
                pltpu.VMEM((SPAN, model), BF),
                pltpu.VMEM((model, width), F32),
            ],
        ),
        out_shape=[
            *[struct((tensor_count // 2, own_count, model), BF)] * 2,
            struct((kept_slots, SMALL + rows, first_columns), BF),
            struct((dp_count - kept_slots, SMALL + rows, first_columns), BF),
            *[struct((dp_low, rows, second_columns), BF)] * kept_slots,
        ],
        compiler_params=arbitrary,
        name="ssd_backward",
    )(
        ids,
        lengths,
        *u_pieces,
        *grad_pieces,
        *sums,
        normed,
        gate_raw,
        mixed,
        merged_grad,
        raw,
        pre,
        act,
        step_in,
        states,
        states,
        weight,
        taps,
        heads_wide,
        skip_gain,
        gain_rows,
    )

    first_kept, first_sent, *branch_far = together(first_kept, first_sent, *branch_far)
    highs_count = first_kept.shape[0]
    first_near = [
        exchange(
            first_sent
            if dp_low == 2
            else first_sent[(near - 1) * highs_count : near * highs_count],
            "dp",
            near,
        )
        for near in nears
    ]
    second_far = [
        exchange(seconds_out[position], "dp", position * dp_low)
        for position in range(1, kept_slots)
    ]
    normed_near = exchange(normed_sent, "tensor", 1)
    landed = together(normed_near, *first_near, *second_far)
    normed_total = normed_kept.astype(F32) + landed[0].astype(F32)
    first_total = first_kept.astype(F32)
    for values in landed[1 : 1 + len(first_near)]:
        first_total = first_total + values.astype(F32)
    second_far = landed[1 + len(first_near) :]
    joined = first_total[:, : SMALL // 2] + first_total[:, SMALL // 2 : SMALL]
    high = lax.reduce_precision(joined, 8, 7)
    first_total = jnp.concatenate([high, joined - high, first_total[:, SMALL:]], axis=1)
    first_parts = [first_total[0]] + far_parts(first_total, "dp", dp_low)
    second_total = seconds_out[0].astype(F32)
    for values in second_far:
        second_total = second_total + values.astype(F32)
    second_parts = [second_total[0]] + [
        exchange(second_total[near].astype(BF), "dp", near) for near in range(1, dp_low)
    ]
    landed = together(*first_parts, *second_parts)
    first_parts = landed[: len(first_parts)]
    second_parts = landed[len(first_parts) :]

    inputs = block_input.astype(F32)
    position_all = tensor_at * own_count + jnp.arange(own_count, dtype=jnp.int32)
    length_of = jnp.sum(
        jnp.where(
            (position_all // LMAX)[:, None]
            == jnp.arange(lengths.shape[0], dtype=jnp.int32)[None, :],
            lengths[None, :],
            0,
        ),
        axis=1,
    )
    live_own = (position_all % LMAX < length_of)[:, None]
    own_squares = lax.dynamic_slice(sum(part[0] for part in sums), (tensor_at * own_count,), (own_count,))
    own_scale = lax.rsqrt(own_squares / INNER + EPSILON)[:, None]
    branch = branch_total[0]
    for values in branch_far:
        branch = branch + values.astype(F32)
    output = (inputs + jnp.where(live_own, branch * own_scale, 0.0)).astype(BF)
    normed_grad = normed_total[0]
    for values in far_parts(normed_total, "tensor", 2):
        normed_grad = normed_grad + values.astype(F32)
    scale = lax.rsqrt(jnp.mean(inputs * inputs, axis=-1, keepdims=True) + EPSILON)
    scaled_grad = normed_grad * gain_whole[None, :]
    input_grad = (
        output_grad.astype(F32)
        + scale * scaled_grad
        - inputs * scale**3 * jnp.mean(scaled_grad * inputs, axis=-1, keepdims=True)
    )

    plain = pltpu.CompilerParams(
        dimension_semantics=("arbitrary",), vmem_limit_bytes=VMEM
    )

    def whole_call(kernel, operands, shapes, name):
        return pl.pallas_call(
            kernel,
            grid_spec=pltpu.PrefetchScalarGridSpec(
                num_scalar_prefetch=1,
                grid=(1,),
                in_specs=[whole_spec(value.shape) for value in operands],
                out_specs=[whole_spec(shape.shape) for shape in shapes],
            ),
            out_shape=shapes,
            compiler_params=plain,
            name=name,
        )(ids, *operands)

    (packed,) = whole_call(
        functools.partial(pack_kernel, width, tensor_count),
        first_parts,
        [struct((tensor_count, maps_rows + 8, MAPS))],
        "pack_maps",
    )
    maps_parts = lax.all_to_all(packed, "tensor", 0, 0)
    def wide_of(values):
        return [values[0], values[1].T] + list(values[2:5])

    wide_shapes = [struct(values.shape) for values in wide_of(masters)]
    wide = whole_call(
        functools.partial(
            lamb_wide_kernel,
            width,
            channels,
            heads,
            float(dp_count),
            len(first_parts),
            len(second_parts),
        ),
        [*first_parts, *second_parts, *wide_of(masters), *wide_of(firsts), *wide_of(seconds)],
        wide_shapes * 4 + [struct((1, LANES))],
        "lamb_wide",
    )

    def flat(values):
        return [values[5], values[6], values[7][None, :]]

    maps_shapes = [struct(values.shape) for values in flat(masters)]
    maps = whole_call(
        lamb_maps_kernel,
        [maps_parts, *flat(masters), *flat(firsts), *flat(seconds), wide[20]],
        maps_shapes * 4 + [struct((everywhere, 1, LANES))],
        "lamb_maps",
    )
    spread = lax.all_to_all(maps[12], ("dp", "tensor"), 0, 0)
    spread, input_grad, output = together(spread, input_grad, output)
    updates = whole_call(
        update_kernel,
        [spread, *wide[15:20], *maps[9:12]],
        wide_shapes + maps_shapes + [struct((2, 8))],
        "lamb_update",
    )

    def joined(kind):
        values = list(wide[5 * kind : 5 * kind + 5]) + list(maps[3 * kind : 3 * kind + 3])
        return (values[0], values[1].T) + tuple(values[2:7]) + (values[7][0],)

    return (
        (output, input_grad)
        + joined(0)
        + joined(1)
        + joined(2)
        + (updates[0], updates[1].T)
        + tuple(updates[2:7])
        + (updates[7][0], updates[8])
    )


WEIGHT_SPECS = (
    P("dp", None, "tensor"),
    P("dp", "tensor"),
    P("dp", "tensor"),
    P(None, "tensor"),
    P(None, "tensor"),
    P(("dp", "tensor"), None),
    P(("dp", "tensor"), None),
    P(("dp", "tensor")),
)


def solution(mesh):
    tokens = P(("dp", "tensor"), None)
    return jax.shard_map(
        local,
        mesh=mesh,
        in_specs=(tokens, tokens, P("dp")) + WEIGHT_SPECS * 3,
        out_specs=(tokens, tokens) + WEIGHT_SPECS * 4 + (P(),),
        check_vma=False,
    )
```

```python
import functools

import jax
import jax.numpy as jnp
from jax import lax
from jax.experimental import pallas as pl
from jax.experimental.pallas import tpu as pltpu
from jax.sharding import PartitionSpec as P

STATE = 128
CONV = 4
SPAN = 256
LMAX = 2048
INNER = 1536
HEAD = 64
MAPS = 2 * STATE
LANES = 128
SMALL = 8
VMEM = 60 * 1024 * 1024

EPSILON = 1e-05
ADAM_EPSILON = 1e-06
DECAY = 0.5
BIAS_FIRST = 0.875
BIAS_SECOND = 0.875
RATE = 0.3
WEIGHT_DECAY = 0.01
HIGHEST = lax.Precision.HIGHEST
BF = jnp.bfloat16
F32 = jnp.float32


def dot(left, right, left_dim=1, right_dim=0, precision=None):
    return lax.dot_general(
        left,
        right,
        (((left_dim,), (right_dim,)), ((), ())),
        precision=precision,
        preferred_element_type=F32,
    )


def exchange(values, axis, mask):
    count = lax.axis_size(axis)
    return lax.ppermute(values, axis, [(at, at ^ mask) for at in range(count)])


def low_count(count):
    low = 1
    while low * low * 4 <= count:
        low *= 2
    return low


def together(*values):
    return list(lax.optimization_barrier(values))


def gather_far(own, axis, low):
    return {high: exchange(own, axis, high) for high in range(low, lax.axis_size(axis), low)}


def gather_near(own, far, axis, low):
    count = lax.axis_size(axis)
    pieces = dict(far)
    pieces[0] = own
    for high in range(0, count, low):
        for near in range(1, low):
            pieces[high + near] = exchange(pieces[high], axis, near)
    return [pieces[mask] for mask in range(count)]


def slot_masks(count, low):
    return [high + near for near in range(low) for high in range(0, count, low)]


def near_sum(kept, sent, axis, low):
    highs = kept.shape[0]
    total = kept.astype(F32)
    for near in range(1, low):
        part = sent if low == 2 else sent[(near - 1) * highs : near * highs]
        total = total + exchange(part, axis, near).astype(F32)
    return total


def far_parts(total, axis, low):
    return [
        exchange(total[position].astype(BF), axis, position * low)
        for position in range(1, total.shape[0])
    ]


def lane_ids(shape):
    return lax.broadcasted_iota(jnp.int32, shape, len(shape) - 1)


def lower_mask(size):
    rows = lax.broadcasted_iota(jnp.int32, (size, size), 0)
    columns = lax.broadcasted_iota(jnp.int32, (size, size), 1)
    return rows >= columns


def paired(left, values, head):
    return jnp.where(left, values[:, head : head + 1], values[:, head + 1 : head + 2])


HALF = SPAN // 2
UP = slice(0, HALF)
DOWN = slice(HALF, SPAN)


def halves(values):
    high = values.astype(BF)
    return high, (values - high.astype(F32)).astype(BF)


def thirds(values):
    high = values.astype(BF)
    rest = values - high.astype(F32)
    middle = rest.astype(BF)
    return high, middle, (rest - middle.astype(F32)).astype(BF)


def sigmoid(values):
    return 0.5 * jnp.tanh(0.5 * values) + 0.5


def forward_kernel(channels, pieces, masks, owners, own_chunks, ids, *refs):
    width = channels
    heads = width // HEAD
    mixed_width = width + MAPS
    u_refs = refs[:owners]
    refs = refs[owners:]
    piece_refs = refs[:pieces]
    (
        state_w_ref,
        gain_ref,
        taps_ref,
        heads_ref,
        skip_ref,
        normed_ref,
        gate_ref,
        raw_ref,
        pre_ref,
        act_ref,
        step_ref,
        state_ref,
        mixed_ref,
        weight_ref,
        gained_ref,
        squares_ref,
        tail,
        carried,
        u_own,
    ) = refs[pieces:]
    at = pl.program_id(0)

    @pl.when(at == 0)
    def _():
        place_rows(
            ids,
            masks,
            piece_refs,
            (
                (slice(0, 2 * width), weight_ref, slice(0, 2 * width)),
                (
                    slice(2 * width, 2 * width + LANES),
                    weight_ref,
                    slice(2 * width + MAPS, 2 * width + MAPS + LANES),
                ),
            ),
        )
        weight_ref[:, 2 * width : 2 * width + MAPS] = state_w_ref[...]

    @pl.when(at % (LMAX // SPAN) == 0)
    def _():
        tail[0:8, :] = jnp.zeros((8, mixed_width), F32)
        carried[...] = jnp.zeros_like(carried)

    pick_piece(ids, at, own_chunks, u_refs, u_own)
    inputs = u_own[...].astype(F32)
    scale = lax.rsqrt(jnp.mean(inputs * inputs, axis=-1, keepdims=True) + EPSILON)
    normed = (inputs * scale * gain_ref[0:1, :]).astype(BF)
    normed_ref[...] = normed
    gate_ref[...] = dot(normed, weight_ref[:, :width])
    raw = dot(normed, weight_ref[:, width : 2 * width + MAPS])
    raw_ref[...] = raw
    tail[8:, :] = raw
    step_in = dot(normed, weight_ref[:, 2 * width + MAPS :]) + heads_ref[1:2, :]
    step_ref[:, :LANES] = step_in
    pre = taps_ref[CONV : CONV + 1, :] + taps_ref[0:1, :] * tail[5 : 5 + SPAN, :]
    for tap in range(1, CONV):
        pre = pre + taps_ref[tap : tap + 1, :] * tail[5 + tap : 5 + tap + SPAN, :]
    tail[0:8, :] = tail[SPAN : SPAN + 8, :]
    pre_ref[...] = pre
    act = (pre * sigmoid(pre)).astype(BF)
    act_ref[...] = act
    signal = act[:, :width].astype(F32)
    b_rows = act[:, width : width + STATE]
    c_rows = act[:, width + STATE :]
    step = jnp.maximum(step_in, 0.0) + jnp.log1p(jnp.exp(-jnp.abs(step_in)))
    decay = -jnp.exp(heads_ref[0:1, :]) * step
    lower = lower_mask(SPAN).astype(F32).astype(BF)
    cumulative = sum(dot(lower, part) for part in thirds(decay))
    step_ref[:, LANES : 2 * LANES] = step
    step_ref[:, 2 * LANES :] = cumulative
    across_rows = jnp.transpose(cumulative)
    closing = cumulative[SPAN - 1 : SPAN, :]
    mask = lower_mask(HALF)
    held_first = jnp.where(mask, dot(c_rows[UP], b_rows[UP], 1, 1), 0.0)
    held_cross = dot(c_rows[DOWN], b_rows[UP], 1, 1)
    held_last = jnp.where(mask, dot(c_rows[DOWN], b_rows[DOWN], 1, 1), 0.0)
    left = lane_ids((SPAN, LANES)) < HEAD
    left_row = left[0:1]
    state = carried[...]
    state_ref[0] = state
    across = dot(
        jnp.concatenate([c_rows, c_rows], axis=1), jnp.concatenate(halves(state), axis=0)
    )
    ended = []
    ends = []
    squares = None
    for head in range(0, heads, 2):
        lanes = slice(head * HEAD, head * HEAD + LANES)
        wide = [
            jnp.broadcast_to(cumulative[:, head + side : head + side + 1], (SPAN, LANES))
            for side in range(2)
        ]
        own = jnp.where(left, wide[0], wide[1])
        end = paired(left_row, closing, head)
        pair = (paired(left, step, head) * signal[:, lanes]).astype(BF)
        first = None
        for side in range(2):
            column = wide[side]
            row = across_rows[head + side : head + side + 1, :]
            top = (held_first * jnp.exp(jnp.minimum(column[UP] - row[:, UP], 0.0))).astype(BF)
            cross = (held_cross * jnp.exp(column[DOWN] - row[:, UP])).astype(BF)
            last = (
                held_last * jnp.exp(jnp.minimum(column[DOWN] - row[:, DOWN], 0.0))
            ).astype(BF)
            kept = jnp.where(left if side == 0 else ~left, pair, jnp.zeros_like(pair))
            up = dot(top, kept[UP])
            down = dot(jnp.concatenate([cross, last], axis=1), kept)
            first, second = (up, down) if first is None else (first + up, second + down)
        mixed_own = (
            jnp.concatenate([first, second], axis=0)
            + across[:, lanes] * jnp.exp(own)
            + skip_ref[0:1, lanes] * signal[:, lanes]
        )
        mixed_ref[:, lanes] = mixed_own
        gate_own = gate_ref[:, lanes]
        gated = mixed_own * (gate_own * sigmoid(gate_own))
        gained_ref[:, lanes] = gated * skip_ref[1:2, lanes]
        squares = gated * gated if squares is None else squares + gated * gated
        ended.append(pair.astype(F32) * jnp.exp(end - own))
        ends.append(jnp.exp(end))
    fresh = sum(
        dot(b_rows, part, 0, 0) for part in halves(jnp.concatenate(ended, axis=1))
    )
    carried[...] = jnp.concatenate(ends, axis=1) * state + fresh
    total = jnp.sum(squares, axis=1, keepdims=True)
    squares_ref[...] = jnp.transpose(jnp.broadcast_to(total, (SPAN, LANES)))[0:8, :]


def place_rows(ids, masks, refs, stores):
    at = 0
    for ref in refs:
        stacked = len(ref.shape) == 3
        for inner in range(ref.shape[0] if stacked else 1):
            rows = ref.shape[-2]
            if masks[at] is None:
                target = slice(None)
            else:
                target = pl.ds(pl.multiple_of((ids[0] ^ masks[at]) * rows, 8), rows)
            for columns, into, lanes in stores:
                into[target, lanes] = ref[inner, :, columns] if stacked else ref[:, columns]
            at += 1


def pick_piece(ids, block, own_chunks, refs, scratch):
    mask = (block // own_chunks) ^ ids[1]
    for at, ref in enumerate(refs):

        @pl.when(mask == at)
        def _():
            scratch[...] = ref[...]


def store_part(ids, block, own_chunks, refs, value):
    odd = ((block // own_chunks) ^ ids[1]) & 1
    for at, ref in enumerate(refs):

        @pl.when(odd == at)
        def _():
            ref[0] = value


def rows_live(ids, at, lengths, span=SPAN):
    sequence = at // (LMAX // span)
    position = (at % (LMAX // span)) * span + lax.broadcasted_iota(jnp.int32, (span, 1), 0)
    return position < lengths[sequence]


def middle_kernel(owners, pieces, masks, own_chunks, ids, lengths, *refs):
    grad_refs = refs[:owners]
    piece_refs = refs[owners : owners + pieces]
    (
        gained_ref,
        squares_ref,
        merged_grad_ref,
        kept_ref,
        sent_ref,
        sums_ref,
        grad_own,
        weight,
    ) = refs[owners + pieces :]
    at = pl.program_id(0)
    span = grad_own.shape[0]

    @pl.when(at == 0)
    def _():
        at_mask = 0
        for ref in piece_refs:
            count = ref.shape[0] if len(ref.shape) == 3 else 1
            place_rows(
                ids,
                masks[at_mask : at_mask + count],
                [ref],
                ((slice(ref.shape[-1] - weight.shape[1], ref.shape[-1]), weight, slice(None)),),
            )
            at_mask += count

    pick_piece(ids, at, own_chunks, grad_refs, grad_own)
    upstream = grad_own[...]
    upstream = jnp.where(rows_live(ids, at, lengths, span), upstream, jnp.zeros_like(upstream))
    merged_grad = dot(upstream, weight[...])
    merged_grad_ref[...] = merged_grad
    gained = gained_ref[...]
    products = jnp.sum(merged_grad * gained, axis=1, keepdims=True)
    branch = dot(gained.astype(BF), weight[...], 1, 1).astype(BF)
    store_part(ids, at, own_chunks, (kept_ref, sent_ref), branch)
    flat = jnp.transpose(jnp.broadcast_to(products, (span, LANES)))
    sums_ref[0:1, :] = squares_ref[0:1, :]
    sums_ref[1:2, :] = flat[0:1, :]


def backward_kernel(channels, masks, owners, own_chunks, ids, lengths, *refs):
    u_refs = refs[:owners]
    grad_refs = refs[owners : 2 * owners]
    sums_refs = refs[2 * owners : 3 * owners]
    backward_step(
        channels, masks, own_chunks, ids, lengths, u_refs, grad_refs, sums_refs, *refs[3 * owners :]
    )


def backward_step(
    channels,
    masks,
    own_chunks,
    ids,
    lengths,
    u_refs,
    grad_refs,
    sums_ref,
    normed_ref,
    gate_ref,
    mixed_ref,
    merged_grad_ref,
    raw_ref,
    pre_ref,
    act_ref,
    step_ref,
    state_ref,
    state_next_ref,
    weight_ref,
    taps_ref,
    heads_ref,
    skip_ref,
    gain_ref,
    part_kept_ref,
    part_sent_ref,
    first_kept_ref,
    first_sent_ref,
    *refs,
):
    low = low_count(len(masks))
    second_refs = refs[: len(masks) // low]
    backward_body(
        channels,
        masks,
        own_chunks,
        ids,
        lengths,
        u_refs,
        grad_refs,
        (sums_ref, normed_ref, gate_ref, mixed_ref, merged_grad_ref, raw_ref, pre_ref, act_ref),
        (step_ref, state_ref, state_next_ref, weight_ref, taps_ref, heads_ref, skip_ref, gain_ref),
        (part_kept_ref, part_sent_ref),
        (first_kept_ref, first_sent_ref, second_refs),
        *refs[len(masks) // low :],
    )


def backward_body(
    channels,
    masks,
    own_chunks,
    ids,
    lengths,
    u_refs,
    grad_refs,
    token_refs,
    other_refs,
    part_refs,
    slot_refs,
    carried,
    ahead,
    weight_sum,
    out_sum,
    tap_sum,
    head_sum,
    gain_sum,
    u_own,
    grad_own,
    out_rows,
):
    sums_ref, normed_ref, gate_ref, mixed_ref, merged_grad_ref, raw_ref, pre_ref, act_ref = token_refs
    step_ref, state_ref, state_next_ref, weight_ref, taps_ref, heads_ref, skip_ref, gain_ref = other_refs
    first_kept_ref, first_sent_ref, second_refs = slot_refs
    width = channels
    heads = width // HEAD
    mixed_width = width + MAPS
    step_at = pl.program_id(0)
    at = pl.num_programs(0) - 1 - step_at

    @pl.when(step_at == 0)
    def _():
        weight_sum[...] = jnp.zeros_like(weight_sum)
        out_sum[...] = jnp.zeros_like(out_sum)
        tap_sum[...] = jnp.zeros_like(tap_sum)
        head_sum[...] = jnp.zeros_like(head_sum)
        gain_sum[...] = jnp.zeros_like(gain_sum)

    @pl.when(step_at % (LMAX // SPAN) == 0)
    def _():
        carried[...] = jnp.zeros_like(carried)
        ahead[SPAN:, :] = jnp.zeros((8, mixed_width), F32)

    pick_piece(ids, at, own_chunks, u_refs, u_own)
    pick_piece(ids, at, own_chunks, grad_refs, grad_own)
    sums = sum(ref[...] for ref in sums_ref)
    scale_row = lax.rsqrt(sums[0:1, :] / INNER + EPSILON)
    cross_row = scale_row * scale_row * scale_row * (sums[1:2, :] / INNER)
    row_ids = lax.broadcasted_iota(jnp.int32, (LANES, SPAN), 0)
    columns = jnp.transpose(jnp.where(row_ids == 0, scale_row, cross_row))
    gate_scale = columns[:, 0:1]
    cross = columns[:, 1:2]

    gate = gate_ref[...]
    gate_s = sigmoid(gate)
    gate_act = gate * gate_s
    mixed = mixed_ref[...]
    gated = mixed * gate_act
    merged_grad = merged_grad_ref[...]
    gain = skip_ref[1:2, :]
    scaled = gated * gate_scale
    tap_sum[5:6, :width] += jnp.sum(merged_grad * scaled, axis=0, keepdims=True)
    merged = (scaled * gain).astype(BF)
    upstream = grad_own[...]
    upstream = jnp.where(rows_live(ids, at, lengths), upstream, jnp.zeros_like(upstream))
    out_sum[...] += dot(merged, upstream, 0, 0)
    gated_grad = gate_scale * (merged_grad * gain) - gated * cross
    mixed_grad = gated_grad * gate_act
    gate_grad = gated_grad * mixed * (gate_s * (1.0 + gate * (1.0 - gate_s)))

    act = act_ref[...]
    signal = act[:, :width].astype(F32)
    b_rows = act[:, width : width + STATE]
    c_rows = act[:, width + STATE :]
    skip = skip_ref[0:1, :]
    tap_sum[6:7, :width] += jnp.sum(mixed_grad * signal, axis=0, keepdims=True)
    grad_high, grad_rest = halves(mixed_grad)
    grad_rows = grad_high.astype(F32) + grad_rest.astype(F32)

    step_in = step_ref[:, :LANES]
    step = step_ref[:, LANES : 2 * LANES]
    cumulative = step_ref[:, 2 * LANES :]
    rate = jnp.exp(heads_ref[0:1, :])
    decay = -rate * step
    across_rows = jnp.transpose(cumulative)
    closing = cumulative[SPAN - 1 : SPAN, :]
    mask = lower_mask(HALF)
    upper = lax.broadcasted_iota(jnp.int32, (HALF, HALF), 0) <= lax.broadcasted_iota(
        jnp.int32, (HALF, HALF), 1
    )
    held_first = jnp.where(upper, dot(b_rows[UP], c_rows[UP], 1, 1), 0.0)
    held_cross = dot(b_rows[UP], c_rows[DOWN], 1, 1)
    held_last = jnp.where(upper, dot(b_rows[DOWN], c_rows[DOWN], 1, 1), 0.0)
    left = lane_ids((SPAN, LANES)) < HEAD
    left_row = left[0:1]
    state_grad = carried[...]
    state_parts = halves(state_grad)
    state_before = halves(state_ref[0])
    from_state = dot(
        jnp.concatenate([b_rows, b_rows], axis=1), jnp.concatenate(state_parts, axis=0)
    )
    grads_first = grads_last = grads_cross = None
    grown, ended, ends, weighted_grads, shaped_grads, signal_grads = [], [], [], [], [], []
    for head in range(0, heads, 2):
        lanes = slice(head * HEAD, head * HEAD + LANES)
        wide = [
            jnp.broadcast_to(cumulative[:, head + side : head + side + 1], (SPAN, LANES))
            for side in range(2)
        ]
        own = jnp.where(left, wide[0], wide[1])
        end = paired(left_row, closing, head)
        end_wide = jnp.exp(end - own)
        ends.append(jnp.exp(end))
        step_wide = paired(left, step, head)
        signal_own = signal[:, lanes]
        pair = (step_wide * signal_own).astype(BF)
        pair_rows = pair.astype(F32)
        pair_twice = jnp.concatenate([pair, pair], axis=1)
        grad_own_rows = grad_rows[:, lanes]
        grown.append(grad_own_rows * jnp.exp(own))
        ended.append(pair_rows * end_wide)
        total_up = None
        for side in range(2):
            column = wide[side]
            row = across_rows[head + side : head + side + 1, :]
            damp_first = jnp.exp(jnp.minimum(row[:, UP] - column[UP], 0.0))
            damp_cross = jnp.exp(row[:, DOWN] - column[UP])
            damp_last = jnp.exp(jnp.minimum(row[:, DOWN] - column[DOWN], 0.0))
            side_lanes = left if side == 0 else ~left
            kept = jnp.concatenate(
                [
                    jnp.where(side_lanes, part[:, lanes], jnp.zeros_like(pair))
                    for part in (grad_high, grad_rest)
                ],
                axis=1,
            )
            terms_up = dot(pair_twice[UP], kept, 1, 1)
            terms_first = terms_up[:, UP] * damp_first
            terms_cross = terms_up[:, DOWN] * damp_cross
            terms_last = dot(pair_twice[DOWN], kept[DOWN], 1, 1) * damp_last
            if grads_first is None:
                grads_first, grads_cross, grads_last = terms_first, terms_cross, terms_last
            else:
                grads_first = grads_first + terms_first
                grads_cross = grads_cross + terms_cross
                grads_last = grads_last + terms_last
            mixing_up = jnp.concatenate(
                [(held_first * damp_first).astype(BF), (held_cross * damp_cross).astype(BF)],
                axis=1,
            )
            up = dot(mixing_up, kept)
            down = dot((held_last * damp_last).astype(BF), kept[DOWN])
            total_up, total_down = (
                (up, down) if total_up is None else (total_up + up, total_down + down)
            )
        total = jnp.concatenate([total_up, total_down], axis=0)
        own_grad = total[:, :LANES] + total[:, LANES:] + end_wide * from_state[:, lanes]
        shaped = mixed[:, lanes] - skip[:, lanes] * signal_own
        weighted_grads.append(signal_own * own_grad)
        shaped_grads.append(grad_own_rows * shaped - pair_rows * own_grad)
        signal_grads.append(step_wide * own_grad + skip[:, lanes] * mixed_grad[:, lanes])
    held_low = jnp.concatenate(
        [
            jnp.concatenate(
                [jnp.where(upper, grads_first, 0.0).astype(BF), grads_cross.astype(BF)], axis=1
            ),
            jnp.concatenate(
                [jnp.zeros((HALF, HALF), BF), jnp.where(upper, grads_last, 0.0).astype(BF)], axis=1
            ),
        ],
        axis=0,
    )
    grown = halves(jnp.concatenate(grown, axis=1))
    ended = halves(jnp.concatenate(ended, axis=1))
    c_grad = (
        dot(held_low, b_rows, 0, 0)
        + dot(grown[0], state_before[0], 1, 1)
        + dot(grown[0], state_before[1], 1, 1)
        + dot(grown[1], state_before[0], 1, 1)
    )
    b_grad = (
        dot(held_low, c_rows)
        + dot(ended[0], state_parts[0], 1, 1)
        + dot(ended[0], state_parts[1], 1, 1)
        + dot(ended[1], state_parts[0], 1, 1)
    )
    fresh = sum(dot(c_rows, part, 0, 0) for part in grown)
    carried[...] = jnp.concatenate(ends, axis=1) * state_grad + fresh
    picker = (
        lax.broadcasted_iota(jnp.int32, (width, LANES), 0) // HEAD
        == lax.broadcasted_iota(jnp.int32, (width, LANES), 1)
    ).astype(F32).astype(BF)
    overlap = jnp.sum(state_grad * state_next_ref[0], axis=0, keepdims=True)
    closing_grad = sum(
        dot(part, picker) for part in thirds(jnp.broadcast_to(overlap, (8, width)))
    )[0:1]
    cumulative_grad = sum(
        dot(part, picker) for part in halves(jnp.concatenate(shaped_grads, axis=1))
    )
    lower = lower_mask(SPAN).astype(F32).astype(BF)
    decay_grad = sum(dot(lower, part, 0, 0) for part in halves(cumulative_grad)) + closing_grad
    step_grad = (
        sum(dot(part, picker) for part in halves(jnp.concatenate(weighted_grads, axis=1)))
        - rate * decay_grad
    )
    step_in_grad = step_grad * sigmoid(step_in)
    head_sum[0:1, :] += jnp.sum(decay * decay_grad, axis=0, keepdims=True)
    head_sum[1:2, :] += jnp.sum(step_in_grad, axis=0, keepdims=True)
    pre = pre_ref[...]
    pre_s = sigmoid(pre)
    slope = pre_s * (1.0 + pre * (1.0 - pre_s))
    ahead[:SPAN, :] = jnp.concatenate(signal_grads + [b_grad, c_grad], axis=1) * slope
    raw = raw_ref[...]
    raw_grad = None
    for shift in range(CONV):
        moved = ahead[shift : shift + SPAN, :]
        tap = CONV - 1 - shift
        term = taps_ref[tap : tap + 1, :] * moved
        raw_grad = term if raw_grad is None else raw_grad + term
        tap_sum[tap : tap + 1, :] += jnp.sum(raw * moved, axis=0, keepdims=True)
        if shift == 0:
            tap_sum[CONV : CONV + 1, :] += jnp.sum(moved, axis=0, keepdims=True)
    ahead[SPAN:, :] = ahead[0:8, :]

    low = jnp.concatenate(
        [gate_grad.astype(BF), raw_grad.astype(BF), step_in_grad.astype(BF)], axis=1
    )
    normed = normed_ref[...]
    weight_sum[...] += dot(normed, low, 0, 0)
    part = dot(low, weight_ref[...], 1, 1)
    store_part(ids, at, own_chunks, part_refs, part.astype(BF))
    inputs = u_own[...].astype(F32)
    scale = lax.rsqrt(jnp.mean(inputs * inputs, axis=-1, keepdims=True) + EPSILON)
    gain_sum[0:1, :] += jnp.sum(part * (inputs * scale), axis=0, keepdims=True)

    @pl.when(step_at == pl.num_programs(0) - 1)
    def _():
        rows = weight_sum.shape[0] // len(masks)
        model = weight_sum.shape[0]
        first = first_kept_ref.shape[2]
        kept_count = first_kept_ref.shape[0]
        out_rows[...] = jnp.transpose(out_sum[...])
        step_lanes = weight_sum.shape[1] - first
        for place, mask in enumerate(masks):
            first_ref = first_kept_ref if place < kept_count else first_sent_ref
            position = place if place < kept_count else place - kept_count
            block = ids[0] ^ mask
            conv_part = pltpu.roll(
                tap_sum[:, width:], (MAPS - block * (MAPS // len(masks))) % MAPS, 1
            )[:, :LANES]
            gain_part = pltpu.roll(gain_sum[...], (model - block * rows) % model, 1)[:, :LANES]
            mixed_part = jnp.concatenate(
                [conv_part[: CONV + 1], gain_part[0:1], head_sum[0:2, :]], axis=0
            )
            small = jnp.concatenate([tap_sum[:, :width], mixed_part], axis=1)
            both = jnp.concatenate(halves(small), axis=1)
            picked = pl.ds(pl.multiple_of(block * rows, 8), rows)
            first_ref[position, 0:SMALL, :] = both
            first_ref[position, SMALL:, :] = weight_sum[picked, :first].astype(BF)
            second_ref = second_refs[place % kept_count]
            near = place // kept_count
            second_ref[near, :, :step_lanes] = weight_sum[picked, first:].astype(BF)
            second_ref[near, :, step_lanes:] = out_rows[picked, :].astype(BF)


def pad_to(values, axis, size):
    if values.shape[axis] == size:
        return values
    pads = [(0, 0)] * values.ndim
    pads[axis] = (0, size - values.shape[axis])
    return jnp.pad(values, pads)


def whole_spec(shape):
    return pl.BlockSpec(shape, lambda *_: (0,) * len(shape))


def lamb_parts(weight, gradient, first_old, second_old):
    first_new = DECAY * first_old + (1.0 - DECAY) * gradient
    second_new = DECAY * second_old + (1.0 - DECAY) * gradient * gradient
    direction = (
        first_new / BIAS_FIRST / (jnp.sqrt(second_new / BIAS_SECOND) + ADAM_EPSILON)
        + WEIGHT_DECAY * weight
    )
    return (first_new, second_new, direction)


def total_of(values):
    while len(values.shape) > 2:
        values = jnp.sum(values, axis=0)
    return jnp.sum(jnp.sum(values, axis=1, keepdims=True), axis=0, keepdims=True)


def lamb_one(position, copies, gradient, olds, outs, norms):
    weight = olds[0][...]
    first_new, second_new, direction = lamb_parts(weight, gradient, olds[1][...], olds[2][...])
    outs[0][...] = gradient
    outs[1][...] = first_new
    outs[2][...] = second_new
    outs[3][...] = direction
    lanes = lane_ids((1, LANES))
    share = 1.0 / copies
    return (
        norms
        + jnp.where(lanes == position, total_of(weight * weight) * share, 0.0)
        + jnp.where(lanes == 8 + position, total_of(direction * direction) * share, 0.0)
    )


def small_sum(rows):
    half = rows.shape[1] // 2
    return rows[:, :half] + rows[:, half:]


def pack_kernel(width, tensor_count, ids, kept_ref, *refs):
    received = refs[:-1]
    packed_ref = refs[-1]
    maps_rows = packed_ref.shape[1] - 8
    lanes = slice(2 * width, 2 * width + MAPS)
    parts = [ref[...].astype(F32) for ref in [kept_ref, *received]]
    state = sum(part[SMALL:, lanes] for part in parts)
    small = small_sum(sum(part[:SMALL] for part in parts))[:, width:]
    for at in range(tensor_count):
        packed_ref[at, 0:8, :LANES] = small
        packed_ref[at, 0:8, LANES:] = small
        packed_ref[at, 8:, :] = state[at * maps_rows : (at + 1) * maps_rows, :]


def lamb_wide_kernel(width, channels, heads, copies, firsts, seconds, ids, *refs):
    whole = sum(ref[...].astype(F32) for ref in refs[:firsts])
    rest = sum(ref[...].astype(F32) for ref in refs[firsts : firsts + seconds])
    count = firsts + seconds
    olds = refs[count : count + 15]
    outs = refs[count + 15 : count + 35]
    norms_ref = refs[count + 35]
    block = whole[SMALL:]
    small = small_sum(whole[:SMALL])
    norms = jnp.zeros((1, LANES), F32)
    in_grad = jnp.stack([block[:, :channels], block[:, width : width + channels]], axis=1)
    step_grad = jnp.transpose(rest[:, :LANES])[:heads]
    out_grad = rest[:, LANES : LANES + channels]
    channel_grad = small[: CONV + 2, :channels]
    picker = (
        lax.broadcasted_iota(jnp.int32, (width, LANES), 0) // HEAD
        == lax.broadcasted_iota(jnp.int32, (width, LANES), 1)
    ).astype(F32)
    skips = dot(small[:, :width], picker, precision=HIGHEST)
    head_grad = jnp.concatenate(
        [small[6:8, width : width + LANES], skips[6:7, :]], axis=0
    )[:, :heads]
    gradients = (in_grad, step_grad, out_grad, channel_grad, head_grad)
    for position, gradient in enumerate(gradients):
        norms = lamb_one(
            position,
            copies if position > 2 else 1.0,
            gradient,
            olds[position::5],
            outs[position::5],
            norms,
        )
    norms_ref[...] = norms


def lamb_maps_kernel(ids, packed_ref, *refs):
    olds = refs[:9]
    norms_in_ref = refs[9]
    outs = refs[10:22]
    norms_ref = refs[22]
    whole = jnp.sum(packed_ref[...], axis=0)
    small = whole[:8]
    conv_rows = olds[1].shape[0]
    gain_size = olds[2].shape[1]
    picker = (
        lax.broadcasted_iota(jnp.int32, (conv_rows, LANES), 0) + ids[1] * conv_rows
        == lax.broadcasted_iota(jnp.int32, (conv_rows, LANES), 1)
    ).astype(F32)
    conv_grad = dot(picker, small[:, :LANES], 1, 1, precision=HIGHEST)[:, : CONV + 1]
    gain_grad = pltpu.roll(small[:, LANES:], (LANES - ids[1] * gain_size) % LANES, 1)[
        CONV + 1 : CONV + 2, :gain_size
    ]
    norms = norms_in_ref[...]
    for position, gradient in enumerate((whole[8:], conv_grad, gain_grad)):
        norms = lamb_one(
            5 + position, 1.0, gradient, olds[position::3], outs[position::3], norms
        )
    norms_ref[...] = jnp.broadcast_to(norms[None], norms_ref.shape)


def update_kernel(ids, norms_ref, *refs):
    norms = jnp.sqrt(jnp.sum(norms_ref[...], axis=0))
    refs[-1][...] = jnp.concatenate([norms[:, :8], norms[:, 8:16]], axis=0)
    for position in range(8):
        ratio = -RATE * norms[:, position : position + 1] / norms[:, 8 + position : 9 + position]
        direction = refs[position][...]
        if direction.ndim == 3:
            ratio = ratio[None]
        refs[8 + position][...] = ratio * direction


def split_three(values):
    high = lax.reduce_precision(values, 8, 7)
    rest = values - high
    middle = lax.reduce_precision(rest, 8, 7)
    return [high.astype(BF), middle.astype(BF), (rest - middle).astype(BF)]


def local(*arguments):
    block_input, output_grad, lengths = arguments[:3]
    masters = arguments[3:11]
    firsts = arguments[11:19]
    seconds = arguments[19:27]
    (
        in_proj,
        step_proj,
        out_proj,
        channel_params,
        head_params,
        state_proj,
        state_conv,
        norm_gain,
    ) = masters
    dp_count = lax.axis_size("dp")
    tensor_count = lax.axis_size("tensor")
    dp_at = lax.axis_index("dp")
    tensor_at = lax.axis_index("tensor")
    everywhere = dp_count * tensor_count
    own_count, model = block_input.shape
    tokens = own_count * tensor_count
    chunks = tokens // SPAN
    own_chunks = own_count // SPAN
    rows = in_proj.shape[0]
    channels = in_proj.shape[2]
    heads = head_params.shape[1]
    width = -(-channels // LANES) * LANES
    mixed_width = width + MAPS
    columns = 2 * width + MAPS + LANES
    dp_low = low_count(dp_count)
    ids = jnp.stack([dp_at, tensor_at]).astype(jnp.int32)

    in_low = jnp.concatenate(
        [
            pad_to(in_proj[:, 0, :].astype(BF), 1, width),
            pad_to(in_proj[:, 1, :].astype(BF), 1, width),
            pad_to(step_proj.astype(BF), 1, LANES),
        ],
        axis=1,
    )
    out_low = pad_to(out_proj.astype(BF), 1, width)
    highs = list(range(dp_low, dp_count, dp_low))
    nears = list(range(1, dp_low))
    tensor_highs = list(range(2, tensor_count, 2))
    landed = together(
        *[exchange(block_input, "tensor", mask) for mask in tensor_highs],
        *[exchange(in_low, "dp", mask) for mask in highs],
        *[exchange(in_low, "dp", mask) for mask in nears],
    )
    u_far = dict(zip(tensor_highs, landed))
    in_far = landed[len(tensor_highs) : len(tensor_highs) + len(highs)]
    in_own_near = landed[len(tensor_highs) + len(highs) :]
    in_stack = jnp.stack(in_far)
    maps_rows = state_proj.shape[0]
    conv_rows = state_conv.shape[0]
    small_own = jnp.concatenate(
        split_three(state_conv.reshape(-1)) + split_three(norm_gain), axis=0
    )
    shared_own = jnp.concatenate(
        [state_proj.astype(BF), pad_to(small_own, 0, MAPS)[None, :]], axis=0
    )
    in_stack, shared_own = together(in_stack, shared_own)
    shared = lax.all_to_all(
        jnp.broadcast_to(shared_own[None], (everywhere,) + shared_own.shape),
        ("dp", "tensor"),
        0,
        0,
    )
    u_pieces = gather_near(block_input, u_far, "tensor", 2)
    out_start, in_stack = together(out_low, in_stack)
    shared, *landed = together(
        shared,
        *u_pieces[1:],
        *[exchange(in_stack, "dp", near) for near in nears],
        *[exchange(out_start, "dp", mask) for mask in highs],
    )
    u_pieces = [block_input] + landed[: tensor_count - 1]
    in_near = landed[tensor_count - 1 : tensor_count - 1 + len(nears)]
    out_far = landed[tensor_count - 1 + len(nears) :]
    out_stack = jnp.stack([out_start] + out_far)
    grad_own, out_stack, *_ = together(output_grad, out_stack, u_far[2])
    grad_far = gather_far(grad_own, "tensor", 2)
    out_near = [exchange(out_stack, "dp", near) for near in nears]
    in_pieces = [in_low] + in_own_near + in_far + in_near
    piece_masks = [0] + nears + highs + [high + near for near in nears for high in highs]
    out_masks = [0] + highs + [high + near for near in nears for high in [0] + highs]
    direct = rows % 16 == 0
    if not direct:
        order = dp_at ^ jnp.arange(dp_count)

        def ordered(pieces, masks):
            parts = [piece if piece.ndim == 3 else piece[None] for piece in pieces]
            places = jnp.array([masks.index(mask) for mask in range(dp_count)])[order]
            return jnp.concatenate(parts, axis=0)[places].reshape(model, -1)

        in_pieces = [ordered(in_pieces, piece_masks)]
    state_weight = shared[:, :maps_rows].reshape(-1, MAPS)
    small_all = shared[:, maps_rows].astype(F32)
    conv_size = conv_rows * (CONV + 1)
    conv_whole = sum(
        small_all[:, part * conv_size : (part + 1) * conv_size] for part in range(3)
    ).reshape(-1, CONV + 1)
    gain_base = 3 * conv_size
    gain_size = norm_gain.shape[0]
    gain_whole = sum(
        small_all[:, gain_base + part * gain_size : gain_base + (part + 1) * gain_size]
        for part in range(3)
    ).reshape(-1)
    channel_wide = pad_to(channel_params, 1, width)
    taps = pad_to(
        jnp.concatenate([channel_wide[: CONV + 1], conv_whole.T], axis=1), 0, 8
    )
    heads_wide = pad_to(pad_to(head_params, 1, LANES), 0, 8)
    skip_wide = jnp.repeat(pad_to(head_params[2], 0, width // HEAD), HEAD)
    skip_gain = pad_to(jnp.stack([skip_wide, channel_wide[CONV + 1]]), 0, 8)
    gain_rows = pad_to(gain_whole[None, :], 0, 8)

    block_rows = min(own_count, 2 * SPAN)

    def token_spec(size, reverse=False, span=SPAN):
        if reverse:
            return pl.BlockSpec((SPAN, size), lambda at, *_: (chunks - 1 - at, 0))
        return pl.BlockSpec((span, size), lambda at, *_: (at, 0))

    def piece_specs(reverse=False, span=SPAN):
        inners = own_count // span

        def spec(mask):
            def index(at, ids_ref, *_):
                block = chunks - 1 - at if reverse else at
                mine = (block // inners) ^ ids_ref[1] == mask
                return (jnp.where(mine, block % inners, 0), 0)

            return pl.BlockSpec((span, model), index)

        return [spec(mask) for mask in range(tensor_count)]

    def part_specs(reverse=False, span=SPAN):
        inners = own_count // span

        def spec(odd):
            def index(at, ids_ref, *_):
                block = chunks - 1 - at if reverse else at
                owner = block // inners
                inner = block % inners
                mine = ((owner ^ ids_ref[1]) & 1) == odd
                if reverse:
                    other = jnp.where(owner > 0, owner - 1, 1)
                    other_inner = jnp.where(owner > 0, inners - 1, 0)
                else:
                    last = tensor_count - 1
                    other = jnp.where(owner < last, owner + 1, last - 1)
                    other_inner = jnp.where(owner < last, 0, inners - 1)
                owner = jnp.where(mine, owner, other)
                return ((owner ^ ids_ref[1]) >> 1, jnp.where(mine, inner, other_inner), 0)

            return pl.BlockSpec((1, span, model), index)

        return [spec(0), spec(1)]

    def struct(shape, dtype=F32):
        return jax.ShapeDtypeStruct(shape, dtype)

    arbitrary = pltpu.CompilerParams(
        dimension_semantics=("arbitrary",), vmem_limit_bytes=VMEM
    )
    if not direct:
        piece_masks = [None]
    normed, gate_raw, raw, pre, act, step_in, states, mixed, weight, gained, squares = pl.pallas_call(
        functools.partial(forward_kernel, width, len(in_pieces), piece_masks, tensor_count, own_chunks),
        grid_spec=pltpu.PrefetchScalarGridSpec(
            num_scalar_prefetch=1,
            grid=(chunks,),
            in_specs=piece_specs()
            + [whole_spec(piece.shape) for piece in in_pieces]
            + [
                whole_spec(state_weight.shape),
                whole_spec(gain_rows.shape),
                whole_spec(taps.shape),
                whole_spec(heads_wide.shape),
                whole_spec(skip_gain.shape),
            ],
            out_specs=[
                token_spec(model),
                token_spec(width),
                token_spec(mixed_width),
                token_spec(mixed_width),
                token_spec(mixed_width),
                token_spec(3 * LANES),
                pl.BlockSpec((1, STATE, width), lambda at, *_: (at, 0, 0)),
                token_spec(width),
                whole_spec((model, columns)),
                token_spec(width),
                pl.BlockSpec((8, SPAN), lambda at, *_: (0, at)),
            ],
            scratch_shapes=[
                pltpu.VMEM((SPAN + 8, mixed_width), F32),
                pltpu.VMEM((STATE, width), F32),
                pltpu.VMEM((SPAN, model), BF),
            ],
        ),
        out_shape=[
            struct((tokens, model), BF),
            struct((tokens, width)),
            struct((tokens, mixed_width)),
            struct((tokens, mixed_width)),
            struct((tokens, mixed_width), BF),
            struct((tokens, 3 * LANES)),
            struct((chunks, STATE, width)),
            struct((tokens, width)),
            struct((model, columns), BF),
            struct((tokens, width)),
            struct((8, tokens)),
        ],
        compiler_params=arbitrary,
        name="ssd_forward",
    )(ids, *u_pieces, *in_pieces, state_weight, gain_rows, taps, heads_wide, skip_gain)

    gate_raw, *landed = together(gate_raw, *grad_far.values(), *out_near)
    grad_far = dict(zip(grad_far, landed))
    out_near = landed[len(grad_far) :]
    grad_pieces = gather_near(grad_own, grad_far, "tensor", 2)
    out_pieces = [out_start] + out_far + out_near
    if not direct:
        out_pieces = [ordered(out_pieces, out_masks)]
        out_masks = [None]
    merged_grad, *branch_parts, sums_part = pl.pallas_call(
        functools.partial(
            middle_kernel, tensor_count, len(out_pieces), out_masks, own_count // block_rows
        ),
        grid_spec=pltpu.PrefetchScalarGridSpec(
            num_scalar_prefetch=2,
            grid=(tokens // block_rows,),
            in_specs=[
                *piece_specs(span=block_rows),
                *[whole_spec(piece.shape) for piece in out_pieces],
                token_spec(width, span=block_rows),
                pl.BlockSpec((8, block_rows), lambda at, *_: (0, at)),
            ],
            out_specs=[
                token_spec(width, span=block_rows),
                *part_specs(span=block_rows),
                pl.BlockSpec((2, block_rows), lambda at, *_: (0, at)),
            ],
            scratch_shapes=[pltpu.VMEM((block_rows, model), BF), pltpu.VMEM((model, width), BF)],
        ),
        out_shape=[
            struct((tokens, width)),
            *[struct((tensor_count // 2, own_count, model), BF)] * 2,
            struct((2, tokens)),
        ],
        compiler_params=arbitrary,
        name="gate_middle",
    )(ids, lengths, *grad_pieces, *out_pieces, gained, squares)

    branch_kept, branch_sent = branch_parts
    branch_near, *sums = together(
        exchange(branch_sent, "tensor", 1),
        *[exchange(sums_part, "tensor", mask) for mask in range(1, tensor_count)],
    )
    sums = [sums_part] + sums
    branch_out = branch_kept[1:].astype(F32) + branch_near[1:].astype(F32)
    branch_far = [
        exchange(branch_out[position].astype(BF), "tensor", 2 * position + 2)
        for position in range(tensor_count // 2 - 1)
    ]
    masks = slot_masks(dp_count, dp_low)
    first_columns = 2 * width + MAPS
    second_columns = LANES + width
    kept_slots = dp_count // dp_low
    token_back = functools.partial(token_spec, reverse=True)
    normed_kept, normed_sent, first_kept, first_sent, *seconds_out = pl.pallas_call(
        functools.partial(backward_kernel, width, masks, tensor_count, own_chunks),
        grid_spec=pltpu.PrefetchScalarGridSpec(
            num_scalar_prefetch=2,
            grid=(chunks,),
            in_specs=[
                *piece_specs(True),
                *piece_specs(True),
                *[pl.BlockSpec((2, SPAN), lambda at, *_: (0, chunks - 1 - at))] * tensor_count,
                token_back(model),
                token_back(width),
                token_back(width),
                token_back(width),
                token_back(mixed_width),
                token_back(mixed_width),
                token_back(mixed_width),
                token_back(3 * LANES),
                pl.BlockSpec((1, STATE, width), lambda at, *_: (chunks - 1 - at, 0, 0)),
                pl.BlockSpec(
                    (1, STATE, width), lambda at, *_: (jnp.minimum(chunks - at, chunks - 1), 0, 0)
                ),
                whole_spec((model, columns)),
                whole_spec(taps.shape),
                whole_spec(heads_wide.shape),
                whole_spec(skip_gain.shape),
                whole_spec(gain_rows.shape),
            ],
            out_specs=[
                *part_specs(True),
                whole_spec((kept_slots, SMALL + rows, first_columns)),
                whole_spec((dp_count - kept_slots, SMALL + rows, first_columns)),
                *[whole_spec((dp_low, rows, second_columns))] * kept_slots,
            ],
            scratch_shapes=[
                pltpu.VMEM((STATE, width), F32),
                pltpu.VMEM((SPAN + 8, mixed_width), F32),
                pltpu.VMEM((model, columns), F32),
                pltpu.VMEM((width, model), F32),
                pltpu.VMEM((8, mixed_width), F32),
                pltpu.VMEM((8, LANES), F32),
                pltpu.VMEM((8, model), F32),
                pltpu.VMEM((SPAN, model), BF),
                pltpu.VMEM((SPAN, model), BF),
                pltpu.VMEM((model, width), F32),
            ],
        ),
        out_shape=[
            *[struct((tensor_count // 2, own_count, model), BF)] * 2,
            struct((kept_slots, SMALL + rows, first_columns), BF),
            struct((dp_count - kept_slots, SMALL + rows, first_columns), BF),
            *[struct((dp_low, rows, second_columns), BF)] * kept_slots,
        ],
        compiler_params=arbitrary,
        name="ssd_backward",
    )(
        ids,
        lengths,
        *u_pieces,
        *grad_pieces,
        *sums,
        normed,
        gate_raw,
        mixed,
        merged_grad,
        raw,
        pre,
        act,
        step_in,
        states,
        states,
        weight,
        taps,
        heads_wide,
        skip_gain,
        gain_rows,
    )

    first_kept, first_sent, *branch_far = together(first_kept, first_sent, *branch_far)
    highs_count = first_kept.shape[0]
    first_near = [
        exchange(
            first_sent
            if dp_low == 2
            else first_sent[(near - 1) * highs_count : near * highs_count],
            "dp",
            near,
        )
        for near in nears
    ]
    second_far = [
        exchange(seconds_out[position], "dp", position * dp_low)
        for position in range(1, kept_slots)
    ]
    normed_near = exchange(normed_sent, "tensor", 1)
    landed = together(normed_near, *first_near, *second_far)
    normed_total = normed_kept.astype(F32) + landed[0].astype(F32)
    first_total = first_kept.astype(F32)
    for values in landed[1 : 1 + len(first_near)]:
        first_total = first_total + values.astype(F32)
    second_far = landed[1 + len(first_near) :]
    middle = first_columns // 2
    joined = first_total[:, :SMALL, :middle] + first_total[:, :SMALL, middle:]
    high = lax.reduce_precision(joined, 8, 7)
    first_total = jnp.concatenate(
        [jnp.concatenate([high, joined - high], axis=2), first_total[:, SMALL:]], axis=1
    )
    first_parts = [first_total[0]] + far_parts(first_total, "dp", dp_low)
    second_total = seconds_out[0].astype(F32)
    for values in second_far:
        second_total = second_total + values.astype(F32)
    second_parts = [second_total[0]] + [
        exchange(second_total[near].astype(BF), "dp", near) for near in range(1, dp_low)
    ]
    landed = together(*first_parts, *second_parts)
    first_parts = landed[: len(first_parts)]
    second_parts = landed[len(first_parts) :]

    inputs = block_input.astype(F32)
    position_all = tensor_at * own_count + jnp.arange(own_count, dtype=jnp.int32)
    length_of = jnp.sum(
        jnp.where(
            (position_all // LMAX)[:, None]
            == jnp.arange(lengths.shape[0], dtype=jnp.int32)[None, :],
            lengths[None, :],
            0,
        ),
        axis=1,
    )
    live_own = (position_all % LMAX < length_of)[:, None]
    own_squares = lax.dynamic_slice(sum(part[0] for part in sums), (tensor_at * own_count,), (own_count,))
    own_scale = lax.rsqrt(own_squares / INNER + EPSILON)[:, None]
    branch = branch_kept[0].astype(F32) + branch_near[0].astype(F32)
    for values in branch_far:
        branch = branch + values.astype(F32)
    output = (inputs + jnp.where(live_own, branch * own_scale, 0.0)).astype(BF)
    normed_grad = normed_total[0]
    for values in far_parts(normed_total, "tensor", 2):
        normed_grad = normed_grad + values.astype(F32)
    scale = lax.rsqrt(jnp.mean(inputs * inputs, axis=-1, keepdims=True) + EPSILON)
    scaled_grad = normed_grad * gain_whole[None, :]
    input_grad = (
        output_grad.astype(F32)
        + scale * scaled_grad
        - inputs * scale**3 * jnp.mean(scaled_grad * inputs, axis=-1, keepdims=True)
    )

    plain = pltpu.CompilerParams(
        dimension_semantics=("arbitrary",), vmem_limit_bytes=VMEM
    )

    def whole_call(kernel, operands, shapes, name):
        return pl.pallas_call(
            kernel,
            grid_spec=pltpu.PrefetchScalarGridSpec(
                num_scalar_prefetch=1,
                grid=(1,),
                in_specs=[whole_spec(value.shape) for value in operands],
                out_specs=[whole_spec(shape.shape) for shape in shapes],
            ),
            out_shape=shapes,
            compiler_params=plain,
            name=name,
        )(ids, *operands)

    (packed,) = whole_call(
        functools.partial(pack_kernel, width, tensor_count),
        first_parts,
        [struct((tensor_count, maps_rows + 8, MAPS))],
        "pack_maps",
    )
    maps_parts = lax.all_to_all(packed, "tensor", 0, 0)
    def wide_of(values):
        return [values[0], values[1].T] + list(values[2:5])

    wide_shapes = [struct(values.shape) for values in wide_of(masters)]
    wide = whole_call(
        functools.partial(
            lamb_wide_kernel,
            width,
            channels,
            heads,
            float(dp_count),
            len(first_parts),
            len(second_parts),
        ),
        [*first_parts, *second_parts, *wide_of(masters), *wide_of(firsts), *wide_of(seconds)],
        wide_shapes * 4 + [struct((1, LANES))],
        "lamb_wide",
    )

    def flat(values):
        return [values[5], values[6], values[7][None, :]]

    maps_shapes = [struct(values.shape) for values in flat(masters)]
    maps = whole_call(
        lamb_maps_kernel,
        [maps_parts, *flat(masters), *flat(firsts), *flat(seconds), wide[20]],
        maps_shapes * 4 + [struct((everywhere, 1, LANES))],
        "lamb_maps",
    )
    spread = lax.all_to_all(maps[12], ("dp", "tensor"), 0, 0)
    spread, input_grad, output = together(spread, input_grad, output)
    updates = whole_call(
        update_kernel,
        [spread, *wide[15:20], *maps[9:12]],
        wide_shapes + maps_shapes + [struct((2, 8))],
        "lamb_update",
    )

    def joined(kind):
        values = list(wide[5 * kind : 5 * kind + 5]) + list(maps[3 * kind : 3 * kind + 3])
        return (values[0], values[1].T) + tuple(values[2:7]) + (values[7][0],)

    return (
        (output, input_grad)
        + joined(0)
        + joined(1)
        + joined(2)
        + (updates[0], updates[1].T)
        + tuple(updates[2:7])
        + (updates[7][0], updates[8])
    )


WEIGHT_SPECS = (
    P("dp", None, "tensor"),
    P("dp", "tensor"),
    P("dp", "tensor"),
    P(None, "tensor"),
    P(None, "tensor"),
    P(("dp", "tensor"), None),
    P(("dp", "tensor"), None),
    P(("dp", "tensor")),
)


def solution(mesh):
    tokens = P(("dp", "tensor"), None)
    return jax.shard_map(
        local,
        mesh=mesh,
        in_specs=(tokens, tokens, P("dp")) + WEIGHT_SPECS * 3,
        out_specs=(tokens, tokens) + WEIGHT_SPECS * 4 + (P(),),
        check_vma=False,
    )
```

```python
import functools

import jax
import jax.numpy as jnp
from jax import lax
from jax.experimental import pallas as pl
from jax.experimental.pallas import tpu as pltpu
from jax.sharding import PartitionSpec as P

STATE = 128
CONV = 4
SPAN = 256
LMAX = 2048
INNER = 1536
HEAD = 64
MAPS = 2 * STATE
LANES = 128
SMALL = 16
VMEM = 60 * 1024 * 1024

EPSILON = 1e-05
ADAM_EPSILON = 1e-06
DECAY = 0.5
BIAS_FIRST = 0.875
BIAS_SECOND = 0.875
RATE = 0.3
WEIGHT_DECAY = 0.01
HIGHEST = lax.Precision.HIGHEST
BF = jnp.bfloat16
F32 = jnp.float32


def dot(left, right, left_dim=1, right_dim=0, precision=None):
    return lax.dot_general(
        left,
        right,
        (((left_dim,), (right_dim,)), ((), ())),
        precision=precision,
        preferred_element_type=F32,
    )


def exchange(values, axis, mask):
    count = lax.axis_size(axis)
    return lax.ppermute(values, axis, [(at, at ^ mask) for at in range(count)])


def low_count(count):
    low = 1
    while low * low * 4 <= count:
        low *= 2
    return low


def together(*values):
    return list(lax.optimization_barrier(values))


def gather_far(own, axis, low):
    return {high: exchange(own, axis, high) for high in range(low, lax.axis_size(axis), low)}


def gather_near(own, far, axis, low):
    count = lax.axis_size(axis)
    pieces = dict(far)
    pieces[0] = own
    for high in range(0, count, low):
        for near in range(1, low):
            pieces[high + near] = exchange(pieces[high], axis, near)
    return [pieces[mask] for mask in range(count)]


def slot_masks(count, low):
    return [high + near for near in range(low) for high in range(0, count, low)]


def near_sum(kept, sent, axis, low):
    highs = kept.shape[0]
    total = kept.astype(F32)
    for near in range(1, low):
        part = sent if low == 2 else sent[(near - 1) * highs : near * highs]
        total = total + exchange(part, axis, near).astype(F32)
    return total


def far_parts(total, axis, low):
    return [
        exchange(total[position].astype(BF), axis, position * low)
        for position in range(1, total.shape[0])
    ]


def lane_ids(shape):
    return lax.broadcasted_iota(jnp.int32, shape, len(shape) - 1)


def lower_mask(size):
    rows = lax.broadcasted_iota(jnp.int32, (size, size), 0)
    columns = lax.broadcasted_iota(jnp.int32, (size, size), 1)
    return rows >= columns


def paired(left, values, head):
    return jnp.where(left, values[:, head : head + 1], values[:, head + 1 : head + 2])


HALF = SPAN // 2
UP = slice(0, HALF)
DOWN = slice(HALF, SPAN)


def halves(values):
    high = values.astype(BF)
    return high, (values - high.astype(F32)).astype(BF)


def thirds(values):
    high = values.astype(BF)
    rest = values - high.astype(F32)
    middle = rest.astype(BF)
    return high, middle, (rest - middle.astype(F32)).astype(BF)


def sigmoid(values):
    return 0.5 * jnp.tanh(0.5 * values) + 0.5


def forward_kernel(channels, pieces, masks, owners, own_chunks, ids, *refs):
    width = channels
    heads = width // HEAD
    mixed_width = width + MAPS
    u_refs = refs[:owners]
    refs = refs[owners:]
    piece_refs = refs[:pieces]
    (
        state_w_ref,
        gain_ref,
        taps_ref,
        heads_ref,
        skip_ref,
        normed_ref,
        gate_ref,
        raw_ref,
        pre_ref,
        act_ref,
        step_ref,
        state_ref,
        mixed_ref,
        weight_ref,
        gained_ref,
        squares_ref,
        tail,
        carried,
        u_own,
    ) = refs[pieces:]
    at = pl.program_id(0)

    @pl.when(at == 0)
    def _():
        place_rows(
            ids,
            masks,
            piece_refs,
            (
                (slice(0, 2 * width), weight_ref, slice(0, 2 * width)),
                (
                    slice(2 * width, 2 * width + LANES),
                    weight_ref,
                    slice(2 * width + MAPS, 2 * width + MAPS + LANES),
                ),
            ),
        )
        weight_ref[:, 2 * width : 2 * width + MAPS] = state_w_ref[...]

    @pl.when(at % (LMAX // SPAN) == 0)
    def _():
        tail[0:8, :] = jnp.zeros((8, mixed_width), F32)
        carried[...] = jnp.zeros_like(carried)

    pick_piece(ids, at, own_chunks, u_refs, u_own)
    inputs = u_own[...].astype(F32)
    scale = lax.rsqrt(jnp.mean(inputs * inputs, axis=-1, keepdims=True) + EPSILON)
    normed = (inputs * scale * gain_ref[0:1, :]).astype(BF)
    normed_ref[...] = normed
    gate_ref[...] = dot(normed, weight_ref[:, :width])
    raw = dot(normed, weight_ref[:, width : 2 * width + MAPS])
    raw_ref[...] = raw
    tail[8:, :] = raw
    step_in = dot(normed, weight_ref[:, 2 * width + MAPS :]) + heads_ref[1:2, :]
    step_ref[:, :LANES] = step_in
    pre = taps_ref[CONV : CONV + 1, :] + taps_ref[0:1, :] * tail[5 : 5 + SPAN, :]
    for tap in range(1, CONV):
        pre = pre + taps_ref[tap : tap + 1, :] * tail[5 + tap : 5 + tap + SPAN, :]
    tail[0:8, :] = tail[SPAN : SPAN + 8, :]
    pre_ref[...] = pre
    act = (pre * sigmoid(pre)).astype(BF)
    act_ref[...] = act
    signal = act[:, :width].astype(F32)
    b_rows = act[:, width : width + STATE]
    c_rows = act[:, width + STATE :]
    step = jnp.maximum(step_in, 0.0) + jnp.log1p(jnp.exp(-jnp.abs(step_in)))
    decay = -jnp.exp(heads_ref[0:1, :]) * step
    lower = lower_mask(SPAN).astype(F32).astype(BF)
    cumulative = sum(dot(lower, part) for part in thirds(decay))
    step_ref[:, LANES : 2 * LANES] = step
    step_ref[:, 2 * LANES :] = cumulative
    across_rows = jnp.transpose(cumulative)
    closing = cumulative[SPAN - 1 : SPAN, :]
    mask = lower_mask(HALF)
    held_first = jnp.where(mask, dot(c_rows[UP], b_rows[UP], 1, 1), 0.0)
    held_cross = dot(c_rows[DOWN], b_rows[UP], 1, 1)
    held_last = jnp.where(mask, dot(c_rows[DOWN], b_rows[DOWN], 1, 1), 0.0)
    left = lane_ids((SPAN, LANES)) < HEAD
    left_row = left[0:1]
    state = carried[...]
    state_ref[0] = state
    across = dot(
        jnp.concatenate([c_rows, c_rows], axis=1), jnp.concatenate(halves(state), axis=0)
    )
    ended = []
    ends = []
    squares = None
    for head in range(0, heads, 2):
        lanes = slice(head * HEAD, head * HEAD + LANES)
        wide = [
            jnp.broadcast_to(cumulative[:, head + side : head + side + 1], (SPAN, LANES))
            for side in range(2)
        ]
        own = jnp.where(left, wide[0], wide[1])
        end = paired(left_row, closing, head)
        pair = (paired(left, step, head) * signal[:, lanes]).astype(BF)
        first = None
        for side in range(2):
            column = wide[side]
            row = across_rows[head + side : head + side + 1, :]
            top = (held_first * jnp.exp(jnp.minimum(column[UP] - row[:, UP], 0.0))).astype(BF)
            cross = (held_cross * jnp.exp(column[DOWN] - row[:, UP])).astype(BF)
            last = (
                held_last * jnp.exp(jnp.minimum(column[DOWN] - row[:, DOWN], 0.0))
            ).astype(BF)
            kept = jnp.where(left if side == 0 else ~left, pair, jnp.zeros_like(pair))
            up = dot(top, kept[UP])
            down = dot(jnp.concatenate([cross, last], axis=1), kept)
            first, second = (up, down) if first is None else (first + up, second + down)
        mixed_own = (
            jnp.concatenate([first, second], axis=0)
            + across[:, lanes] * jnp.exp(own)
            + skip_ref[0:1, lanes] * signal[:, lanes]
        )
        mixed_ref[:, lanes] = mixed_own
        gate_own = gate_ref[:, lanes]
        gated = mixed_own * (gate_own * sigmoid(gate_own))
        gained_ref[:, lanes] = gated * skip_ref[1:2, lanes]
        squares = gated * gated if squares is None else squares + gated * gated
        ended.append(pair.astype(F32) * jnp.exp(end - own))
        ends.append(jnp.exp(end))
    fresh = sum(
        dot(b_rows, part, 0, 0) for part in halves(jnp.concatenate(ended, axis=1))
    )
    carried[...] = jnp.concatenate(ends, axis=1) * state + fresh
    total = jnp.sum(squares, axis=1, keepdims=True)
    squares_ref[...] = jnp.transpose(jnp.broadcast_to(total, (SPAN, LANES)))[0:8, :]


def place_rows(ids, masks, refs, stores):
    at = 0
    for ref in refs:
        stacked = len(ref.shape) == 3
        for inner in range(ref.shape[0] if stacked else 1):
            rows = ref.shape[-2]
            if masks[at] is None:
                target = slice(None)
            else:
                target = pl.ds(pl.multiple_of((ids[0] ^ masks[at]) * rows, 8), rows)
            for columns, into, lanes in stores:
                into[target, lanes] = ref[inner, :, columns] if stacked else ref[:, columns]
            at += 1


def pick_piece(ids, block, own_chunks, refs, scratch):
    mask = (block // own_chunks) ^ ids[1]
    for at, ref in enumerate(refs):

        @pl.when(mask == at)
        def _():
            scratch[...] = ref[...]


def store_part(ids, block, own_chunks, refs, value):
    odd = ((block // own_chunks) ^ ids[1]) & 1
    for at, ref in enumerate(refs):

        @pl.when(odd == at)
        def _():
            ref[0] = value


def rows_live(ids, at, lengths, span=SPAN):
    sequence = at // (LMAX // span)
    position = (at % (LMAX // span)) * span + lax.broadcasted_iota(jnp.int32, (span, 1), 0)
    return position < lengths[sequence]


def middle_kernel(owners, pieces, masks, own_chunks, ids, lengths, *refs):
    grad_refs = refs[:owners]
    piece_refs = refs[owners : owners + pieces]
    (
        gained_ref,
        squares_ref,
        merged_grad_ref,
        kept_ref,
        sent_ref,
        sums_ref,
        grad_own,
        weight,
    ) = refs[owners + pieces :]
    at = pl.program_id(0)
    span = grad_own.shape[0]

    @pl.when(at == 0)
    def _():
        at_mask = 0
        for ref in piece_refs:
            count = ref.shape[0] if len(ref.shape) == 3 else 1
            place_rows(
                ids,
                masks[at_mask : at_mask + count],
                [ref],
                ((slice(ref.shape[-1] - weight.shape[1], ref.shape[-1]), weight, slice(None)),),
            )
            at_mask += count

    pick_piece(ids, at, own_chunks, grad_refs, grad_own)
    upstream = grad_own[...]
    upstream = jnp.where(rows_live(ids, at, lengths, span), upstream, jnp.zeros_like(upstream))
    merged_grad = dot(upstream, weight[...])
    merged_grad_ref[...] = merged_grad
    gained = gained_ref[...]
    products = jnp.sum(merged_grad * gained, axis=1, keepdims=True)
    branch = dot(gained.astype(BF), weight[...], 1, 1).astype(BF)
    store_part(ids, at, own_chunks, (kept_ref, sent_ref), branch)
    flat = jnp.transpose(jnp.broadcast_to(products, (span, LANES)))
    sums_ref[0:1, :] = squares_ref[0:1, :]
    sums_ref[1:2, :] = flat[0:1, :]


def early_kernel(owners, inners, ids, lengths, *refs):
    grad_refs = refs[:owners]
    (
        sums_ref,
        normed_ref,
        gate_ref,
        mixed_ref,
        merged_grad_ref,
        skip_ref,
        slots_ref,
        grad_own,
        gate_sum,
        out_sum,
    ) = refs[owners:]
    at = pl.program_id(0)
    span = grad_own.shape[0]

    @pl.when(at == 0)
    def _():
        gate_sum[...] = jnp.zeros_like(gate_sum)
        out_sum[...] = jnp.zeros_like(out_sum)

    pick_piece(ids, at, inners, grad_refs, grad_own)
    upstream = grad_own[...]
    upstream = jnp.where(rows_live(ids, at, lengths, span), upstream, jnp.zeros_like(upstream))
    gate_scale, cross = scale_columns(sums_ref[...])
    gate = gate_ref[...]
    gate_s = sigmoid(gate)
    mixed = mixed_ref[...]
    gated = mixed * (gate * gate_s)
    gain = skip_ref[1:2, :]
    merged = (gated * gate_scale * gain).astype(BF)
    gated_grad = gate_scale * (merged_grad_ref[...] * gain) - gated * cross
    gate_grad = gated_grad * mixed * (gate_s * (1.0 + gate * (1.0 - gate_s)))
    out_sum[...] += dot(merged, upstream, 0, 0)
    gate_sum[...] += dot(gate_grad.astype(BF), normed_ref[...], 0, 0)

    @pl.when(at == pl.num_programs(0) - 1)
    def _():
        count, rows, columns = slots_ref.shape
        both = jnp.concatenate(
            [jnp.transpose(gate_sum[...]), jnp.transpose(out_sum[...])], axis=1
        ).astype(BF)
        slots_ref[...] = both.reshape(count, rows, columns)


def scale_columns(sums):
    scale_row = lax.rsqrt(sums[0:1, :] / INNER + EPSILON)
    cross_row = scale_row * scale_row * scale_row * (sums[1:2, :] / INNER)
    row_ids = lax.broadcasted_iota(jnp.int32, (LANES, sums.shape[1]), 0)
    columns = jnp.transpose(jnp.where(row_ids == 0, scale_row, cross_row))
    return columns[:, 0:1], columns[:, 1:2]


def backward_kernel(channels, masks, owners, own_chunks, ids, lengths, *refs):
    u_refs = refs[:owners]
    backward_step(channels, masks, own_chunks, ids, lengths, u_refs, (), *refs[owners:])


def backward_step(
    channels,
    masks,
    own_chunks,
    ids,
    lengths,
    u_refs,
    grad_refs,
    sums_ref,
    normed_ref,
    gate_ref,
    mixed_ref,
    merged_grad_ref,
    raw_ref,
    pre_ref,
    act_ref,
    step_ref,
    state_ref,
    state_next_ref,
    weight_ref,
    taps_ref,
    heads_ref,
    skip_ref,
    gain_ref,
    part_kept_ref,
    part_sent_ref,
    first_kept_ref,
    first_sent_ref,
    *refs,
):
    low = low_count(len(masks))
    second_refs = refs[: len(masks) // low]
    backward_body(
        channels,
        masks,
        own_chunks,
        ids,
        lengths,
        u_refs,
        grad_refs,
        (sums_ref, normed_ref, gate_ref, mixed_ref, merged_grad_ref, raw_ref, pre_ref, act_ref),
        (step_ref, state_ref, state_next_ref, weight_ref, taps_ref, heads_ref, skip_ref, gain_ref),
        (part_kept_ref, part_sent_ref),
        (first_kept_ref, first_sent_ref, second_refs),
        *refs[len(masks) // low :],
    )


def backward_body(
    channels,
    masks,
    own_chunks,
    ids,
    lengths,
    u_refs,
    grad_refs,
    token_refs,
    other_refs,
    part_refs,
    slot_refs,
    carried,
    ahead,
    weight_sum,
    tap_sum,
    head_sum,
    gain_sum,
    u_own,
):
    sums_ref, normed_ref, gate_ref, mixed_ref, merged_grad_ref, raw_ref, pre_ref, act_ref = token_refs
    step_ref, state_ref, state_next_ref, weight_ref, taps_ref, heads_ref, skip_ref, gain_ref = other_refs
    first_kept_ref, first_sent_ref, second_refs = slot_refs
    width = channels
    heads = width // HEAD
    mixed_width = width + MAPS
    step_at = pl.program_id(0)
    at = pl.num_programs(0) - 1 - step_at

    @pl.when(step_at == 0)
    def _():
        weight_sum[...] = jnp.zeros_like(weight_sum)
        tap_sum[...] = jnp.zeros_like(tap_sum)
        head_sum[...] = jnp.zeros_like(head_sum)
        gain_sum[...] = jnp.zeros_like(gain_sum)

    @pl.when(step_at % (LMAX // SPAN) == 0)
    def _():
        carried[...] = jnp.zeros_like(carried)
        ahead[SPAN:, :] = jnp.zeros((8, mixed_width), F32)

    pick_piece(ids, at, own_chunks, u_refs, u_own)
    gate_scale, cross = scale_columns(sums_ref[...])

    gate = gate_ref[...]
    gate_s = sigmoid(gate)
    gate_act = gate * gate_s
    mixed = mixed_ref[...]
    gated = mixed * gate_act
    merged_grad = merged_grad_ref[...]
    gain = skip_ref[1:2, :]
    scaled = gated * gate_scale
    tap_sum[5:6, :width] += jnp.sum(merged_grad * scaled, axis=0, keepdims=True)
    gated_grad = gate_scale * (merged_grad * gain) - gated * cross
    mixed_grad = gated_grad * gate_act
    gate_grad = gated_grad * mixed * (gate_s * (1.0 + gate * (1.0 - gate_s)))

    act = act_ref[...]
    signal = act[:, :width].astype(F32)
    b_rows = act[:, width : width + STATE]
    c_rows = act[:, width + STATE :]
    skip = skip_ref[0:1, :]
    tap_sum[6:7, :width] += jnp.sum(mixed_grad * signal, axis=0, keepdims=True)
    grad_high, grad_rest = halves(mixed_grad)
    grad_rows = grad_high.astype(F32) + grad_rest.astype(F32)

    step_in = step_ref[:, :LANES]
    step = step_ref[:, LANES : 2 * LANES]
    cumulative = step_ref[:, 2 * LANES :]
    rate = jnp.exp(heads_ref[0:1, :])
    decay = -rate * step
    across_rows = jnp.transpose(cumulative)
    closing = cumulative[SPAN - 1 : SPAN, :]
    mask = lower_mask(HALF)
    upper = lax.broadcasted_iota(jnp.int32, (HALF, HALF), 0) <= lax.broadcasted_iota(
        jnp.int32, (HALF, HALF), 1
    )
    held_first = jnp.where(upper, dot(b_rows[UP], c_rows[UP], 1, 1), 0.0)
    held_cross = dot(b_rows[UP], c_rows[DOWN], 1, 1)
    held_last = jnp.where(upper, dot(b_rows[DOWN], c_rows[DOWN], 1, 1), 0.0)
    left = lane_ids((SPAN, LANES)) < HEAD
    left_row = left[0:1]
    state_grad = carried[...]
    state_parts = halves(state_grad)
    state_before = halves(state_ref[0])
    from_state = dot(
        jnp.concatenate([b_rows, b_rows], axis=1), jnp.concatenate(state_parts, axis=0)
    )
    grads_first = grads_last = grads_cross = None
    grown, ended, ends, weighted_grads, shaped_grads, signal_grads = [], [], [], [], [], []
    for head in range(0, heads, 2):
        lanes = slice(head * HEAD, head * HEAD + LANES)
        wide = [
            jnp.broadcast_to(cumulative[:, head + side : head + side + 1], (SPAN, LANES))
            for side in range(2)
        ]
        own = jnp.where(left, wide[0], wide[1])
        end = paired(left_row, closing, head)
        end_wide = jnp.exp(end - own)
        ends.append(jnp.exp(end))
        step_wide = paired(left, step, head)
        signal_own = signal[:, lanes]
        pair = (step_wide * signal_own).astype(BF)
        pair_rows = pair.astype(F32)
        pair_twice = jnp.concatenate([pair, pair], axis=1)
        grad_own_rows = grad_rows[:, lanes]
        grown.append(grad_own_rows * jnp.exp(own))
        ended.append(pair_rows * end_wide)
        total_up = None
        for side in range(2):
            column = wide[side]
            row = across_rows[head + side : head + side + 1, :]
            damp_first = jnp.exp(jnp.minimum(row[:, UP] - column[UP], 0.0))
            damp_cross = jnp.exp(row[:, DOWN] - column[UP])
            damp_last = jnp.exp(jnp.minimum(row[:, DOWN] - column[DOWN], 0.0))
            side_lanes = left if side == 0 else ~left
            kept = jnp.concatenate(
                [
                    jnp.where(side_lanes, part[:, lanes], jnp.zeros_like(pair))
                    for part in (grad_high, grad_rest)
                ],
                axis=1,
            )
            terms_up = dot(pair_twice[UP], kept, 1, 1)
            terms_first = terms_up[:, UP] * damp_first
            terms_cross = terms_up[:, DOWN] * damp_cross
            terms_last = dot(pair_twice[DOWN], kept[DOWN], 1, 1) * damp_last
            if grads_first is None:
                grads_first, grads_cross, grads_last = terms_first, terms_cross, terms_last
            else:
                grads_first = grads_first + terms_first
                grads_cross = grads_cross + terms_cross
                grads_last = grads_last + terms_last
            mixing_up = jnp.concatenate(
                [(held_first * damp_first).astype(BF), (held_cross * damp_cross).astype(BF)],
                axis=1,
            )
            up = dot(mixing_up, kept)
            down = dot((held_last * damp_last).astype(BF), kept[DOWN])
            total_up, total_down = (
                (up, down) if total_up is None else (total_up + up, total_down + down)
            )
        total = jnp.concatenate([total_up, total_down], axis=0)
        own_grad = total[:, :LANES] + total[:, LANES:] + end_wide * from_state[:, lanes]
        shaped = mixed[:, lanes] - skip[:, lanes] * signal_own
        weighted_grads.append(signal_own * own_grad)
        shaped_grads.append(grad_own_rows * shaped - pair_rows * own_grad)
        signal_grads.append(step_wide * own_grad + skip[:, lanes] * mixed_grad[:, lanes])
    held_low = jnp.concatenate(
        [
            jnp.concatenate(
                [jnp.where(upper, grads_first, 0.0).astype(BF), grads_cross.astype(BF)], axis=1
            ),
            jnp.concatenate(
                [jnp.zeros((HALF, HALF), BF), jnp.where(upper, grads_last, 0.0).astype(BF)], axis=1
            ),
        ],
        axis=0,
    )
    grown = halves(jnp.concatenate(grown, axis=1))
    ended = halves(jnp.concatenate(ended, axis=1))
    c_grad = (
        dot(held_low, b_rows, 0, 0)
        + dot(grown[0], state_before[0], 1, 1)
        + dot(grown[0], state_before[1], 1, 1)
        + dot(grown[1], state_before[0], 1, 1)
    )
    b_grad = (
        dot(held_low, c_rows)
        + dot(ended[0], state_parts[0], 1, 1)
        + dot(ended[0], state_parts[1], 1, 1)
        + dot(ended[1], state_parts[0], 1, 1)
    )
    fresh = sum(dot(c_rows, part, 0, 0) for part in grown)
    carried[...] = jnp.concatenate(ends, axis=1) * state_grad + fresh
    picker = (
        lax.broadcasted_iota(jnp.int32, (width, LANES), 0) // HEAD
        == lax.broadcasted_iota(jnp.int32, (width, LANES), 1)
    ).astype(F32).astype(BF)
    overlap = jnp.sum(state_grad * state_next_ref[0], axis=0, keepdims=True)
    closing_grad = sum(
        dot(part, picker) for part in thirds(jnp.broadcast_to(overlap, (8, width)))
    )[0:1]
    cumulative_grad = sum(
        dot(part, picker) for part in halves(jnp.concatenate(shaped_grads, axis=1))
    )
    lower = lower_mask(SPAN).astype(F32).astype(BF)
    decay_grad = sum(dot(lower, part, 0, 0) for part in halves(cumulative_grad)) + closing_grad
    step_grad = (
        sum(dot(part, picker) for part in halves(jnp.concatenate(weighted_grads, axis=1)))
        - rate * decay_grad
    )
    step_in_grad = step_grad * sigmoid(step_in)
    head_sum[0:1, :] += jnp.sum(decay * decay_grad, axis=0, keepdims=True)
    head_sum[1:2, :] += jnp.sum(step_in_grad, axis=0, keepdims=True)
    pre = pre_ref[...]
    pre_s = sigmoid(pre)
    slope = pre_s * (1.0 + pre * (1.0 - pre_s))
    ahead[:SPAN, :] = jnp.concatenate(signal_grads + [b_grad, c_grad], axis=1) * slope
    raw = raw_ref[...]
    raw_grad = None
    for shift in range(CONV):
        moved = ahead[shift : shift + SPAN, :]
        tap = CONV - 1 - shift
        term = taps_ref[tap : tap + 1, :] * moved
        raw_grad = term if raw_grad is None else raw_grad + term
        tap_sum[tap : tap + 1, :] += jnp.sum(raw * moved, axis=0, keepdims=True)
        if shift == 0:
            tap_sum[CONV : CONV + 1, :] += jnp.sum(moved, axis=0, keepdims=True)
    ahead[SPAN:, :] = ahead[0:8, :]

    low = jnp.concatenate(
        [gate_grad.astype(BF), raw_grad.astype(BF), step_in_grad.astype(BF)], axis=1
    )
    normed = normed_ref[...]
    weight_sum[...] += dot(normed, low[:, width:], 0, 0)
    part = dot(low, weight_ref[...], 1, 1)
    store_part(ids, at, own_chunks, part_refs, part.astype(BF))
    inputs = u_own[...].astype(F32)
    scale = lax.rsqrt(jnp.mean(inputs * inputs, axis=-1, keepdims=True) + EPSILON)
    gain_sum[0:1, :] += jnp.sum(part * (inputs * scale), axis=0, keepdims=True)

    @pl.when(step_at == pl.num_programs(0) - 1)
    def _():
        rows = weight_sum.shape[0] // len(masks)
        model = weight_sum.shape[0]
        first = first_kept_ref.shape[2]
        kept_count = first_kept_ref.shape[0]
        for place, mask in enumerate(masks):
            first_ref = first_kept_ref if place < kept_count else first_sent_ref
            position = place if place < kept_count else place - kept_count
            block = ids[0] ^ mask
            conv_part = pltpu.roll(
                tap_sum[:, width:], (MAPS - block * (MAPS // len(masks))) % MAPS, 1
            )[:, :LANES]
            gain_part = pltpu.roll(gain_sum[...], (model - block * rows) % model, 1)[:, :LANES]
            mixed_part = jnp.concatenate(
                [conv_part[: CONV + 1], gain_part[0:1], head_sum[0:2, :]], axis=0
            )
            small = jnp.concatenate([tap_sum[:, :width], mixed_part], axis=1)
            both = jnp.concatenate(halves(small), axis=0)
            picked = pl.ds(pl.multiple_of(block * rows, 8), rows)
            first_ref[position, 0:SMALL, : both.shape[1]] = both
            first_ref[position, 0:SMALL, both.shape[1] :] = jnp.zeros(
                (SMALL, first - both.shape[1]), BF
            )
            first_ref[position, SMALL:, :] = weight_sum[picked, :first].astype(BF)
            second_ref = second_refs[place % kept_count]
            near = place // kept_count
            second_ref[near, :, :] = weight_sum[picked, first:].astype(BF)


def pad_to(values, axis, size):
    if values.shape[axis] == size:
        return values
    pads = [(0, 0)] * values.ndim
    pads[axis] = (0, size - values.shape[axis])
    return jnp.pad(values, pads)


def whole_spec(shape):
    return pl.BlockSpec(shape, lambda *_: (0,) * len(shape))


def lamb_parts(weight, gradient, first_old, second_old):
    first_new = DECAY * first_old + (1.0 - DECAY) * gradient
    second_new = DECAY * second_old + (1.0 - DECAY) * gradient * gradient
    direction = (
        first_new / BIAS_FIRST / (jnp.sqrt(second_new / BIAS_SECOND) + ADAM_EPSILON)
        + WEIGHT_DECAY * weight
    )
    return (first_new, second_new, direction)


def total_of(values):
    while len(values.shape) > 2:
        values = jnp.sum(values, axis=0)
    return jnp.sum(jnp.sum(values, axis=1, keepdims=True), axis=0, keepdims=True)


def lamb_one(position, copies, gradient, olds, outs, norms):
    weight = olds[0][...]
    first_new, second_new, direction = lamb_parts(weight, gradient, olds[1][...], olds[2][...])
    outs[0][...] = gradient
    outs[1][...] = first_new
    outs[2][...] = second_new
    outs[3][...] = direction
    lanes = lane_ids((1, LANES))
    share = 1.0 / copies
    return (
        norms
        + jnp.where(lanes == position, total_of(weight * weight) * share, 0.0)
        + jnp.where(lanes == 8 + position, total_of(direction * direction) * share, 0.0)
    )


def small_sum(rows):
    return rows[: SMALL // 2] + rows[SMALL // 2 :]


def pack_kernel(width, tensor_count, ids, kept_ref, *refs):
    received = refs[:-1]
    packed_ref = refs[-1]
    maps_rows = packed_ref.shape[1] - 8
    lanes = slice(width, width + MAPS)
    parts = [ref[...].astype(F32) for ref in [kept_ref, *received]]
    state = sum(part[SMALL:, lanes] for part in parts)
    small = small_sum(sum(part[:SMALL] for part in parts))[:, width : width + LANES]
    for at in range(tensor_count):
        packed_ref[at, 0:8, :LANES] = small
        packed_ref[at, 0:8, LANES:] = small
        packed_ref[at, 8:, :] = state[at * maps_rows : (at + 1) * maps_rows, :]


def lamb_wide_kernel(width, channels, heads, copies, firsts, seconds, ids, early_ref, *refs):
    early = jnp.sum(early_ref[...].astype(F32), axis=0)
    whole = sum(ref[...].astype(F32) for ref in refs[:firsts])
    rest = sum(ref[...].astype(F32) for ref in refs[firsts : firsts + seconds])
    count = firsts + seconds
    olds = refs[count : count + 15]
    outs = refs[count + 15 : count + 35]
    norms_ref = refs[count + 35]
    block = whole[SMALL:]
    small = small_sum(whole[:SMALL])
    norms = jnp.zeros((1, LANES), F32)
    in_grad = jnp.stack([early[:, :channels], block[:, :channels]], axis=1)
    step_grad = jnp.transpose(rest[:, :LANES])[:heads]
    out_grad = early[:, width : width + channels]
    channel_grad = small[: CONV + 2, :channels]
    picker = (
        lax.broadcasted_iota(jnp.int32, (width, LANES), 0) // HEAD
        == lax.broadcasted_iota(jnp.int32, (width, LANES), 1)
    ).astype(F32)
    skips = dot(small[:, :width], picker, precision=HIGHEST)
    head_grad = jnp.concatenate(
        [small[6:8, width : width + LANES], skips[6:7, :]], axis=0
    )[:, :heads]
    gradients = (in_grad, step_grad, out_grad, channel_grad, head_grad)
    for position, gradient in enumerate(gradients):
        norms = lamb_one(
            position,
            copies if position > 2 else 1.0,
            gradient,
            olds[position::5],
            outs[position::5],
            norms,
        )
    norms_ref[...] = norms


def lamb_maps_kernel(ids, packed_ref, *refs):
    olds = refs[:9]
    norms_in_ref = refs[9]
    outs = refs[10:22]
    norms_ref = refs[22]
    whole = jnp.sum(packed_ref[...], axis=0)
    small = whole[:8]
    conv_rows = olds[1].shape[0]
    gain_size = olds[2].shape[1]
    picker = (
        lax.broadcasted_iota(jnp.int32, (conv_rows, LANES), 0) + ids[1] * conv_rows
        == lax.broadcasted_iota(jnp.int32, (conv_rows, LANES), 1)
    ).astype(F32)
    conv_grad = dot(picker, small[:, :LANES], 1, 1, precision=HIGHEST)[:, : CONV + 1]
    gain_grad = pltpu.roll(small[:, LANES:], (LANES - ids[1] * gain_size) % LANES, 1)[
        CONV + 1 : CONV + 2, :gain_size
    ]
    norms = norms_in_ref[...]
    for position, gradient in enumerate((whole[8:], conv_grad, gain_grad)):
        norms = lamb_one(
            5 + position, 1.0, gradient, olds[position::3], outs[position::3], norms
        )
    norms_ref[...] = jnp.broadcast_to(norms[None], norms_ref.shape)


def update_kernel(ids, norms_ref, *refs):
    norms = jnp.sqrt(jnp.sum(norms_ref[...], axis=0))
    refs[-1][...] = jnp.concatenate([norms[:, :8], norms[:, 8:16]], axis=0)
    for position in range(8):
        ratio = -RATE * norms[:, position : position + 1] / norms[:, 8 + position : 9 + position]
        direction = refs[position][...]
        if direction.ndim == 3:
            ratio = ratio[None]
        refs[8 + position][...] = ratio * direction


def split_three(values):
    high = lax.reduce_precision(values, 8, 7)
    rest = values - high
    middle = lax.reduce_precision(rest, 8, 7)
    return [high.astype(BF), middle.astype(BF), (rest - middle).astype(BF)]


def local(*arguments):
    block_input, output_grad, lengths = arguments[:3]
    masters = arguments[3:11]
    firsts = arguments[11:19]
    seconds = arguments[19:27]
    (
        in_proj,
        step_proj,
        out_proj,
        channel_params,
        head_params,
        state_proj,
        state_conv,
        norm_gain,
    ) = masters
    dp_count = lax.axis_size("dp")
    tensor_count = lax.axis_size("tensor")
    dp_at = lax.axis_index("dp")
    tensor_at = lax.axis_index("tensor")
    everywhere = dp_count * tensor_count
    own_count, model = block_input.shape
    tokens = own_count * tensor_count
    chunks = tokens // SPAN
    own_chunks = own_count // SPAN
    rows = in_proj.shape[0]
    channels = in_proj.shape[2]
    heads = head_params.shape[1]
    width = -(-channels // LANES) * LANES
    mixed_width = width + MAPS
    columns = 2 * width + MAPS + LANES
    dp_low = low_count(dp_count)
    ids = jnp.stack([dp_at, tensor_at]).astype(jnp.int32)

    in_low = jnp.concatenate(
        [
            pad_to(in_proj[:, 0, :].astype(BF), 1, width),
            pad_to(in_proj[:, 1, :].astype(BF), 1, width),
            pad_to(step_proj.astype(BF), 1, LANES),
        ],
        axis=1,
    )
    out_low = pad_to(out_proj.astype(BF), 1, width)
    highs = list(range(dp_low, dp_count, dp_low))
    nears = list(range(1, dp_low))
    tensor_highs = list(range(2, tensor_count, 2))
    landed = together(
        *[exchange(block_input, "tensor", mask) for mask in tensor_highs],
        *[exchange(in_low, "dp", mask) for mask in highs],
        *[exchange(in_low, "dp", mask) for mask in nears],
    )
    u_far = dict(zip(tensor_highs, landed))
    in_far = landed[len(tensor_highs) : len(tensor_highs) + len(highs)]
    in_own_near = landed[len(tensor_highs) + len(highs) :]
    in_stack = jnp.stack(in_far)
    maps_rows = state_proj.shape[0]
    conv_rows = state_conv.shape[0]
    small_own = jnp.concatenate(
        split_three(state_conv.reshape(-1)) + split_three(norm_gain), axis=0
    )
    shared_own = jnp.concatenate(
        [state_proj.astype(BF), pad_to(small_own, 0, MAPS)[None, :]], axis=0
    )
    in_stack, shared_own = together(in_stack, shared_own)
    shared = lax.all_to_all(
        jnp.broadcast_to(shared_own[None], (everywhere,) + shared_own.shape),
        ("dp", "tensor"),
        0,
        0,
    )
    u_pieces = gather_near(block_input, u_far, "tensor", 2)
    out_start, in_stack = together(out_low, in_stack)
    shared, *landed = together(
        shared,
        *u_pieces[1:],
        *[exchange(in_stack, "dp", near) for near in nears],
        *[exchange(out_start, "dp", mask) for mask in highs],
    )
    u_pieces = [block_input] + landed[: tensor_count - 1]
    in_near = landed[tensor_count - 1 : tensor_count - 1 + len(nears)]
    out_far = landed[tensor_count - 1 + len(nears) :]
    out_stack = jnp.stack([out_start] + out_far)
    grad_own, out_stack, *_ = together(output_grad, out_stack, u_far[2])
    grad_far = gather_far(grad_own, "tensor", 2)
    out_near = [exchange(out_stack, "dp", near) for near in nears]
    in_pieces = [in_low] + in_own_near + in_far + in_near
    piece_masks = [0] + nears + highs + [high + near for near in nears for high in highs]
    out_masks = [0] + highs + [high + near for near in nears for high in [0] + highs]
    direct = rows % 16 == 0
    if not direct:
        order = dp_at ^ jnp.arange(dp_count)

        def ordered(pieces, masks):
            parts = [piece if piece.ndim == 3 else piece[None] for piece in pieces]
            places = jnp.array([masks.index(mask) for mask in range(dp_count)])[order]
            return jnp.concatenate(parts, axis=0)[places].reshape(model, -1)

        in_pieces = [ordered(in_pieces, piece_masks)]
    state_weight = shared[:, :maps_rows].reshape(-1, MAPS)
    small_all = shared[:, maps_rows].astype(F32)
    conv_size = conv_rows * (CONV + 1)
    conv_whole = sum(
        small_all[:, part * conv_size : (part + 1) * conv_size] for part in range(3)
    ).reshape(-1, CONV + 1)
    gain_base = 3 * conv_size
    gain_size = norm_gain.shape[0]
    gain_whole = sum(
        small_all[:, gain_base + part * gain_size : gain_base + (part + 1) * gain_size]
        for part in range(3)
    ).reshape(-1)
    channel_wide = pad_to(channel_params, 1, width)
    taps = pad_to(
        jnp.concatenate([channel_wide[: CONV + 1], conv_whole.T], axis=1), 0, 8
    )
    heads_wide = pad_to(pad_to(head_params, 1, LANES), 0, 8)
    skip_wide = jnp.repeat(pad_to(head_params[2], 0, width // HEAD), HEAD)
    skip_gain = pad_to(jnp.stack([skip_wide, channel_wide[CONV + 1]]), 0, 8)
    gain_rows = pad_to(gain_whole[None, :], 0, 8)

    block_rows = min(own_count, 2 * SPAN)

    def token_spec(size, reverse=False, span=SPAN):
        if reverse:
            return pl.BlockSpec((SPAN, size), lambda at, *_: (chunks - 1 - at, 0))
        return pl.BlockSpec((span, size), lambda at, *_: (at, 0))

    def piece_specs(reverse=False, span=SPAN):
        inners = own_count // span

        def spec(mask):
            def index(at, ids_ref, *_):
                block = chunks - 1 - at if reverse else at
                mine = (block // inners) ^ ids_ref[1] == mask
                return (jnp.where(mine, block % inners, 0), 0)

            return pl.BlockSpec((span, model), index)

        return [spec(mask) for mask in range(tensor_count)]

    def part_specs(reverse=False, span=SPAN):
        inners = own_count // span

        def spec(odd):
            def index(at, ids_ref, *_):
                block = chunks - 1 - at if reverse else at
                owner = block // inners
                inner = block % inners
                mine = ((owner ^ ids_ref[1]) & 1) == odd
                if reverse:
                    other = jnp.where(owner > 0, owner - 1, 1)
                    other_inner = jnp.where(owner > 0, inners - 1, 0)
                else:
                    last = tensor_count - 1
                    other = jnp.where(owner < last, owner + 1, last - 1)
                    other_inner = jnp.where(owner < last, 0, inners - 1)
                owner = jnp.where(mine, owner, other)
                return ((owner ^ ids_ref[1]) >> 1, jnp.where(mine, inner, other_inner), 0)

            return pl.BlockSpec((1, span, model), index)

        return [spec(0), spec(1)]

    def struct(shape, dtype=F32):
        return jax.ShapeDtypeStruct(shape, dtype)

    arbitrary = pltpu.CompilerParams(
        dimension_semantics=("arbitrary",), vmem_limit_bytes=VMEM
    )
    if not direct:
        piece_masks = [None]
    normed, gate_raw, raw, pre, act, step_in, states, mixed, weight, gained, squares = pl.pallas_call(
        functools.partial(forward_kernel, width, len(in_pieces), piece_masks, tensor_count, own_chunks),
        grid_spec=pltpu.PrefetchScalarGridSpec(
            num_scalar_prefetch=1,
            grid=(chunks,),
            in_specs=piece_specs()
            + [whole_spec(piece.shape) for piece in in_pieces]
            + [
                whole_spec(state_weight.shape),
                whole_spec(gain_rows.shape),
                whole_spec(taps.shape),
                whole_spec(heads_wide.shape),
                whole_spec(skip_gain.shape),
            ],
            out_specs=[
                token_spec(model),
                token_spec(width),
                token_spec(mixed_width),
                token_spec(mixed_width),
                token_spec(mixed_width),
                token_spec(3 * LANES),
                pl.BlockSpec((1, STATE, width), lambda at, *_: (at, 0, 0)),
                token_spec(width),
                whole_spec((model, columns)),
                token_spec(width),
                pl.BlockSpec((8, SPAN), lambda at, *_: (0, at)),
            ],
            scratch_shapes=[
                pltpu.VMEM((SPAN + 8, mixed_width), F32),
                pltpu.VMEM((STATE, width), F32),
                pltpu.VMEM((SPAN, model), BF),
            ],
        ),
        out_shape=[
            struct((tokens, model), BF),
            struct((tokens, width)),
            struct((tokens, mixed_width)),
            struct((tokens, mixed_width)),
            struct((tokens, mixed_width), BF),
            struct((tokens, 3 * LANES)),
            struct((chunks, STATE, width)),
            struct((tokens, width)),
            struct((model, columns), BF),
            struct((tokens, width)),
            struct((8, tokens)),
        ],
        compiler_params=arbitrary,
        name="ssd_forward",
    )(ids, *u_pieces, *in_pieces, state_weight, gain_rows, taps, heads_wide, skip_gain)

    gate_raw, *landed = together(gate_raw, *grad_far.values(), *out_near)
    grad_far = dict(zip(grad_far, landed))
    out_near = landed[len(grad_far) :]
    grad_pieces = gather_near(grad_own, grad_far, "tensor", 2)
    out_pieces = [out_start] + out_far + out_near
    if not direct:
        out_pieces = [ordered(out_pieces, out_masks)]
        out_masks = [None]
    merged_grad, *branch_parts, sums_part = pl.pallas_call(
        functools.partial(
            middle_kernel, tensor_count, len(out_pieces), out_masks, own_count // block_rows
        ),
        grid_spec=pltpu.PrefetchScalarGridSpec(
            num_scalar_prefetch=2,
            grid=(tokens // block_rows,),
            in_specs=[
                *piece_specs(span=block_rows),
                *[whole_spec(piece.shape) for piece in out_pieces],
                token_spec(width, span=block_rows),
                pl.BlockSpec((8, block_rows), lambda at, *_: (0, at)),
            ],
            out_specs=[
                token_spec(width, span=block_rows),
                *part_specs(span=block_rows),
                pl.BlockSpec((2, block_rows), lambda at, *_: (0, at)),
            ],
            scratch_shapes=[pltpu.VMEM((block_rows, model), BF), pltpu.VMEM((model, width), BF)],
        ),
        out_shape=[
            struct((tokens, width)),
            *[struct((tensor_count // 2, own_count, model), BF)] * 2,
            struct((2, tokens)),
        ],
        compiler_params=arbitrary,
        name="gate_middle",
    )(ids, lengths, *grad_pieces, *out_pieces, gained, squares)

    branch_kept, branch_sent = branch_parts
    branch_near, *sums = together(
        exchange(branch_sent, "tensor", 1),
        *[exchange(sums_part, "tensor", mask) for mask in range(1, tensor_count)],
    )
    sums = sum(sums, sums_part)
    branch_out = branch_kept[1:].astype(F32) + branch_near[1:].astype(F32)
    branch_far = [
        exchange(branch_out[position].astype(BF), "tensor", 2 * position + 2)
        for position in range(tensor_count // 2 - 1)
    ]
    (early,) = pl.pallas_call(
        functools.partial(early_kernel, tensor_count, own_count // block_rows),
        grid_spec=pltpu.PrefetchScalarGridSpec(
            num_scalar_prefetch=2,
            grid=(tokens // block_rows,),
            in_specs=[
                *piece_specs(span=block_rows),
                pl.BlockSpec((2, block_rows), lambda at, *_: (0, at)),
                token_spec(model, span=block_rows),
                token_spec(width, span=block_rows),
                token_spec(width, span=block_rows),
                token_spec(width, span=block_rows),
                whole_spec(skip_gain.shape),
            ],
            out_specs=[whole_spec((dp_count, rows, 2 * width))],
            scratch_shapes=[
                pltpu.VMEM((block_rows, model), BF),
                pltpu.VMEM((width, model), F32),
                pltpu.VMEM((width, model), F32),
            ],
        ),
        out_shape=[struct((dp_count, rows, 2 * width), BF)],
        compiler_params=arbitrary,
        name="early_grads",
    )(ids, lengths, *grad_pieces, sums, normed, gate_raw, mixed, merged_grad, skip_gain)
    early = lax.all_to_all(early, "dp", 0, 0)
    masks = slot_masks(dp_count, dp_low)
    first_columns = mixed_width
    second_columns = LANES
    kept_slots = dp_count // dp_low
    token_back = functools.partial(token_spec, reverse=True)
    normed_kept, normed_sent, first_kept, first_sent, *seconds_out = pl.pallas_call(
        functools.partial(backward_kernel, width, masks, tensor_count, own_chunks),
        grid_spec=pltpu.PrefetchScalarGridSpec(
            num_scalar_prefetch=2,
            grid=(chunks,),
            in_specs=[
                *piece_specs(True),
                pl.BlockSpec((2, SPAN), lambda at, *_: (0, chunks - 1 - at)),
                token_back(model),
                token_back(width),
                token_back(width),
                token_back(width),
                token_back(mixed_width),
                token_back(mixed_width),
                token_back(mixed_width),
                token_back(3 * LANES),
                pl.BlockSpec((1, STATE, width), lambda at, *_: (chunks - 1 - at, 0, 0)),
                pl.BlockSpec(
                    (1, STATE, width), lambda at, *_: (jnp.minimum(chunks - at, chunks - 1), 0, 0)
                ),
                whole_spec((model, columns)),
                whole_spec(taps.shape),
                whole_spec(heads_wide.shape),
                whole_spec(skip_gain.shape),
                whole_spec(gain_rows.shape),
            ],
            out_specs=[
                *part_specs(True),
                whole_spec((kept_slots, SMALL + rows, first_columns)),
                whole_spec((dp_count - kept_slots, SMALL + rows, first_columns)),
                *[whole_spec((dp_low, rows, second_columns))] * kept_slots,
            ],
            scratch_shapes=[
                pltpu.VMEM((STATE, width), F32),
                pltpu.VMEM((SPAN + 8, mixed_width), F32),
                pltpu.VMEM((model, columns - width), F32),
                pltpu.VMEM((8, mixed_width), F32),
                pltpu.VMEM((8, LANES), F32),
                pltpu.VMEM((8, model), F32),
                pltpu.VMEM((SPAN, model), BF),
            ],
        ),
        out_shape=[
            *[struct((tensor_count // 2, own_count, model), BF)] * 2,
            struct((kept_slots, SMALL + rows, first_columns), BF),
            struct((dp_count - kept_slots, SMALL + rows, first_columns), BF),
            *[struct((dp_low, rows, second_columns), BF)] * kept_slots,
        ],
        compiler_params=arbitrary,
        name="ssd_backward",
    )(
        ids,
        lengths,
        *u_pieces,
        sums,
        normed,
        gate_raw,
        mixed,
        merged_grad,
        raw,
        pre,
        act,
        step_in,
        states,
        states,
        weight,
        taps,
        heads_wide,
        skip_gain,
        gain_rows,
    )

    first_kept, first_sent, early = together(first_kept, first_sent, early)
    highs_count = first_kept.shape[0]
    first_near = [
        exchange(
            first_sent
            if dp_low == 2
            else first_sent[(near - 1) * highs_count : near * highs_count],
            "dp",
            near,
        )
        for near in nears
    ]
    second_far = [
        exchange(seconds_out[position], "dp", position * dp_low)
        for position in range(1, kept_slots)
    ]
    normed_near = exchange(normed_sent, "tensor", 1)
    landed = together(normed_near, *first_near, *second_far)
    normed_total = normed_kept.astype(F32) + landed[0].astype(F32)
    first_total = first_kept.astype(F32)
    for values in landed[1 : 1 + len(first_near)]:
        first_total = first_total + values.astype(F32)
    second_far = landed[1 + len(first_near) :]
    joined = first_total[:, : SMALL // 2] + first_total[:, SMALL // 2 : SMALL]
    high = lax.reduce_precision(joined, 8, 7)
    first_total = jnp.concatenate([high, joined - high, first_total[:, SMALL:]], axis=1)
    first_parts = [first_total[0]] + far_parts(first_total, "dp", dp_low)
    second_total = seconds_out[0].astype(F32)
    for values in second_far:
        second_total = second_total + values.astype(F32)
    second_parts = [second_total[0]] + [
        exchange(second_total[near].astype(BF), "dp", near) for near in range(1, dp_low)
    ]
    landed = together(*first_parts, *second_parts)
    first_parts = landed[: len(first_parts)]
    second_parts = landed[len(first_parts) :]

    inputs = block_input.astype(F32)
    position_all = tensor_at * own_count + jnp.arange(own_count, dtype=jnp.int32)
    length_of = jnp.sum(
        jnp.where(
            (position_all // LMAX)[:, None]
            == jnp.arange(lengths.shape[0], dtype=jnp.int32)[None, :],
            lengths[None, :],
            0,
        ),
        axis=1,
    )
    live_own = (position_all % LMAX < length_of)[:, None]
    own_squares = lax.dynamic_slice(sums[0], (tensor_at * own_count,), (own_count,))
    own_scale = lax.rsqrt(own_squares / INNER + EPSILON)[:, None]
    branch = branch_kept[0].astype(F32) + branch_near[0].astype(F32)
    for values in branch_far:
        branch = branch + values.astype(F32)
    output = (inputs + jnp.where(live_own, branch * own_scale, 0.0)).astype(BF)
    normed_grad = normed_total[0]
    for values in far_parts(normed_total, "tensor", 2):
        normed_grad = normed_grad + values.astype(F32)
    scale = lax.rsqrt(jnp.mean(inputs * inputs, axis=-1, keepdims=True) + EPSILON)
    scaled_grad = normed_grad * gain_whole[None, :]
    input_grad = (
        output_grad.astype(F32)
        + scale * scaled_grad
        - inputs * scale**3 * jnp.mean(scaled_grad * inputs, axis=-1, keepdims=True)
    )

    plain = pltpu.CompilerParams(
        dimension_semantics=("arbitrary",), vmem_limit_bytes=VMEM
    )

    def whole_call(kernel, operands, shapes, name):
        return pl.pallas_call(
            kernel,
            grid_spec=pltpu.PrefetchScalarGridSpec(
                num_scalar_prefetch=1,
                grid=(1,),
                in_specs=[whole_spec(value.shape) for value in operands],
                out_specs=[whole_spec(shape.shape) for shape in shapes],
            ),
            out_shape=shapes,
            compiler_params=plain,
            name=name,
        )(ids, *operands)

    (packed,) = whole_call(
        functools.partial(pack_kernel, width, tensor_count),
        first_parts,
        [struct((tensor_count, maps_rows + 8, MAPS))],
        "pack_maps",
    )
    maps_parts = lax.all_to_all(packed, "tensor", 0, 0)
    def wide_of(values):
        return [values[0], values[1].T] + list(values[2:5])

    wide_shapes = [struct(values.shape) for values in wide_of(masters)]
    wide = whole_call(
        functools.partial(
            lamb_wide_kernel,
            width,
            channels,
            heads,
            float(dp_count),
            len(first_parts),
            len(second_parts),
        ),
        [early, *first_parts, *second_parts, *wide_of(masters), *wide_of(firsts), *wide_of(seconds)],
        wide_shapes * 4 + [struct((1, LANES))],
        "lamb_wide",
    )

    def flat(values):
        return [values[5], values[6], values[7][None, :]]

    maps_shapes = [struct(values.shape) for values in flat(masters)]
    maps = whole_call(
        lamb_maps_kernel,
        [maps_parts, *flat(masters), *flat(firsts), *flat(seconds), wide[20]],
        maps_shapes * 4 + [struct((everywhere, 1, LANES))],
        "lamb_maps",
    )
    spread = lax.all_to_all(maps[12], ("dp", "tensor"), 0, 0)
    spread, input_grad, output = together(spread, input_grad, output)
    updates = whole_call(
        update_kernel,
        [spread, *wide[15:20], *maps[9:12]],
        wide_shapes + maps_shapes + [struct((2, 8))],
        "lamb_update",
    )

    def joined(kind):
        values = list(wide[5 * kind : 5 * kind + 5]) + list(maps[3 * kind : 3 * kind + 3])
        return (values[0], values[1].T) + tuple(values[2:7]) + (values[7][0],)

    return (
        (output, input_grad)
        + joined(0)
        + joined(1)
        + joined(2)
        + (updates[0], updates[1].T)
        + tuple(updates[2:7])
        + (updates[7][0], updates[8])
    )


WEIGHT_SPECS = (
    P("dp", None, "tensor"),
    P("dp", "tensor"),
    P("dp", "tensor"),
    P(None, "tensor"),
    P(None, "tensor"),
    P(("dp", "tensor"), None),
    P(("dp", "tensor"), None),
    P(("dp", "tensor")),
)


def solution(mesh):
    tokens = P(("dp", "tensor"), None)
    return jax.shard_map(
        local,
        mesh=mesh,
        in_specs=(tokens, tokens, P("dp")) + WEIGHT_SPECS * 3,
        out_specs=(tokens, tokens) + WEIGHT_SPECS * 4 + (P(),),
        check_vma=False,
    )
```
